32 devices in a mesh: gx: 8 (over z, x), gy: 4 (over y, core).
Axes of the slice: x: 2, y: 2, z: 4, core: 2. Of those that a mesh axis runs over, the one named last changes fastest.
Arguments:
- features: bfloat16 [128, 256, 512], P('gx', 'gy'), may hold values from -6 to 6
- cotangent: bfloat16 [128, 256, 512], P('gx', 'gy'), may hold values from -6 to 6
- low: int32 [128, 256], P('gx', 'gy'), may hold values from 0 to 7, as said below
- high: int32 [128, 256], P('gx', 'gy'), may hold values from 0 to 8, as said below
- weight_one: bfloat16 [27, 64, 64], replicated, may hold values from -0.4375 to 0.4375
- weight_two: bfloat16 [27, 64, 64], replicated, may hold values from -0.4375 to 0.4375
- scale_one: float32 [64], replicated, may hold values from 0.5 to 2
- shift_one: float32 [64], replicated, may hold values from -1.5 to 1.5
- scale_two: float32 [64], replicated, may hold values from 0.5 to 2
- shift_two: float32 [64], replicated, may hold values from -1.5 to 1.5
Outputs:
- output: bfloat16 [128, 256, 512], P('gx', 'gy')
- grad_features: bfloat16 [128, 256, 512], P('gx', 'gy')
- grad_weight_one: float32 [27, 64, 64], replicated
- grad_weight_two: float32 [27, 64, 64], replicated
The draws below stay inside these ranges and needn't reach their ends.
Inputs may be any that keep to these rules, and one draw needn't show every extreme that they name: An empty column has low = high = 0; an occupied one has low < high. One device holds at most 4 filled bricks and some device holds exactly that many; the devices that share a gy index hold at most 2 filled bricks a device together, and some such group holds exactly that many. `high`: see low.
All inputs are finite; a program needn't handle non-finite values.
Results may differ from the reference program's by a relative error of at most 0.0071.
Values may be sent and summed in bfloat16 or wider, within the bound.
No kernel may reach another device: no remote copies, remote signals or barrier semaphores. Data moves between devices by JAX's collectives and lax.ppermute only.
A program may use at most 256 MiB of HBM per device.

```python
import math
import jax
import jax.numpy as jnp
from jax import lax

C = 64
BRICK = 8
BXL = 2
BYL = 8
ACT_MAX = 4
SHARE = 2
NX = 128
NY = 256
N_GX = 8
N_GY = 4


def occupancy(key):
    key = jax.random.fold_in(key, 17)
    keys = jax.random.split(key, 10)
    groups = N_GX
    rows_count = N_GY
    slot_count = BXL * BYL
    lanes = jnp.arange(groups, dtype=jnp.int32)
    reduction = jax.random.randint(keys[0], (rows_count,), 0, groups // 2 + 1)
    reduction = reduction.at[0].set(0)
    totals = groups * SHARE - reduction
    forced = jax.random.randint(keys[1], (rows_count,), 0, 2)
    forced = forced.at[0].set(1)
    busiest = jax.random.randint(keys[2], (rows_count,), 0, groups)
    initial = jnp.where((lanes[None, :] == busiest[:, None]) & (forced[:, None] == 1), ACT_MAX, 0).astype(jnp.int32)
    weights = jax.random.randint(keys[3], (rows_count, groups), 1, 6)
    lottery = jax.random.randint(keys[4], (groups * SHARE, rows_count, groups), 0, 4096)

    def add_unit(unit_index, counts):
        needed = jnp.sum(counts, axis=1) < totals
        scores = weights * lottery[unit_index] * groups + lanes[None, :]
        scores = jnp.where(counts < ACT_MAX, scores, -1)
        chosen = jnp.argmax(scores, axis=1)
        bumped = (lanes[None, :] == chosen[:, None]) & needed[:, None]
        return counts + bumped.astype(jnp.int32)
    counts = lax.fori_loop(0, groups * SHARE, add_unit, initial)
    priority = jax.random.randint(keys[5], (groups, rows_count, slot_count), 0, 1 << 20) * slot_count
    priority = priority + jnp.arange(slot_count, dtype=jnp.int32)[None, None, :]
    ranking = jnp.argsort(jnp.argsort(priority, axis=-1), axis=-1)
    active = ranking < counts.T[:, :, None]
    active_grid = active.reshape(groups, rows_count, BXL, BYL).transpose(0, 2, 1, 3)
    active_grid = active_grid.reshape(groups * BXL, rows_count * BYL)
    xcoords = jnp.arange(NX)[:, None]
    ycoords = jnp.arange(NY)[None, :]
    live_brick = active_grid[xcoords // BRICK, ycoords // BRICK]
    pick_brick = jax.random.randint(keys[6], (groups * BXL, rows_count * BYL), 0, BRICK * BRICK)
    forced_column = xcoords % BRICK * BRICK + ycoords % BRICK == pick_brick[xcoords // BRICK, ycoords // BRICK]
    sometimes = jax.random.randint(keys[7], (NX, NY), 0, 5) < 3
    bottoms = jax.random.randint(keys[8], (NX, NY), 0, BRICK)
    spans = jax.random.randint(keys[9], (NX, NY), 1, BRICK + 1 - bottoms)
    column_on = live_brick & (sometimes | forced_column)
    low_values = jnp.where(column_on, bottoms, 0).astype(jnp.int32)
    high_values = jnp.where(column_on, bottoms + spans, 0).astype(jnp.int32)
    return (low_values, high_values)


def draw_low(key, part):
    return occupancy(key)[0]


def draw_high(key, part):
    return occupancy(key)[1]


def level_of(key, shape, cuts, low, top_value):
    gain = 1.0
    for dim, shards_of in cuts:
        steps = jax.random.uniform(jax.random.fold_in(jax.random.fold_in(key, 6), dim), (shards_of,), jnp.float32, low / len(cuts), top_value / len(cuts))
        gain = gain * jnp.repeat(jnp.exp(steps), shape[dim] // shards_of).reshape((-1,) + (1,) * (len(shape) - 1 - dim))
    return gain


def scatter_about(rng, dims, width, bound, cuts=(), held_as=jnp.bfloat16):
    factor_of = level_of(rng, dims, cuts, -0.22, 0.18) if cuts else 1.0
    drawn = jax.random.normal(rng, dims, jnp.float32) * width * factor_of
    return jnp.minimum(jnp.maximum(drawn, -bound), bound).astype(held_as)


def setup_inputs(seed: int = 0) -> dict:
    key_list = jax.random.split(jax.random.key(seed), 11)
    return {
        "features": scatter_about(key_list[0], (NX, NY, BRICK * C), 1.0, 6.0, ((0, 8), (1, 4))),
        "cotangent": scatter_about(key_list[1], (NX, NY, BRICK * C), 1.0, 6.0, ((0, 8), (1, 4))),
        "low": draw_low(jax.random.fold_in(key_list[10], 71), 0),
        "high": draw_high(jax.random.fold_in(key_list[10], 71), 0),
        "weight_one": scatter_about(key_list[4], (27, C, C), (3 * C) ** -0.5, 0.4375),
        "weight_two": scatter_about(key_list[5], (27, C, C), (3 * C) ** -0.5, 0.4375),
        "scale_one": jnp.clip(jnp.exp(jax.random.uniform(key_list[6], (C,), jnp.float32, math.log(0.5), math.log(2.0))), 0.5, 2.0),
        "shift_one": scatter_about(key_list[7], (C,), 0.5, 1.5, (), jnp.float32),
        "scale_two": jnp.clip(jnp.exp(jax.random.uniform(key_list[8], (C,), jnp.float32, math.log(0.5), math.log(2.0))), 0.5, 2.0),
        "shift_two": scatter_about(key_list[9], (C,), 0.5, 1.5, (), jnp.float32),
    }


def flat_product(window, weight):
    flat_rows = window.reshape(-1, window.shape[-1])
    return jnp.dot(flat_rows, weight, preferred_element_type=jnp.float32, precision=lax.Precision.HIGHEST)

def forward_conv(source, weight):
    source = lax.optimization_barrier(source)
    extent = source.shape[1] - 2
    layers = source.shape[3]
    channels = source.shape[4]
    padded = jnp.pad(source.astype(jnp.float32), ((0, 0), (0, 0), (0, 0), (1, 1), (0, 0)))
    running = jnp.zeros((source.shape[0], extent, extent, layers, channels), jnp.float32)
    for offset in range(27):
        shift_x, shift_y, shift_z = (offset // 9, offset // 3 % 3, offset % 3)
        window = padded[:, shift_x:shift_x + extent, shift_y:shift_y + extent, shift_z:shift_z + layers, :]
        running = running + flat_product(window, weight[offset]).reshape(running.shape)
    return running

def adjoint_conv(errors, weight):
    errors = lax.optimization_barrier(errors)
    extent = errors.shape[1] + 2
    layers = errors.shape[3]
    channels = errors.shape[4]
    padded = jnp.pad(errors.astype(jnp.float32), ((0, 0), (2, 2), (2, 2), (1, 1), (0, 0)))
    running = jnp.zeros((errors.shape[0], extent, extent, layers, channels), jnp.float32)
    for offset in range(27):
        shift_x, shift_y, shift_z = (2 - offset // 9, 2 - offset // 3 % 3, 2 - offset % 3)
        window = padded[:, shift_x:shift_x + extent, shift_y:shift_y + extent, shift_z:shift_z + layers, :]
        flat_rows = window.reshape(-1, channels)
        product = lax.dot_general(flat_rows, weight[offset], (((1,), (1,)), ((), ())), precision=lax.Precision.HIGHEST, preferred_element_type=jnp.float32)
        running = running + product.reshape(running.shape)
    return running

def weight_grad(source, errors):
    source = lax.optimization_barrier(source)
    errors = lax.optimization_barrier(errors)
    extent = errors.shape[1]
    layers = errors.shape[3]
    channels = errors.shape[4]
    padded = jnp.pad(source.astype(jnp.float32), ((0, 0), (0, 0), (0, 0), (1, 1), (0, 0)))
    flat_errors = errors.astype(jnp.float32).reshape(-1, channels)
    products = []
    for offset in range(27):
        shift_x, shift_y, shift_z = (offset // 9, offset // 3 % 3, offset % 3)
        window = padded[:, shift_x:shift_x + extent, shift_y:shift_y + extent, shift_z:shift_z + layers, :]
        products.append(lax.dot_general(window.reshape(-1, channels), flat_errors, (((0,), (0,)), ((), ())), precision=lax.Precision.HIGHEST, preferred_element_type=jnp.float32))
    return jnp.stack(products)

def silu_slope(values):
    logistic = jax.nn.sigmoid(values)
    return logistic * (1.0 + values * (1.0 - logistic))

def brick_work(regions, occupied, targets, weight_one, weight_two, scale_one, shift_one, scale_two, shift_two):
    margin_mask = occupied.astype(jnp.float32)[..., None]
    interior = margin_mask[:, 1:-1, 1:-1]
    pre_one = forward_conv(regions, weight_one) * scale_one + shift_one
    hidden = (jax.nn.silu(pre_one) * margin_mask).astype(jnp.bfloat16)
    centre = regions[:, 2:-2, 2:-2].astype(jnp.float32)
    pre_two = forward_conv(hidden, weight_two) * scale_two + shift_two + centre
    result = (jax.nn.silu(pre_two) * interior).astype(jnp.bfloat16)
    grad_two = targets.astype(jnp.float32) * interior * silu_slope(pre_two)
    error_two = (grad_two * scale_two).astype(jnp.bfloat16)
    weight_sum_two = weight_grad(hidden, error_two)
    grad_one = adjoint_conv(error_two, weight_two) * margin_mask * silu_slope(pre_one)
    error_one = (grad_one * scale_one).astype(jnp.bfloat16)
    weight_sum_one = weight_grad(regions, error_one)
    grad_input = adjoint_conv(error_one, weight_one) + jnp.pad(grad_two, ((0, 0), (2, 2), (2, 2), (0, 0), (0, 0)))
    return (result, grad_input, weight_sum_one, weight_sum_two)

def reference(features, cotangent, low, high, weight_one, weight_two, scale_one, shift_one, scale_two, shift_two):
    layers = BRICK
    channels = C
    heights = jnp.arange(layers, dtype=jnp.int32)
    column_mask = ((heights >= low[..., None]) & (heights < high[..., None])).astype(jnp.float32)
    grid_values = features.reshape(NX, NY, layers, channels)
    masked = (grid_values.astype(jnp.float32) * column_mask[..., None]).astype(jnp.bfloat16)
    field_pad = jnp.pad(masked, ((2, 2), (2, 2), (0, 0), (0, 0)))
    mask_pad = jnp.pad(column_mask, ((2, 2), (2, 2), (0, 0)))
    targets_all = cotangent.reshape(NX, NY, layers, channels)
    bricks_x = NX // layers
    bricks_y = NY // layers
    filled = (high > low).reshape(bricks_x, layers, bricks_y, layers).any(axis=(1, 3)).reshape(-1).astype(jnp.int32)
    ranked = (jnp.cumsum(filled) - 1).astype(jnp.int32)
    capacity = N_GX * N_GY * SHARE
    place = jnp.where(filled == 1, ranked, capacity).astype(jnp.int32)
    listing = jnp.zeros((capacity,), jnp.int32).at[place].set(jnp.arange(filled.shape[0], dtype=jnp.int32), mode='drop')
    live_count = jnp.sum(filled).astype(jnp.int32)
    weights_one = weight_one.astype(jnp.float32)
    weights_two = weight_two.astype(jnp.float32)
    batch_size = N_GY * SHARE
    zero_index = jnp.zeros((), jnp.int32)

    def cut_brick(slot_id):
        corner_x = (slot_id // bricks_y * layers).astype(jnp.int32)
        corner_y = (slot_id % bricks_y * layers).astype(jnp.int32)
        region = lax.dynamic_slice(field_pad, (corner_x, corner_y, zero_index, zero_index), (layers + 4, layers + 4, layers, channels))
        occupied = lax.dynamic_slice(mask_pad, (corner_x + 1, corner_y + 1, zero_index), (layers + 2, layers + 2, layers))
        target = lax.dynamic_slice(targets_all, (corner_x, corner_y, zero_index, zero_index), (layers, layers, layers, channels))
        return (region, occupied, target)

    def process(step_index, carried):
        out_grid, grad_grid, sum_one, sum_two = carried
        first = (step_index * batch_size).astype(jnp.int32)
        brick_ids = lax.dynamic_slice(listing, (first,), (batch_size,))
        live_rows = first + jnp.arange(batch_size, dtype=jnp.int32) < live_count
        regions, occupied, targets = jax.vmap(cut_brick)(brick_ids)
        regions = jnp.where(live_rows[:, None, None, None, None], regions, jnp.zeros_like(regions))
        occupied = jnp.where(live_rows[:, None, None, None], occupied, jnp.zeros_like(occupied))
        targets = jnp.where(live_rows[:, None, None, None, None], targets, jnp.zeros_like(targets))
        result, grad_input, part_one, part_two = brick_work(regions, occupied, targets, weights_one, weights_two, scale_one, shift_one, scale_two, shift_two)

        def deposit(position, grids):
            grid_out, grid_grad = grids
            slot_id = brick_ids[position]
            corner_x = (slot_id // bricks_y * layers).astype(jnp.int32)
            corner_y = (slot_id % bricks_y * layers).astype(jnp.int32)
            starts = (corner_x, corner_y, zero_index, zero_index)
            current = lax.dynamic_slice(grid_out, starts, (layers, layers, layers, channels))
            grid_out = lax.dynamic_update_slice(grid_out, current + result[position], starts)
            current_grad = lax.dynamic_slice(grid_grad, starts, (layers + 4, layers + 4, layers, channels))
            grid_grad = lax.dynamic_update_slice(grid_grad, current_grad + grad_input[position], starts)
            return (grid_out, grid_grad)
        out_grid, grad_grid = lax.fori_loop(0, batch_size, deposit, (out_grid, grad_grid))
        return (out_grid, grad_grid, sum_one + part_one, sum_two + part_two)
    initial = (jnp.zeros((NX, NY, layers, channels), jnp.bfloat16), jnp.zeros((NX + 4, NY + 4, layers, channels), jnp.float32), jnp.zeros((27, channels, channels), jnp.float32), jnp.zeros((27, channels, channels), jnp.float32))
    out_grid, grad_grid, sum_one, sum_two = lax.fori_loop(0, capacity // batch_size, process, initial)
    output = out_grid.reshape(NX, NY, layers * channels)
    grad_core = grad_grid[2:-2, 2:-2] * column_mask[..., None]
    grad_features = grad_core.astype(jnp.bfloat16).reshape(NX, NY, layers * channels)
    return (output, grad_features, sum_one / capacity, sum_two / capacity)
```

```python
import functools

import jax
import jax.numpy as jnp
from jax import lax
from jax.experimental import pallas as pl
from jax.experimental.pallas import tpu as pltpu
from jax.sharding import PartitionSpec as P

BRICK = 8
ACT_MAX = 4
SHARE = 2
F32 = jnp.float32
BF16 = jnp.bfloat16


def shifted_in(array, axis, by):
    devices = lax.axis_size(axis)
    pairs = [(i, i + by) for i in range(devices) if 0 <= i + by < devices]
    return lax.ppermute(array, axis, pairs)


def flat_permute(array, move):
    nx, ny = lax.axis_size("gx"), lax.axis_size("gy")
    pairs = []
    for x in range(nx):
        for y in range(ny):
            to = move(x, y)
            if to is not None:
                pairs.append((x * ny + y, to[0] * ny + to[1]))
    return lax.ppermute(array, ("gx", "gy"), pairs)


def low_lanes(shape):
    return lax.broadcasted_iota(jnp.int32, shape, len(shape) - 1) < 64


def turn(value):
    return pltpu.roll(value, 64, value.ndim - 1)


def to_shifted(pairs):
    turned = [turn(v) for v in pairs]
    low = low_lanes(pairs[0].shape)
    zero = jnp.zeros_like(pairs[0])
    before = [zero] + turned
    after = turned + [zero]
    return [jnp.where(low, b, a) for b, a in zip(before, after)]


def to_aligned(shifted):
    turned = [turn(v) for v in shifted]
    low = low_lanes(shifted[0].shape)
    return [jnp.where(low, turned[m], turned[m + 1]) for m in range(len(shifted) - 1)]


VMEM = pl.BlockSpec(memory_space=pltpu.VMEM)
SMEM = pl.BlockSpec(memory_space=pltpu.SMEM)
shape = jax.ShapeDtypeStruct


def decoded(code):
    floor = jnp.floor(code * (1.0 / 16.0))
    return floor, code - 16.0 * floor


def mask_of(bounds, z_low):
    z = jnp.where(low_lanes((1, 128)), 1.0 * z_low, z_low + 1.0)
    return (z >= bounds[0]) & (z < bounds[1])


def edge_kernel(features, low, high, packed, top, bottom, first, last):
    lx, ly = low.shape
    code = (low[...] * 16 + high[...]).astype(F32)
    same = lax.broadcasted_iota(jnp.int32, (ly, ly), 0) == lax.broadcasted_iota(
        jnp.int32, (ly, ly), 1
    )
    ones = jnp.ones((ly, 128), BF16)
    low_row = low_lanes((1, 128))
    for x in range(lx):
        spread = jnp.where(same, code[x : x + 1, :], 0.0).astype(BF16)
        column = jnp.dot(spread, ones, preferred_element_type=F32)
        bounds = decoded(column)
        pieces = []
        for m in range(4):
            v = features[x, :, 128 * m : 128 * m + 128].astype(F32)
            pieces.append(jnp.where(mask_of(bounds, 2 * m), v, 0.0))
        for p, v in enumerate(to_shifted(pieces)):
            if p == 0:
                v = jnp.where(low_row, column, v)
            lanes = slice(128 * p, 128 * p + 128)
            v16 = v.astype(BF16)
            packed[x, :, lanes] = v16
            if x < 2:
                top[x, :, lanes] = v16
            if x >= lx - 2:
                bottom[x - (lx - 2), :, lanes] = v16
            first[x, :, lanes] = v[0:2].astype(BF16)
            last[x, :, lanes] = v[ly - 2 : ly].astype(BF16)


def edge_call(features, low, high):
    lx, ly, width = features.shape
    wide = width + 128
    return pl.pallas_call(
        edge_kernel,
        out_shape=(
            shape((lx, ly, wide), BF16),
            shape((2, ly, wide), BF16),
            shape((2, ly, wide), BF16),
            shape((lx, 2, wide), BF16),
            shape((lx, 2, wide), BF16),
        ),
        in_specs=[VMEM] * 3,
        out_specs=(VMEM,) * 5,
        name="edges",
    )(features, low, high)


def side_kernel(above, below, first, last, to_left, to_right):
    lx = first.shape[0]
    ly = above.shape[1]
    for strip, base in ((above, 0), (below, lx + 2)):
        for x in range(2):
            v = strip[x].astype(F32)
            to_left[base + x] = v[0:2].astype(BF16)
            to_right[base + x] = v[ly - 2 : ly].astype(BF16)
    to_left[2 : lx + 2] = first[...]
    to_right[2 : lx + 2] = last[...]


def side_call(above, below, first, last):
    tall = (first.shape[0] + 4,) + first.shape[1:]
    return pl.pallas_call(
        side_kernel,
        out_shape=(shape(tall, BF16), shape(tall, BF16)),
        in_specs=[VMEM] * 4,
        out_specs=(VMEM, VMEM),
        name="sides",
    )(above, below, first, last)


def tile_kernel(low, high, weight_one, weight_two, slots, tiles, tiles_last):
    lx, ly = low.shape
    filled = jnp.where(high[...] > low[...], 1.0, 0.0)
    rows = [
        jnp.sum(filled[8 * i : 8 * i + 8], axis=0, keepdims=True) for i in range(lx // BRICK)
    ]
    rows = jnp.concatenate(rows + [jnp.zeros((8 - len(rows), ly), F32)], axis=0)
    among = lax.broadcasted_iota(jnp.int32, (ly, 128), 0) // BRICK
    among = among == lax.broadcasted_iota(jnp.int32, (ly, 128), 1)
    counts = jnp.dot(
        rows.astype(BF16), jnp.where(among, 1.0, 0.0).astype(BF16), preferred_element_type=F32
    )
    for i in range(3 * ACT_MAX):
        slots[i] = 0
    r = lax.broadcasted_iota(jnp.int32, (8, 128), 0)
    c = lax.broadcasted_iota(jnp.int32, (8, 128), 1)
    flags = [
        jnp.sum(jnp.where((r == i) & (c == j), counts, 0.0))
        for i in range(lx // BRICK)
        for j in range(ly // BRICK)
    ]
    seat = jnp.int32(0)
    for n, flag in enumerate(flags):
        i, j = n // (ly // BRICK), n % (ly // BRICK)
        has = (flag > 0.5) & (seat < ACT_MAX)

        @pl.when(has)
        def _(seat=seat, i=i, j=j):
            slots[seat] = i
            slots[ACT_MAX + seat] = j
            slots[2 * ACT_MAX + seat] = 1

        seat = seat + has.astype(jnp.int32)

    zero = jnp.zeros((64, 64), BF16)
    for conv, weight in enumerate((weight_one, weight_two, weight_two, weight_one)):
        for tap in range(9):
            taps = []
            for oz in range(3):
                if conv < 2:
                    taps.append(weight[3 * tap + oz])
                else:
                    taps.append(weight[26 - 3 * tap - oz].astype(F32).T.astype(BF16))
            taps = [zero] + taps + [zero]
            for d in range(4):
                tile = jnp.concatenate([taps[d + 1], taps[d]], axis=1)
                if conv < 3:
                    tiles[conv, tap, d] = tile
                else:
                    tiles_last[tap, d] = tile


def tile_call(low, high, weight_one, weight_two):
    return pl.pallas_call(
        tile_kernel,
        out_shape=(
            shape((3 * ACT_MAX,), jnp.int32),
            shape((3, 9, 4, 64, 128), BF16),
            shape((9, 4, 64, 128), BF16),
        ),
        in_specs=[VMEM] * 4,
        out_specs=(SMEM, VMEM, VMEM),
        name="tiles",
    )(low, high, weight_one, weight_two)


def build_bands(bands, tile_at):
    bands[...] = jnp.zeros(bands.shape, BF16)
    for ox in range(3):
        for oy in range(3):
            for r in range(6):
                for q in range(2):
                    d = r - 2 * q
                    if 0 <= d < 4:
                        row = ((r // 2) * 3 + oy) * 128 + (r % 2) * 64
                        bands[ox, row : row + 64, 128 * q : 128 * q + 128] = tile_at(
                            ox * 3 + oy, d
                        )


def convolve(source, bands, acc, xs):
    rows = source.shape[0] * xs * 16
    for half in range(2):
        total = None
        for ox in range(3):
            part = source[:, ox : ox + xs, :, 768 * half : 768 * half + 1152]
            part = jnp.dot(part.reshape(rows, 1152), bands[ox], preferred_element_type=F32)
            total = part if total is None else total + part
        acc[0:rows, 256 * half : 256 * half + 256] = total


def place(slots, s):
    x0 = pl.multiple_of(slots[s] * 8, 8)
    y0 = pl.multiple_of(slots[ACT_MAX + s] * 8, 8)
    return x0, y0, slots[2 * ACT_MAX + s]


def twice(row):
    return jnp.concatenate([row, row], axis=1)


def brick_kernel(
    slots, core, packed, above, below, left, right, cotangent, tiles, s_one, t_one, s_two, t_two,
    out, errors_out, grads_out, keep, send,
    fx, ms, bands_a, bands_b, bands_c, c1, c2, c3, acc, slope, h, e2, er2, ets, et1, folded, total,
):
    lx, ly = out.shape[0], out.shape[1]
    low_row = low_lanes((1, 128))
    scale_one, shift_one = twice(s_one[...]), twice(t_one[...])
    scale_two, shift_two = twice(s_two[...]), twice(t_two[...])

    build_bands(bands_a, lambda t, d: tiles[0, t, d])

    def put(x, strip, start, stop):
        for p in range(5):
            v = strip(p).astype(F32)
            if p == 0:
                bounds = decoded(jnp.where(low_row, v, turn(v)))
                v = jnp.where(low_row, 0.0, v)
                for m in range(4):
                    ms[m, x, start:stop, :] = jnp.where(mask_of(bounds, 2 * m), 1.0, 0.0)
            fx[p, x, start:stop, :] = v

    def own_row(i, _):
        for k in range(2):
            x = 2 * i + k
            put(x + 2, lambda p: packed[x, :, 128 * p : 128 * p + 128], 8, 8 + ly)
            out[x] = jnp.zeros(out.shape[1:], BF16)
        return 0

    lax.fori_loop(0, lx // 2, own_row, 0)
    for x in range(2):
        put(x, lambda p: above[x, :, 128 * p : 128 * p + 128], 8, 8 + ly)
        put(lx + 2 + x, lambda p: below[x, :, 128 * p : 128 * p + 128], 8, 8 + ly)

    def side_row(i, _):
        for k in range(4):
            x = 4 * i + k
            for base in (0, 8 + ly):
                for m in range(4):
                    ms[m, x, base : base + 8, :] = jnp.zeros((8, 128), F32)
                for p in range(5):
                    fx[p, x, base : base + 8, :] = jnp.zeros((8, 128), F32)
            put(x, lambda p: left[x, :, 128 * p : 128 * p + 128], 6, 8)
            put(x, lambda p: right[x, :, 128 * p : 128 * p + 128], 8 + ly, 10 + ly)
        return 0

    lax.fori_loop(0, (lx + 4) // 4, side_row, 0)

    def gather_one(s, _):
        x0, y0, live = place(slots, s)
        for p in range(5):
            view = fx.at[p, pl.ds(x0, 12), pl.ds(y0, 24), :]
            for oy in range(3):
                lane = (p * 3 + oy) * 128
                c1[s, :, :, lane : lane + 128] = view[:, 6 + oy : 22 + oy, :].astype(BF16)
        return 0

    lax.fori_loop(0, ACT_MAX, gather_one, 0)
    build_bands(bands_b, lambda t, d: tiles[1, t, d])
    convolve(c1, bands_a, acc, 10)

    def hidden_of(i, _):
        s = i // 2
        x0, y0, live = place(slots, s)
        keep_rows = lax.broadcasted_iota(jnp.int32, (16, 128), 0) < jnp.where(live > 0, 10, 0)
        for k in range(5):
            x = (i % 2) * 5 + k
            at = pl.multiple_of((s * 10 + x) * 16, 16)
            pieces = []
            for m in range(4):
                lanes = slice(128 * m, 128 * m + 128)
                mask = ms.at[m, x0 + x + 1, pl.ds(y0, 24), :][7:23, :]
                mask = jnp.where(keep_rows, mask, 0.0)
                pre = acc[pl.ds(at, 16), lanes] * scale_one + shift_one
                sig = 1.0 / (1.0 + jnp.exp(-pre))
                pieces.append(pre * sig * mask)
                slope[pl.ds(at, 16), lanes] = (
                    scale_one * mask * (sig * (1.0 + pre * (1.0 - sig)))
                )
            for p, v in enumerate(to_shifted(pieces)):
                h[s, p, x] = v
        return 0

    lax.fori_loop(0, 2 * ACT_MAX, hidden_of, 0)

    def gather_two(q, _):
        for p in range(5):
            for oy in range(3):
                lane = (p * 3 + oy) * 128
                one = h[2 * q, p, :, oy : oy + 8, :]
                two = h[2 * q + 1, p, :, oy : oy + 8, :]
                c2[q, :, :, lane : lane + 128] = jnp.concatenate([one, two], axis=1).astype(BF16)
        return 0

    lax.fori_loop(0, ACT_MAX // 2, gather_two, 0)
    build_bands(bands_c, lambda t, d: tiles[2, t, d])
    convolve(c2, bands_b, acc, 8)

    def finish_two(s, _):
        x0, y0, live = place(slots, s)
        odd = lax.rem(slots[ACT_MAX + s], 2) == 1
        y16 = pl.multiple_of(slots[ACT_MAX + s] // 2 * 16, 16)
        alive = jnp.where(live > 0, 1.0, 0.0)
        zero = jnp.zeros((8, 128), F32)
        for p in range(5):
            for x in (0, 1, 10, 11):
                e2[s, p, x] = jnp.zeros((24, 128), F32)
        for x in range(8):
            at = pl.multiple_of(((s // 2) * 8 + x) * 16 + (s % 2) * 8, 8)
            centre = to_aligned([fx[p, x0 + 2 + x, pl.ds(y0 + 8, 8), :] for p in range(5)])
            errors = []
            for m in range(4):
                lanes = slice(128 * m, 128 * m + 128)
                mask = ms[m, x0 + 2 + x, pl.ds(y0 + 8, 8), :] * alive
                pre = acc[pl.ds(at, 8), lanes] * scale_two + shift_two + centre[m]
                sig = 1.0 / (1.0 + jnp.exp(-pre))
                result = pre * sig * mask
                both = cotangent[x0 + x, pl.ds(y16, 16), lanes].astype(F32)
                target = jnp.where(odd, both[8:16], both[0:8])
                grad = target * mask * (sig * (1.0 + pre * (1.0 - sig)))
                error = grad * scale_two
                errors.append(error)
                er2[pl.ds(at, 8), lanes] = error
                grads_out[s, x, :, lanes] = grad
                result = jnp.where(
                    odd,
                    jnp.concatenate([zero, result], axis=0),
                    jnp.concatenate([result, zero], axis=0),
                )
                now = out[x0 + x, pl.ds(y16, 16), lanes].astype(F32)
                out[x0 + x, pl.ds(y16, 16), lanes] = (now + result).astype(BF16)
            for p, v in enumerate(to_shifted(errors)):
                e2[s, p, x + 2, 0:8, :] = zero
                e2[s, p, x + 2, 8:16, :] = v
                e2[s, p, x + 2, 16:24, :] = zero
        return 0

    lax.fori_loop(0, ACT_MAX, finish_two, 0)

    def gather_three(s, _):
        for p in range(5):
            for oy in range(3):
                lane = (p * 3 + oy) * 128
                c3[s, :, :, lane : lane + 128] = e2[s, p, :, 6 + oy : 22 + oy, :].astype(BF16)
        return 0

    lax.fori_loop(0, ACT_MAX, gather_three, 0)
    ets[0:128] = jnp.zeros((128, ets.shape[1]), BF16)
    ets[640:768] = jnp.zeros((128, ets.shape[1]), BF16)
    ets[128:640] = er2[...].astype(BF16).T
    convolve(c3, bands_c, acc, 10)

    def finish_three(i, _):
        for k in range(4):
            at = pl.multiple_of((i * 4 + k) * 16, 16)
            for m in range(4):
                lanes = slice(128 * m, 128 * m + 128)
                error = acc[pl.ds(at, 16), lanes] * slope[pl.ds(at, 16), lanes]
                errors_out[pl.ds(at, 16), lanes] = error.astype(BF16)
        return 0

    lax.fori_loop(0, ACT_MAX * 10 // 4, finish_three, 0)

    def weight_sums(source, errors_t, xs, which):
        rows = source.shape[0] * xs * 16
        for ox in range(3):
            sums = None
            for p in range(5):
                part = source[:, ox : ox + xs, :, 384 * p : 384 * p + 384].reshape(rows, 384)
                part = jnp.dot(
                    errors_t[128 * p : 128 * p + 256, :], part, preferred_element_type=F32
                )
                sums = part if sums is None else sums + part
            for oy in range(3):
                block = sums[:, 128 * oy : 128 * oy + 128]
                turned = turn(block)
                for oz in range(3):
                    one, two = 64 * (2 - oz), 64 * (3 - oz)
                    n = ox * 9 + oy * 3 + oz
                    if which == 0:
                        folded[n] = block[one : one + 64] + turned[two : two + 64]
                    else:
                        v = turned[one : one + 64] + block[two : two + 64]
                        total[n] = jnp.where(low_row, folded[n], v).astype(BF16)

    et1[0:128] = jnp.zeros((128, et1.shape[1]), BF16)
    et1[640:768] = jnp.zeros((128, et1.shape[1]), BF16)
    et1[128:640] = errors_out[...].T
    weight_sums(c1, et1, 10, 0)
    weight_sums(c2, ets, 8, 1)
    total[27] = jnp.zeros((64, 128), BF16)
    mine = core[0] * 14
    keep[...] = total[pl.ds(mine, 14)]
    send[...] = total[pl.ds(14 - mine, 14)]


def brick_call(slots, core, packed, above, below, left, right, cotangent, tiles, *vectors):
    lx, ly, width = cotangent.shape
    n = ACT_MAX
    wide = ly + 16
    return pl.pallas_call(
        brick_kernel,
        out_shape=(
            shape((lx, ly, width), BF16),
            shape((n * 160, width), BF16),
            shape((n, 8, 8, width), F32),
            shape((14, 64, 128), BF16),
            shape((14, 64, 128), BF16),
        ),
        in_specs=[SMEM, SMEM] + [VMEM] * 11,
        out_specs=(VMEM,) * 5,
        scratch_shapes=[
            pltpu.VMEM((5, lx + 4, wide, 128), F32),
            pltpu.VMEM((4, lx + 4, wide, 128), F32),
            pltpu.VMEM((3, 1152, 256), BF16),
            pltpu.VMEM((3, 1152, 256), BF16),
            pltpu.VMEM((3, 1152, 256), BF16),
            pltpu.VMEM((n, 12, 16, 1920), BF16),
            pltpu.VMEM((n // 2, 10, 16, 1920), BF16),
            pltpu.VMEM((n, 12, 16, 1920), BF16),
            pltpu.VMEM((n * 160, width), F32),
            pltpu.VMEM((n * 160, width), F32),
            pltpu.VMEM((n, 5, 10, 16, 128), F32),
            pltpu.VMEM((n, 5, 12, 24, 128), F32),
            pltpu.VMEM((n * 64, width), F32),
            pltpu.VMEM((768, n * 64), BF16),
            pltpu.VMEM((768, n * 160), BF16),
            pltpu.VMEM((27, 64, 128), F32),
            pltpu.VMEM((28, 64, 128), BF16),
        ],
        name="bricks",
    )(slots, core, packed, above, below, left, right, cotangent, tiles, *vectors)


def input_kernel(
    slots, errors, grads, codes, tiles, grad_own, grad_left, grad_right, e1, c4, bands, acc, grid
):
    lx, ly = grad_own.shape[0] - 4, grad_own.shape[1]
    wide = grid.shape[2]
    build_bands(bands, lambda t, d: tiles[t, d])

    def clear_row(i, _):
        for k in range(2):
            for m in range(4):
                grid[m, 2 * i + k] = jnp.zeros((wide, 128), F32)
        return 0

    lax.fori_loop(0, (lx + 4) // 2, clear_row, 0)

    def spread(s, _):
        for p in range(5):
            for x in (0, 1, 12, 13):
                e1[p, x] = jnp.zeros((24, 128), F32)
        for x in range(10):
            at = pl.multiple_of((s * 10 + x) * 16, 16)
            rows = [
                errors[pl.ds(at, 16), 128 * m : 128 * m + 128].astype(F32) for m in range(4)
            ]
            for p, v in enumerate(to_shifted(rows)):
                e1[p, x + 2, 0:8, :] = jnp.zeros((8, 128), F32)
                e1[p, x + 2, 8:24, :] = v
        for p in range(5):
            for oy in range(3):
                lane = (p * 3 + oy) * 128
                c4[s, :, :, lane : lane + 128] = e1[p, :, 6 + oy : 22 + oy, :].astype(BF16)
        return 0

    lax.fori_loop(0, ACT_MAX, spread, 0)
    convolve(c4, bands, acc, 12)

    def finish(s, _):
        x0, y0, live = place(slots, s)
        for x in range(12):
            at = pl.multiple_of((s * 12 + x) * 16, 16)
            for m in range(4):
                lanes = slice(128 * m, 128 * m + 128)
                view = grid.at[m, x0 + x, pl.ds(y0, 24), :]
                view[6:22, :] = view[6:22, :] + acc[pl.ds(at, 16), lanes]
        for x in range(8):
            for m in range(4):
                lanes = slice(128 * m, 128 * m + 128)
                view = grid.at[m, x0 + 2 + x, pl.ds(y0 + 8, 8), :]
                view[...] = view[...] + grads[s, x, :, lanes]
        return 0

    lax.fori_loop(0, ACT_MAX, finish, 0)

    def write_row(x, inside):
        low_row = low_lanes((1, 128))
        if inside:
            v = codes[x - 2].astype(F32)
            bounds = decoded(jnp.where(low_row, v, turn(v)))
        for m in range(4):
            lanes = slice(128 * m, 128 * m + 128)
            v = grid[m, x, 8 : 8 + ly, :]
            if inside:
                v = jnp.where(mask_of(bounds, 2 * m), v, 0.0)
            grad_own[x, :, lanes] = v.astype(BF16)
            grad_left[x, :, lanes] = grid[m, x, 6:8, :].astype(BF16)
            grad_right[x, :, lanes] = grid[m, x, 8 + ly : 10 + ly, :].astype(BF16)

    def own_rows(i, _):
        for k in range(2):
            write_row(2 + 2 * i + k, True)
        return 0

    lax.fori_loop(0, lx // 2, own_rows, 0)
    for x in (0, 1, lx + 2, lx + 3):
        write_row(x, False)


def input_call(slots, errors, grads, packed, tiles):
    lx, ly, wide = packed.shape
    width = wide - 128
    n = ACT_MAX
    return pl.pallas_call(
        input_kernel,
        out_shape=(
            shape((lx + 4, ly, width), BF16),
            shape((lx + 4, 2, width), BF16),
            shape((lx + 4, 2, width), BF16),
        ),
        grid=(1,),
        in_specs=[
            SMEM,
            VMEM,
            VMEM,
            pl.BlockSpec((lx, ly, 128), lambda i: (0, 0, 0)),
            VMEM,
        ],
        out_specs=(VMEM,) * 3,
        scratch_shapes=[
            pltpu.VMEM((5, 14, 24, 128), F32),
            pltpu.VMEM((n, 14, 16, 1920), BF16),
            pltpu.VMEM((3, 1152, 256), BF16),
            pltpu.VMEM((n * 192, width), F32),
            pltpu.VMEM((4, lx + 4, ly + 16, 128), F32),
        ],
        name="inputs",
    )(slots, errors, grads, packed, tiles)


def ends_kernel(above, below, from_left, from_right, top, bottom):
    ly = above.shape[1]
    lx = from_left.shape[0] - 4
    for source, base, target in ((above, 0, top), (below, lx + 2, bottom)):
        for x in range(2):
            v = source[x].astype(F32)
            one = jnp.concatenate(
                [from_left[base + x].astype(F32), jnp.zeros((6, v.shape[1]), F32)], axis=0
            )
            two = jnp.concatenate(
                [jnp.zeros((6, v.shape[1]), F32), from_right[base + x].astype(F32)], axis=0
            )
            v = jnp.concatenate([v[0:8] + one, v[8 : ly - 8], v[ly - 8 : ly] + two], axis=0)
            target[x] = v.astype(BF16)


def ends_call(grads, from_left, from_right):
    lx4, ly, width = grads.shape
    half = lx4 // 2 - 1
    return pl.pallas_call(
        ends_kernel,
        out_shape=(shape((2, ly, width), BF16), shape((2, ly, width), BF16)),
        grid=(1,),
        in_specs=[
            pl.BlockSpec((2, ly, width), lambda i: (0, 0, 0)),
            pl.BlockSpec((2, ly, width), lambda i: (half, 0, 0)),
            VMEM,
            VMEM,
        ],
        out_specs=(VMEM, VMEM),
        name="ends",
    )(grads, grads, from_left, from_right)


def join_kernel(grads, codes, from_left, from_right, from_above, from_below, grad_features):
    lx, ly = grad_features.shape[0], grad_features.shape[1]
    low_row = low_lanes((1, 128))

    def row(x, extra):
        code = codes[x].astype(F32)
        bounds = decoded(jnp.where(low_row, code, turn(code)))
        for m in range(4):
            lanes = slice(128 * m, 128 * m + 128)
            v = grads[x + 2, :, lanes].astype(F32)
            zero = jnp.zeros((6, 128), F32)
            one = jnp.concatenate([from_left[x + 2, :, lanes].astype(F32), zero], axis=0)
            two = jnp.concatenate([zero, from_right[x + 2, :, lanes].astype(F32)], axis=0)
            v = jnp.concatenate([v[0:8] + one, v[8 : ly - 8], v[ly - 8 : ly] + two], axis=0)
            if extra is not None:
                v = v + extra[0][extra[1], :, lanes].astype(F32)
            grad_features[x, :, lanes] = jnp.where(mask_of(bounds, 2 * m), v, 0.0).astype(BF16)

    def inner(i, _):
        for k in range(2):
            row(2 + 2 * i + k, None)
        return 0

    lax.fori_loop(0, (lx - 4) // 2, inner, 0)
    for x in range(2):
        row(x, (from_above, x))
        row(lx - 2 + x, (from_below, x))


def join_call(grads, packed, from_left, from_right, from_above, from_below):
    lx4, ly, width = grads.shape
    lx = lx4 - 4
    return pl.pallas_call(
        join_kernel,
        out_shape=shape((lx, ly, width), BF16),
        grid=(1,),
        in_specs=[VMEM, pl.BlockSpec((lx, ly, 128), lambda i: (0, 0, 0))] + [VMEM] * 4,
        out_specs=VMEM,
        name="join",
    )(grads, packed, from_left, from_right, from_above, from_below)


def pair_kernel(member, keep, got, *parts):
    for o, part in enumerate(parts):
        at = member[0] ^ o
        part[...] = (keep[at].astype(F32) + got[at].astype(F32)).astype(BF16)


def pair_call(member, keep, got, count):
    rows = keep.shape[0] * keep.shape[1] // count
    keep, got = keep.reshape(count, rows, 128), got.reshape(count, rows, 128)
    return pl.pallas_call(
        pair_kernel,
        out_shape=tuple(shape((rows, 128), BF16) for _ in range(count)),
        in_specs=[SMEM, VMEM, VMEM],
        out_specs=(VMEM,) * count,
        name="pair",
    )(member, keep, got)


def seat_kernel(member, *refs):
    parts, whole = refs[:-1], refs[-1]
    for o, part in enumerate(parts):
        whole[member[0] ^ o] = part[...]


def seat_call(member, parts):
    rows = parts[0].shape[0]
    return pl.pallas_call(
        seat_kernel,
        out_shape=shape((len(parts), rows, 128), BF16),
        in_specs=[SMEM] + [VMEM] * len(parts),
        out_specs=VMEM,
        name="seat",
    )(member, *parts)


def sums_kernel(core, mine, other, grad_one, grad_two, both, *, scale):
    both[core[0]] = mine[...]
    both[1 - core[0]] = other[...]
    for n in range(27):
        v = both[n // 14, n % 14].astype(F32).T * scale
        grad_one[n] = v[0:64]
        grad_two[n] = v[64:128]


def sums_call(core, mine, other, scale):
    return pl.pallas_call(
        functools.partial(sums_kernel, scale=scale),
        out_shape=(shape((27, 64, 64), F32), shape((27, 64, 64), F32)),
        in_specs=[SMEM, VMEM, VMEM],
        out_specs=(VMEM, VMEM),
        scratch_shapes=[pltpu.VMEM((2, 14, 64, 128), BF16)],
        name="sums",
    )(core, mine, other)


def reduce_sums(keep, send):
    nx, ny = lax.axis_size("gx"), lax.axis_size("gy")
    gx, gy = lax.axis_index("gx"), lax.axis_index("gy")
    core = (gy % 2).reshape(1)
    lines = ny // 2
    near = max(nx // 4, 1)
    far = nx // near

    got = flat_permute(send, lambda x, y: (x, y ^ 1))
    count = lines * near
    member = ((gy // 2) * near + gx % near).reshape(1)

    def in_plane(o):
        def move(x, y):
            to = ((y // 2) * near + x % near) ^ o
            return (x // near * near + to % near, to // near * 2 + y % 2)

        return move

    def along(o):
        return lambda x, y: (((x // near) ^ o) * near + x % near, y)

    parts = pair_call(member, keep, got, count)
    own = parts[0].astype(F32)
    for o in range(1, count):
        own = own + flat_permute(parts[o], in_plane(o)).astype(F32)
    own = own.astype(BF16)
    values = [own.astype(F32)] + [flat_permute(own, along(o)).astype(F32) for o in range(1, far)]
    while len(values) > 1:
        values = [values[i] + values[i + 1] for i in range(0, len(values), 2)]
    own = values[0].astype(BF16)
    others = [flat_permute(own, in_plane(o)) for o in range(1, count)]
    half = seat_call(member, [own] + others).reshape(keep.shape)
    other = flat_permute(half, lambda x, y: (x, y ^ 1))
    return core, half, other


def shards(
    features, cotangent, low, high, weight_one, weight_two, scale_one, shift_one, scale_two,
    shift_two,
):
    packed, top, bottom, first, last = edge_call(features, low, high)
    above = shifted_in(bottom, "gx", 1)
    below = shifted_in(top, "gx", -1)
    slots, tiles, tiles_last = tile_call(low, high, weight_one, weight_two)
    to_left, to_right = side_call(above, below, first, last)
    left = shifted_in(to_right, "gy", 1)
    right = shifted_in(to_left, "gy", -1)
    core = (lax.axis_index("gy") % 2).reshape(1)
    vectors = [v.reshape(1, -1) for v in (scale_one, shift_one, scale_two, shift_two)]
    out, errors, grads, keep, send = brick_call(
        slots, core, packed, above, below, left, right, cotangent, tiles, *vectors
    )
    core, half, other = reduce_sums(keep, send)
    grads, grad_left, grad_right = input_call(slots, errors, grads, packed, tiles_last)
    from_right = shifted_in(grad_left, "gy", -1)
    from_left = shifted_in(grad_right, "gy", 1)
    top, bottom = ends_call(grads, from_left, from_right)
    from_below = shifted_in(top, "gx", -1)
    from_above = shifted_in(bottom, "gx", 1)
    grad_features = join_call(grads, packed, from_left, from_right, from_above, from_below)
    capacity = lax.axis_size("gx") * lax.axis_size("gy") * SHARE
    grad_one, grad_two = sums_call(core, half, other, 1.0 / capacity)
    return (out, grad_features, grad_one, grad_two)


def solution(mesh):
    whole = P("gx", "gy", None)
    columns = P("gx", "gy")
    return jax.shard_map(
        shards,
        mesh=mesh,
        in_specs=(whole, whole, columns, columns) + (P(),) * 6,
        out_specs=(whole, whole, P(), P()),
        check_vma=False,
    )
```

```python
import functools

import jax
import jax.numpy as jnp
from jax import lax
from jax.experimental import pallas as pl
from jax.experimental.pallas import tpu as pltpu
from jax.sharding import PartitionSpec as P


BRICK = 8
ACT_MAX = 4
SHARE = 2
F32 = jnp.float32
BF16 = jnp.bfloat16


def shifted_in(array, axis, by):
    devices = lax.axis_size(axis)
    pairs = [(i, i + by) for i in range(devices) if 0 <= i + by < devices]
    return lax.ppermute(array, axis, pairs)


def low_lanes(shape):
    return lax.broadcasted_iota(jnp.int32, shape, len(shape) - 1) < 64


def turn(value):
    return pltpu.roll(value, 64, value.ndim - 1)


def to_shifted(pairs):
    turned = [turn(v) for v in pairs]
    low = low_lanes(pairs[0].shape)
    zero = jnp.zeros_like(pairs[0])
    before = [zero] + turned
    after = turned + [zero]
    return [jnp.where(low, b, a) for b, a in zip(before, after)]


def to_aligned(shifted):
    turned = [turn(v) for v in shifted]
    low = low_lanes(shifted[0].shape)
    return [jnp.where(low, turned[m], turned[m + 1]) for m in range(len(shifted) - 1)]


VMEM = pl.BlockSpec(memory_space=pltpu.VMEM)
SMEM = pl.BlockSpec(memory_space=pltpu.SMEM)
shape = jax.ShapeDtypeStruct


EMPTY_FEATURE = 256.0


def encode(feature, low, high, z_low):
    z = jnp.where(low_lanes((1, 128)), 1.0 * z_low, z_low + 1.0)
    feature = jnp.where(feature == 0.0, EMPTY_FEATURE, feature)
    return jnp.where((z >= low) & (z < high), feature, 0.0)


def column_bounds(low, high, x):
    ly = low.shape[1]
    code = (low[x : x + 1, :] * 16 + high[x : x + 1, :]).astype(F32)
    same = lax.broadcasted_iota(jnp.int32, (ly, ly), 0) == lax.broadcasted_iota(
        jnp.int32, (ly, ly), 1
    )
    spread = jnp.where(same, code, 0.0).astype(BF16)
    column = jnp.dot(spread, jnp.ones((ly, 128), BF16), preferred_element_type=F32)
    floor = jnp.floor(column * (1.0 / 16.0))
    return floor, column - 16.0 * floor


def strip_kernel(top_in, bottom_in, low, high, top, bottom):
    lx = low.shape[0]
    for source, target, base in ((top_in, top, 0), (bottom_in, bottom, lx - 2)):
        for x in range(2):
            floor, high_of = column_bounds(low, high, base + x)
            for m in range(4):
                lanes = slice(128 * m, 128 * m + 128)
                v = encode(source[x, :, lanes].astype(F32), floor, high_of, 2 * m)
                target[x, :, lanes] = v.astype(BF16)


def strip_call(features, low, high):
    lx, ly, width = features.shape
    end = lx // 2 - 1
    return pl.pallas_call(
        strip_kernel,
        out_shape=(shape((2, ly, width), BF16), shape((2, ly, width), BF16)),
        grid=(1,),
        in_specs=[
            pl.BlockSpec((2, ly, width), lambda i: (0, 0, 0)),
            pl.BlockSpec((2, ly, width), lambda i: (end, 0, 0)),
            VMEM,
            VMEM,
        ],
        out_specs=(VMEM, VMEM),
        name="strips",
    )(features, features, low, high)


def side_kernel(above, below, first, last, to_left, to_right):
    lx = first.shape[0]
    ly = above.shape[1]
    for strip, base in ((above, 0), (below, lx + 2)):
        for x in range(2):
            v = strip[x].astype(F32)
            to_left[base + x] = v[0:2].astype(BF16)
            to_right[base + x] = v[ly - 2 : ly].astype(BF16)
    to_left[2 : lx + 2] = first[...]
    to_right[2 : lx + 2] = last[...]


def side_call(above, below, first, last):
    tall = (first.shape[0] + 4,) + first.shape[1:]
    return pl.pallas_call(
        side_kernel,
        out_shape=(shape(tall, BF16), shape(tall, BF16)),
        in_specs=[VMEM] * 4,
        out_specs=(VMEM, VMEM),
        name="sides",
    )(above, below, first, last)


def tile_kernel(
    features, low, high, weight_one, weight_two, slots, tiles, tiles_last, packed, first, last
):
    lx, ly = low.shape
    filled = jnp.where(high[...] > low[...], 1.0, 0.0)
    rows = [
        jnp.sum(filled[8 * i : 8 * i + 8], axis=0, keepdims=True) for i in range(lx // BRICK)
    ]
    rows = jnp.concatenate(rows + [jnp.zeros((8 - len(rows), ly), F32)], axis=0)
    among = lax.broadcasted_iota(jnp.int32, (ly, 128), 0) // BRICK
    among = among == lax.broadcasted_iota(jnp.int32, (ly, 128), 1)
    counts = jnp.dot(
        rows.astype(BF16), jnp.where(among, 1.0, 0.0).astype(BF16), preferred_element_type=F32
    )
    for i in range(3 * ACT_MAX):
        slots[i] = 0
    r = lax.broadcasted_iota(jnp.int32, (8, 128), 0)
    c = lax.broadcasted_iota(jnp.int32, (8, 128), 1)
    flags = [
        jnp.sum(jnp.where((r == i) & (c == j), counts, 0.0))
        for i in range(lx // BRICK)
        for j in range(ly // BRICK)
    ]
    seat = jnp.int32(0)
    for n, flag in enumerate(flags):
        i, j = n // (ly // BRICK), n % (ly // BRICK)
        has = (flag > 0.5) & (seat < ACT_MAX)

        @pl.when(has)
        def _(seat=seat, i=i, j=j):
            slots[seat] = i
            slots[ACT_MAX + seat] = j
            slots[2 * ACT_MAX + seat] = 1

        seat = seat + has.astype(jnp.int32)

    for x in range(lx):
        floor, high_of = column_bounds(low, high, x)
        for m in range(4):
            lanes = slice(128 * m, 128 * m + 128)
            v = encode(features[x, :, lanes].astype(F32), floor, high_of, 2 * m)
            packed[x, :, lanes] = v.astype(BF16)
            first[x, :, lanes] = v[0:2].astype(BF16)
            last[x, :, lanes] = v[ly - 2 : ly].astype(BF16)

    zero = jnp.zeros((64, 64), BF16)
    for conv, weight in enumerate((weight_one, weight_two, weight_two, weight_one)):
        for tap in range(9):
            taps = []
            for oz in range(3):
                if conv < 2:
                    taps.append(weight[3 * tap + oz])
                else:
                    taps.append(weight[26 - 3 * tap - oz].astype(F32).T.astype(BF16))
            taps = [zero] + taps + [zero]
            for d in range(4):
                tile = jnp.concatenate([taps[d + 1], taps[d]], axis=1)
                if conv < 3:
                    tiles[conv, tap, d] = tile
                else:
                    tiles_last[tap, d] = tile


def tile_call(features, low, high, weight_one, weight_two):
    lx, _, width = features.shape
    return pl.pallas_call(
        tile_kernel,
        out_shape=(
            shape((3 * ACT_MAX,), jnp.int32),
            shape((3, 9, 4, 64, 128), BF16),
            shape((9, 4, 64, 128), BF16),
            shape(features.shape, BF16),
            shape((lx, 2, width), BF16),
            shape((lx, 2, width), BF16),
        ),
        in_specs=[VMEM] * 5,
        out_specs=(SMEM,) + (VMEM,) * 5,
        name="tiles",
    )(features, low, high, weight_one, weight_two)


def build_bands(bands, tile_at):
    bands[...] = jnp.zeros(bands.shape, BF16)
    for ox in range(3):
        for oy in range(3):
            for r in range(6):
                for q in range(2):
                    d = r - 2 * q
                    if 0 <= d < 4:
                        row = ((r // 2) * 3 + oy) * 128 + (r % 2) * 64
                        bands[ox, row : row + 64, 128 * q : 128 * q + 128] = tile_at(
                            ox * 3 + oy, d
                        )


def convolve(source, bands, acc, xs):
    rows = source.shape[0] * xs * 16
    for half in range(2):
        total = None
        for ox in range(3):
            part = source[:, ox : ox + xs, :, 768 * half : 768 * half + 1152]
            part = jnp.dot(part.reshape(rows, 1152), bands[ox], preferred_element_type=F32)
            total = part if total is None else total + part
        acc[0:rows, 256 * half : 256 * half + 256] = total


def place(slots, s):
    x0 = pl.multiple_of(slots[s] * 8, 8)
    y0 = pl.multiple_of(slots[ACT_MAX + s] * 8, 8)
    return x0, y0, slots[2 * ACT_MAX + s]


def twice(row):
    return jnp.concatenate([row, row], axis=1)


def brick_kernel(
    slots, packed, above, below, left, right, cotangent, tiles, s_one, t_one, s_two, t_two,
    out, errors_out, grads_out, total,
    fx, ms, bands_a, bands_b, bands_c, c1, c2, c3, acc, slope, h, e2, er2, ets, et1, folded,
):
    lx, ly = out.shape[0], out.shape[1]
    low_row = low_lanes((1, 128))
    scale_one, shift_one = twice(s_one[...]), twice(t_one[...])
    scale_two, shift_two = twice(s_two[...]), twice(t_two[...])

    build_bands(bands_a, lambda t, d: tiles[0, t, d])

    def put(x, strip, start, stop):
        pieces = []
        for m in range(4):
            v = strip(m).astype(F32)
            ms[m, x, start:stop, :] = jnp.where(v == 0.0, 0.0, 1.0)
            pieces.append(jnp.where(v == EMPTY_FEATURE, 0.0, v))
        for p, v in enumerate(to_shifted(pieces)):
            fx[p, x, start:stop, :] = v

    def own_row(i, _):
        for k in range(2):
            x = 2 * i + k
            put(x + 2, lambda m: packed[x, :, 128 * m : 128 * m + 128], 8, 8 + ly)
            out[x] = jnp.zeros(out.shape[1:], BF16)
        return 0

    lax.fori_loop(0, lx // 2, own_row, 0)
    for x in range(2):
        put(x, lambda m: above[x, :, 128 * m : 128 * m + 128], 8, 8 + ly)
        put(lx + 2 + x, lambda m: below[x, :, 128 * m : 128 * m + 128], 8, 8 + ly)

    def side_row(i, _):
        for k in range(4):
            x = 4 * i + k
            for base in (0, 8 + ly):
                for m in range(4):
                    ms[m, x, base : base + 8, :] = jnp.zeros((8, 128), F32)
                for p in range(5):
                    fx[p, x, base : base + 8, :] = jnp.zeros((8, 128), F32)
            put(x, lambda m: left[x, :, 128 * m : 128 * m + 128], 6, 8)
            put(x, lambda m: right[x, :, 128 * m : 128 * m + 128], 8 + ly, 10 + ly)
        return 0

    lax.fori_loop(0, (lx + 4) // 4, side_row, 0)

    def gather_one(s, _):
        x0, y0, _ = place(slots, s)
        for p in range(5):
            view = fx.at[p, pl.ds(x0, 12), pl.ds(y0, 24), :]
            for oy in range(3):
                lane = (p * 3 + oy) * 128
                c1[s, :, :, lane : lane + 128] = view[:, 6 + oy : 22 + oy, :].astype(BF16)
        return 0

    lax.fori_loop(0, ACT_MAX, gather_one, 0)
    build_bands(bands_b, lambda t, d: tiles[1, t, d])
    convolve(c1, bands_a, acc, 10)

    def hidden_of(i, _):
        s = i // 2
        x0, y0, live = place(slots, s)
        keep_rows = lax.broadcasted_iota(jnp.int32, (16, 128), 0) < jnp.where(live > 0, 10, 0)
        for k in range(5):
            x = (i % 2) * 5 + k
            at = pl.multiple_of((s * 10 + x) * 16, 16)
            pieces = []
            for m in range(4):
                lanes = slice(128 * m, 128 * m + 128)
                mask = ms.at[m, x0 + x + 1, pl.ds(y0, 24), :][7:23, :]
                mask = jnp.where(keep_rows, mask, 0.0)
                pre = acc[pl.ds(at, 16), lanes] * scale_one + shift_one
                sig = 1.0 / (1.0 + jnp.exp(-pre))
                pieces.append(pre * sig * mask)
                slope[pl.ds(at, 16), lanes] = (
                    scale_one * mask * (sig * (1.0 + pre * (1.0 - sig)))
                )
            for p, v in enumerate(to_shifted(pieces)):
                h[s, p, x] = v
        return 0

    lax.fori_loop(0, 2 * ACT_MAX, hidden_of, 0)

    def gather_two(q, _):
        for p in range(5):
            for oy in range(3):
                lane = (p * 3 + oy) * 128
                one = h[2 * q, p, :, oy : oy + 8, :]
                two = h[2 * q + 1, p, :, oy : oy + 8, :]
                c2[q, :, :, lane : lane + 128] = jnp.concatenate([one, two], axis=1).astype(BF16)
        return 0

    lax.fori_loop(0, ACT_MAX // 2, gather_two, 0)
    build_bands(bands_c, lambda t, d: tiles[2, t, d])
    convolve(c2, bands_b, acc, 8)

    def finish_two(s, _):
        x0, y0, live = place(slots, s)
        odd = lax.rem(slots[ACT_MAX + s], 2) == 1
        y16 = pl.multiple_of(slots[ACT_MAX + s] // 2 * 16, 16)
        alive = jnp.where(live > 0, 1.0, 0.0)
        zero = jnp.zeros((8, 128), F32)
        for p in range(5):
            for x in (0, 1, 10, 11):
                e2[s, p, x] = jnp.zeros((24, 128), F32)
        for x in range(8):
            at = pl.multiple_of(((s // 2) * 8 + x) * 16 + (s % 2) * 8, 8)
            centre = to_aligned([fx[p, x0 + 2 + x, pl.ds(y0 + 8, 8), :] for p in range(5)])
            errors = []
            for m in range(4):
                lanes = slice(128 * m, 128 * m + 128)
                mask = ms[m, x0 + 2 + x, pl.ds(y0 + 8, 8), :] * alive
                pre = acc[pl.ds(at, 8), lanes] * scale_two + shift_two + centre[m]
                sig = 1.0 / (1.0 + jnp.exp(-pre))
                result = pre * sig * mask
                both = cotangent[x0 + x, pl.ds(y16, 16), lanes].astype(F32)
                target = jnp.where(odd, both[8:16], both[0:8])
                grad = target * mask * (sig * (1.0 + pre * (1.0 - sig)))
                error = grad * scale_two
                errors.append(error)
                er2[pl.ds(at, 8), lanes] = error
                grads_out[s, x, :, lanes] = grad
                result = jnp.where(
                    odd,
                    jnp.concatenate([zero, result], axis=0),
                    jnp.concatenate([result, zero], axis=0),
                )
                now = out[x0 + x, pl.ds(y16, 16), lanes].astype(F32)
                out[x0 + x, pl.ds(y16, 16), lanes] = (now + result).astype(BF16)
            for p, v in enumerate(to_shifted(errors)):
                e2[s, p, x + 2, 0:8, :] = zero
                e2[s, p, x + 2, 8:16, :] = v
                e2[s, p, x + 2, 16:24, :] = zero
        return 0

    lax.fori_loop(0, ACT_MAX, finish_two, 0)

    def gather_three(s, _):
        for p in range(5):
            for oy in range(3):
                lane = (p * 3 + oy) * 128
                c3[s, :, :, lane : lane + 128] = e2[s, p, :, 6 + oy : 22 + oy, :].astype(BF16)
        return 0

    lax.fori_loop(0, ACT_MAX, gather_three, 0)
    ets[0:128] = jnp.zeros((128, ets.shape[1]), BF16)
    ets[640:768] = jnp.zeros((128, ets.shape[1]), BF16)
    ets[128:640] = er2[...].astype(BF16).T
    convolve(c3, bands_c, acc, 10)

    def finish_three(i, _):
        for k in range(4):
            at = pl.multiple_of((i * 4 + k) * 16, 16)
            for m in range(4):
                lanes = slice(128 * m, 128 * m + 128)
                error = acc[pl.ds(at, 16), lanes] * slope[pl.ds(at, 16), lanes]
                errors_out[pl.ds(at, 16), lanes] = error.astype(BF16)
        return 0

    lax.fori_loop(0, ACT_MAX * 10 // 4, finish_three, 0)

    def weight_sums(source, errors_t, xs, which):
        rows = source.shape[0] * xs * 16
        for ox in range(3):
            sums = None
            for p in range(5):
                part = source[:, ox : ox + xs, :, 384 * p : 384 * p + 384].reshape(rows, 384)
                part = jnp.dot(
                    errors_t[128 * p : 128 * p + 256, :], part, preferred_element_type=F32
                )
                sums = part if sums is None else sums + part
            for oy in range(3):
                block = sums[:, 128 * oy : 128 * oy + 128]
                turned = turn(block)
                for oz in range(3):
                    one, two = 64 * (2 - oz), 64 * (3 - oz)
                    n = ox * 9 + oy * 3 + oz
                    if which == 0:
                        folded[n] = block[one : one + 64] + turned[two : two + 64]
                    else:
                        v = turned[one : one + 64] + block[two : two + 64]
                        total[n] = jnp.where(low_row, folded[n], v).astype(BF16)

    et1[0:128] = jnp.zeros((128, et1.shape[1]), BF16)
    et1[640:768] = jnp.zeros((128, et1.shape[1]), BF16)
    et1[128:640] = errors_out[...].T
    weight_sums(c1, et1, 10, 0)
    weight_sums(c2, ets, 8, 1)
    total[27] = jnp.zeros((64, 128), BF16)


def brick_call(slots, packed, above, below, left, right, cotangent, tiles, *vectors):
    lx, ly, width = cotangent.shape
    n = ACT_MAX
    wide = ly + 16
    return pl.pallas_call(
        brick_kernel,
        out_shape=(
            shape((lx, ly, width), BF16),
            shape((n * 160, width), BF16),
            shape((n, 8, 8, width), F32),
            shape((28, 64, 128), BF16),
        ),
        in_specs=[SMEM] + [VMEM] * 11,
        out_specs=(VMEM,) * 4,
        scratch_shapes=[
            pltpu.VMEM((5, lx + 4, wide, 128), F32),
            pltpu.VMEM((4, lx + 4, wide, 128), F32),
            pltpu.VMEM((3, 1152, 256), BF16),
            pltpu.VMEM((3, 1152, 256), BF16),
            pltpu.VMEM((3, 1152, 256), BF16),
            pltpu.VMEM((n, 12, 16, 1920), BF16),
            pltpu.VMEM((n // 2, 10, 16, 1920), BF16),
            pltpu.VMEM((n, 12, 16, 1920), BF16),
            pltpu.VMEM((n * 160, width), F32),
            pltpu.VMEM((n * 160, width), F32),
            pltpu.VMEM((n, 5, 10, 16, 128), F32),
            pltpu.VMEM((n, 5, 12, 24, 128), F32),
            pltpu.VMEM((n * 64, width), F32),
            pltpu.VMEM((768, n * 64), BF16),
            pltpu.VMEM((768, n * 160), BF16),
            pltpu.VMEM((27, 64, 128), F32),
        ],
        name="bricks",
    )(slots, packed, above, below, left, right, cotangent, tiles, *vectors)


def input_kernel(
    slots, errors, grads, packed, tiles, grad_own, grad_above, grad_below, grad_left, grad_right,
    e1, c4, bands, acc, grid,
):
    lx, ly = grad_own.shape[0], grad_own.shape[1]
    wide = grid.shape[2]
    build_bands(bands, lambda t, d: tiles[t, d])

    def clear_row(i, _):
        for k in range(2):
            for m in range(4):
                grid[m, 2 * i + k] = jnp.zeros((wide, 128), F32)
        return 0

    lax.fori_loop(0, (lx + 4) // 2, clear_row, 0)

    def spread(s, _):
        for p in range(5):
            for x in (0, 1, 12, 13):
                e1[p, x] = jnp.zeros((24, 128), F32)
        for x in range(10):
            at = pl.multiple_of((s * 10 + x) * 16, 16)
            rows = [
                errors[pl.ds(at, 16), 128 * m : 128 * m + 128].astype(F32) for m in range(4)
            ]
            for p, v in enumerate(to_shifted(rows)):
                e1[p, x + 2, 0:8, :] = jnp.zeros((8, 128), F32)
                e1[p, x + 2, 8:24, :] = v
        for p in range(5):
            for oy in range(3):
                lane = (p * 3 + oy) * 128
                c4[s, :, :, lane : lane + 128] = e1[p, :, 6 + oy : 22 + oy, :].astype(BF16)
        return 0

    lax.fori_loop(0, ACT_MAX, spread, 0)
    convolve(c4, bands, acc, 12)

    def finish(s, _):
        x0, y0, _ = place(slots, s)
        for x in range(12):
            at = pl.multiple_of((s * 12 + x) * 16, 16)
            for m in range(4):
                lanes = slice(128 * m, 128 * m + 128)
                view = grid.at[m, x0 + x, pl.ds(y0, 24), :]
                view[6:22, :] = view[6:22, :] + acc[pl.ds(at, 16), lanes]
        for x in range(8):
            for m in range(4):
                lanes = slice(128 * m, 128 * m + 128)
                view = grid.at[m, x0 + 2 + x, pl.ds(y0 + 8, 8), :]
                view[...] = view[...] + grads[s, x, :, lanes]
        return 0

    lax.fori_loop(0, ACT_MAX, finish, 0)

    def own_rows(i, _):
        for k in range(2):
            x = 2 * i + k
            for m in range(4):
                lanes = slice(128 * m, 128 * m + 128)
                v = grid[m, x + 2, 8 : 8 + ly, :]
                v = jnp.where(packed[x, :, lanes].astype(F32) == 0.0, 0.0, v)
                grad_own[x, :, lanes] = v.astype(BF16)
                grad_left[x, :, lanes] = grid[m, x + 2, 6:8, :].astype(BF16)
                grad_right[x, :, lanes] = grid[m, x + 2, 8 + ly : 10 + ly, :].astype(BF16)
        return 0

    lax.fori_loop(0, lx // 2, own_rows, 0)
    for target, base in ((grad_above, 0), (grad_below, lx + 2)):
        for x in range(2):
            for m in range(4):
                lanes = slice(128 * m, 128 * m + 128)
                target[x, 0:ly, lanes] = grid[m, base + x, 8 : 8 + ly, :].astype(BF16)
                corners = [
                    grid[m, base + x, 6:8, :],
                    grid[m, base + x, 8 + ly : 10 + ly, :],
                    jnp.zeros((4, 128), F32),
                ]
                target[x, ly : ly + 8, lanes] = jnp.concatenate(corners, axis=0).astype(BF16)


def input_call(slots, errors, grads, packed, tiles):
    lx, ly, width = packed.shape
    n = ACT_MAX
    return pl.pallas_call(
        input_kernel,
        out_shape=(
            shape((lx, ly, width), BF16),
            shape((2, ly + 8, width), BF16),
            shape((2, ly + 8, width), BF16),
            shape((lx, 2, width), BF16),
            shape((lx, 2, width), BF16),
        ),
        in_specs=[SMEM] + [VMEM] * 4,
        out_specs=(VMEM,) * 5,
        scratch_shapes=[
            pltpu.VMEM((5, 14, 24, 128), F32),
            pltpu.VMEM((n, 14, 16, 1920), BF16),
            pltpu.VMEM((3, 1152, 256), BF16),
            pltpu.VMEM((n * 192, width), F32),
            pltpu.VMEM((4, lx + 4, ly + 16, 128), F32),
        ],
        name="inputs",
    )(slots, errors, grads, packed, tiles)


def ends_kernel(left, right, from_above, from_below, to_left, to_right):
    lx = left.shape[0]
    to_left[...] = left[...]
    to_right[...] = right[...]
    for source, base in ((from_above, 0), (from_below, lx - 2)):
        for x in range(2):
            v = source[x].astype(F32)
            for strip, target, at in ((left, to_left, 0), (right, to_right, 2)):
                target[base + x] = (strip[base + x].astype(F32) + v[at : at + 2]).astype(BF16)


def ends_call(left, right, from_above, from_below):
    ly, width = from_above.shape[1] - 8, from_above.shape[2]
    corners = pl.BlockSpec((2, 8, width), lambda i: (0, ly // 8, 0))
    return pl.pallas_call(
        ends_kernel,
        out_shape=(shape(left.shape, BF16), shape(left.shape, BF16)),
        grid=(1,),
        in_specs=[VMEM, VMEM, corners, corners],
        out_specs=(VMEM, VMEM),
        name="ends",
    )(left, right, from_above, from_below)


def join_kernel(
    grads, top, bottom, first, last, from_left, from_right, from_above, from_below, joined,
    rows_a, rows_b, cols_a, cols_b, sems,
):
    lx, ly, _ = joined.shape
    places = (
        (rows_a, lambda ref: ref.at[0:2]),
        (rows_b, lambda ref: ref.at[lx - 2 : lx]),
        (cols_a, lambda ref: ref.at[2 : lx - 2, 0:16, :]),
        (cols_b, lambda ref: ref.at[2 : lx - 2, ly - 16 : ly, :]),
    )
    copies = [
        pltpu.make_async_copy(at(grads), held, sems.at[n]) for n, (held, at) in enumerate(places)
    ]
    for copy in copies:
        copy.start()
    for copy in copies:
        copy.wait()
    width = rows_a.shape[2]

    def first_add(strip, rows):
        return jnp.concatenate([strip.astype(F32), jnp.zeros((rows - 2, width), F32)], axis=0)

    def last_add(strip, rows):
        return jnp.concatenate([jnp.zeros((rows - 2, width), F32), strip.astype(F32)], axis=0)

    for held, code, extra, base in (
        (rows_a, top, from_above, 0),
        (rows_b, bottom, from_below, lx - 2),
    ):
        for x in range(2):
            v = held[x].astype(F32) + extra[x, 0:ly].astype(F32)
            one = v[0:8] + first_add(from_left[base + x], 8)
            two = v[ly - 8 : ly] + last_add(from_right[base + x], 8)
            v = jnp.concatenate([one, v[8 : ly - 8], two], axis=0)
            held[x] = jnp.where(code[x].astype(F32) == 0.0, 0.0, v).astype(BF16)
    for x in range(2, lx - 2):
        kept = jnp.where(first[x].astype(F32) == 0.0, 0.0, from_left[x].astype(F32))
        kept = first_add(kept, 16)
        cols_a[x - 2] = (cols_a[x - 2].astype(F32) + kept).astype(BF16)
        kept = jnp.where(last[x].astype(F32) == 0.0, 0.0, from_right[x].astype(F32))
        kept = last_add(kept, 16)
        cols_b[x - 2] = (cols_b[x - 2].astype(F32) + kept).astype(BF16)
    copies = [
        pltpu.make_async_copy(held, at(joined), sems.at[n]) for n, (held, at) in enumerate(places)
    ]
    for copy in copies:
        copy.start()
    for copy in copies:
        copy.wait()


def join_call(grads, *strips):
    lx, ly, width = grads.shape
    anywhere = pl.BlockSpec(memory_space=pl.ANY)
    return pl.pallas_call(
        join_kernel,
        out_shape=shape(grads.shape, BF16),
        in_specs=[anywhere] + [VMEM] * 8,
        out_specs=anywhere,
        scratch_shapes=[
            pltpu.VMEM((2, ly, width), BF16),
            pltpu.VMEM((2, ly, width), BF16),
            pltpu.VMEM((lx - 4, 16, width), BF16),
            pltpu.VMEM((lx - 4, 16, width), BF16),
            pltpu.SemaphoreType.DMA((4,)),
        ],
        input_output_aliases={0: 0},
        name="join",
    )(grads, *strips)


def sums_kernel(sums, grad_one, grad_two, *, scale):
    for n in range(27):
        v = sums[64 * n : 64 * n + 64].astype(F32).T * scale
        grad_one[n] = v[0:64]
        grad_two[n] = v[64:128]


def sums_call(sums, scale):
    return pl.pallas_call(
        functools.partial(sums_kernel, scale=scale),
        out_shape=(shape((27, 64, 64), F32), shape((27, 64, 64), F32)),
        in_specs=[VMEM],
        out_specs=(VMEM, VMEM),
        name="sums",
    )(sums)


def shards(
    features, cotangent, low, high, weight_one, weight_two, scale_one, shift_one, scale_two,
    shift_two,
):
    nx, ny = lax.axis_size("gx"), lax.axis_size("gy")
    top, bottom = strip_call(features, low, high)
    above = shifted_in(bottom, "gx", 1)
    below = shifted_in(top, "gx", -1)
    slots, tiles, tiles_last, packed, first, last = tile_call(
        features, low, high, weight_one, weight_two
    )
    to_left, to_right = side_call(above, below, first, last)
    left = shifted_in(to_right, "gy", 1)
    right = shifted_in(to_left, "gy", -1)
    vectors = [v.reshape(1, -1) for v in (scale_one, shift_one, scale_two, shift_two)]
    out, errors, grads, sums = brick_call(
        slots, packed, above, below, left, right, cotangent, tiles, *vectors
    )

    devices = nx * ny
    parts = sums.reshape(devices, -1, 128)
    slots, errors, parts = lax.optimization_barrier((slots, errors, parts))
    got = lax.all_to_all(parts, ("gx", "gy"), 0, 0, tiled=True)
    own, grad_above, grad_below, grad_left, grad_right = input_call(
        slots, errors, grads, packed, tiles_last
    )
    from_below = shifted_in(grad_above, "gx", -1)
    from_above = shifted_in(grad_below, "gx", 1)
    got, own = lax.optimization_barrier((got, own))
    mine = jnp.sum(got.astype(F32), axis=0, keepdims=True).astype(BF16)
    back = lax.all_to_all(
        jnp.broadcast_to(mine, parts.shape), ("gx", "gy"), 0, 0, tiled=True
    )
    to_left, to_right = ends_call(grad_left, grad_right, from_above, from_below)
    from_right = shifted_in(to_left, "gy", -1)
    from_left = shifted_in(to_right, "gy", 1)
    grad_features = join_call(
        own, top, bottom, first, last, from_left, from_right, from_above, from_below
    )
    back, grad_features = lax.optimization_barrier((back, grad_features))
    grad_one, grad_two = sums_call(back.reshape(-1, 128), 1.0 / (devices * SHARE))
    return (out, grad_features, grad_one, grad_two)


def solution(mesh):
    whole = P("gx", "gy", None)
    columns = P("gx", "gy")

    return jax.shard_map(
        shards,
        mesh=mesh,
        in_specs=(whole, whole, columns, columns) + (P(),) * 6,
        out_specs=(whole, whole, P(), P()),
        check_vma=False,
    )
```

```python
import functools

import jax
import jax.numpy as jnp
from jax import lax
from jax.experimental import pallas as pl
from jax.experimental.pallas import tpu as pltpu
from jax.sharding import PartitionSpec as P


BRICK = 8
ACT_MAX = 4
SHARE = 2
F32 = jnp.float32
BF16 = jnp.bfloat16


def shifted_in(array, axis, by):
    devices = lax.axis_size(axis)
    pairs = [(i, i + by) for i in range(devices) if 0 <= i + by < devices]
    return lax.ppermute(array, axis, pairs)


def low_lanes(shape):
    return lax.broadcasted_iota(jnp.int32, shape, len(shape) - 1) < 64


def turn(value):
    return pltpu.roll(value, 64, value.ndim - 1)


def to_shifted(pairs):
    turned = [turn(v) for v in pairs]
    low = low_lanes(pairs[0].shape)
    zero = jnp.zeros_like(pairs[0])
    before = [zero] + turned
    after = turned + [zero]
    return [jnp.where(low, b, a) for b, a in zip(before, after)]


def to_aligned(shifted):
    turned = [turn(v) for v in shifted]
    low = low_lanes(shifted[0].shape)
    return [jnp.where(low, turned[m], turned[m + 1]) for m in range(len(shifted) - 1)]


VMEM = pl.BlockSpec(memory_space=pltpu.VMEM)
SMEM = pl.BlockSpec(memory_space=pltpu.SMEM)
shape = jax.ShapeDtypeStruct
held = pltpu.VMEM


def near(*arrays):
    return [pltpu.with_memory_space_constraint(a, pltpu.VMEM) for a in arrays]


EMPTY_FEATURE = 256.0


def encode(feature, low, high, z_low):
    z = jnp.where(low_lanes((1, 128)), 1.0 * z_low, z_low + 1.0)
    feature = jnp.where(feature == 0.0, EMPTY_FEATURE, feature)
    return jnp.where((z >= low) & (z < high), feature, 0.0)


def column_bounds(low, high, x):
    ly = low.shape[1]
    code = (low[x : x + 1, :] * 16 + high[x : x + 1, :]).astype(F32)
    same = lax.broadcasted_iota(jnp.int32, (ly, ly), 0) == lax.broadcasted_iota(
        jnp.int32, (ly, ly), 1
    )
    spread = jnp.where(same, code, 0.0).astype(BF16)
    column = jnp.dot(spread, jnp.ones((ly, 128), BF16), preferred_element_type=F32)
    floor = jnp.floor(column * (1.0 / 16.0))
    return floor, column - 16.0 * floor


def strip_kernel(top_in, bottom_in, low, high, top, bottom):
    lx = low.shape[0]
    for source, target, base in ((top_in, top, 0), (bottom_in, bottom, lx - 2)):
        for x in range(2):
            floor, high_of = column_bounds(low, high, base + x)
            for m in range(4):
                lanes = slice(128 * m, 128 * m + 128)
                v = encode(source[x, :, lanes].astype(F32), floor, high_of, 2 * m)
                target[x, :, lanes] = v.astype(BF16)


def strip_call(features, low, high):
    lx, ly, width = features.shape
    end = lx // 2 - 1
    return pl.pallas_call(
        strip_kernel,
        out_shape=(held((2, ly, width), BF16), held((2, ly, width), BF16)),
        grid=(1,),
        in_specs=[
            pl.BlockSpec((2, ly, width), lambda i: (0, 0, 0)),
            pl.BlockSpec((2, ly, width), lambda i: (end, 0, 0)),
            VMEM,
            VMEM,
        ],
        out_specs=(VMEM, VMEM),
        compiler_params=pltpu.CompilerParams(vmem_limit_bytes=12 << 20),
        name="strips",
    )(features, features, low, high)


def side_kernel(above, below, first, last, to_left, to_right):
    lx = first.shape[0]
    ly = above.shape[1]
    for strip, base in ((above, 0), (below, lx + 2)):
        for x in range(2):
            v = strip[x].astype(F32)
            to_left[base + x] = v[0:2].astype(BF16)
            to_right[base + x] = v[ly - 2 : ly].astype(BF16)
    to_left[2 : lx + 2] = first[...]
    to_right[2 : lx + 2] = last[...]


def side_call(above, below, first, last):
    tall = (first.shape[0] + 4,) + first.shape[1:]
    return pl.pallas_call(
        side_kernel,
        out_shape=(held(tall, BF16), held(tall, BF16)),
        in_specs=[VMEM] * 4,
        out_specs=(VMEM, VMEM),
        compiler_params=pltpu.CompilerParams(vmem_limit_bytes=12 << 20),
        name="sides",
    )(*near(above, below, first, last))


def tile_kernel(
    features, low, high, weight_one, weight_two, slots, tiles, tiles_last, packed, first, last
):
    lx, ly = low.shape
    filled = jnp.where(high[...] > low[...], 1.0, 0.0)
    rows = [
        jnp.sum(filled[8 * i : 8 * i + 8], axis=0, keepdims=True) for i in range(lx // BRICK)
    ]
    rows = jnp.concatenate(rows + [jnp.zeros((8 - len(rows), ly), F32)], axis=0)
    among = lax.broadcasted_iota(jnp.int32, (ly, 128), 0) // BRICK
    among = among == lax.broadcasted_iota(jnp.int32, (ly, 128), 1)
    counts = jnp.dot(
        rows.astype(BF16), jnp.where(among, 1.0, 0.0).astype(BF16), preferred_element_type=F32
    )
    for i in range(3 * ACT_MAX):
        slots[i] = 0
    r = lax.broadcasted_iota(jnp.int32, (8, 128), 0)
    c = lax.broadcasted_iota(jnp.int32, (8, 128), 1)
    flags = [
        jnp.sum(jnp.where((r == i) & (c == j), counts, 0.0))
        for i in range(lx // BRICK)
        for j in range(ly // BRICK)
    ]
    seat = jnp.int32(0)
    for n, flag in enumerate(flags):
        i, j = n // (ly // BRICK), n % (ly // BRICK)
        has = (flag > 0.5) & (seat < ACT_MAX)

        @pl.when(has)
        def _(seat=seat, i=i, j=j):
            slots[seat] = i
            slots[ACT_MAX + seat] = j
            slots[2 * ACT_MAX + seat] = 1

        seat = seat + has.astype(jnp.int32)

    for x in range(lx):
        floor, high_of = column_bounds(low, high, x)
        for m in range(4):
            lanes = slice(128 * m, 128 * m + 128)
            v = encode(features[x, :, lanes].astype(F32), floor, high_of, 2 * m)
            packed[x, :, lanes] = v.astype(BF16)
            first[x, :, lanes] = v[0:2].astype(BF16)
            last[x, :, lanes] = v[ly - 2 : ly].astype(BF16)

    zero = jnp.zeros((64, 64), BF16)
    for conv, weight in enumerate((weight_one, weight_two, weight_two, weight_one)):
        for tap in range(9):
            taps = []
            for oz in range(3):
                if conv < 2:
                    taps.append(weight[3 * tap + oz])
                else:
                    taps.append(weight[26 - 3 * tap - oz].astype(F32).T.astype(BF16))
            taps = [zero] + taps + [zero]
            for d in range(4):
                tile = jnp.concatenate([taps[d + 1], taps[d]], axis=1)
                if conv < 3:
                    tiles[conv, tap, d] = tile
                else:
                    tiles_last[tap, d] = tile


def tile_call(features, low, high, weight_one, weight_two):
    lx, _, width = features.shape
    return pl.pallas_call(
        tile_kernel,
        out_shape=(
            shape((3 * ACT_MAX,), jnp.int32),
            held((3, 9, 4, 64, 128), BF16),
            held((9, 4, 64, 128), BF16),
            held(features.shape, BF16),
            held((lx, 2, width), BF16),
            held((lx, 2, width), BF16),
        ),
        in_specs=[VMEM] * 5,
        out_specs=(SMEM,) + (VMEM,) * 5,
        compiler_params=pltpu.CompilerParams(vmem_limit_bytes=16 << 20),
        name="tiles",
    )(features, low, high, weight_one, weight_two)


def build_bands(bands, tile_at):
    bands[...] = jnp.zeros(bands.shape, BF16)
    for ox in range(3):
        for oy in range(3):
            for r in range(6):
                for q in range(2):
                    d = r - 2 * q
                    if 0 <= d < 4:
                        row = 1152 * ox + ((r // 2) * 3 + oy) * 128 + (r % 2) * 64
                        bands[row : row + 64, 128 * q : 128 * q + 128] = tile_at(
                            ox * 3 + oy, d
                        )


def convolve(source, bands, acc, xs):
    rows = source.shape[0] * xs * 16
    for half in range(2):
        parts = [
            source[:, ox : ox + xs, :, 768 * half : 768 * half + 1152].reshape(rows, 1152)
            for ox in range(3)
        ]
        acc[0:rows, 256 * half : 256 * half + 256] = jnp.dot(
            jnp.concatenate(parts, axis=1), bands[...], preferred_element_type=F32
        )


def place(slots, s):
    x0 = pl.multiple_of(slots[s] * 8, 8)
    y0 = pl.multiple_of(slots[ACT_MAX + s] * 8, 8)
    return x0, y0, slots[2 * ACT_MAX + s]


def twice(row):
    return jnp.concatenate([row, row], axis=1)


def brick_kernel(
    slots, packed, above, below, left, right, cotangent, tiles, s_one, t_one, s_two, t_two,
    out, errors_out, grads_out, total,
    fx, ms, bands_a, bands_b, bands_c, c1, c2, c3, acc, slope, h, e2, er2, ets, et1, folded,
):
    lx, ly = out.shape[0], out.shape[1]
    low_row = low_lanes((1, 128))
    scale_one, shift_one = twice(s_one[...]), twice(t_one[...])
    scale_two, shift_two = twice(s_two[...]), twice(t_two[...])

    build_bands(bands_a, lambda t, d: tiles[0, t, d])

    def put(x, strip, start, stop):
        pieces = []
        for m in range(4):
            v = strip(m).astype(F32)
            ms[m, x, start:stop, :] = jnp.where(v == 0.0, 0.0, 1.0)
            pieces.append(jnp.where(v == EMPTY_FEATURE, 0.0, v))
        for p, v in enumerate(to_shifted(pieces)):
            fx[p, x, start:stop, :] = v

    def own_row(i, _):
        for k in range(2):
            x = 2 * i + k
            put(x + 2, lambda m: packed[x, :, 128 * m : 128 * m + 128], 8, 8 + ly)
            out[x] = jnp.zeros(out.shape[1:], BF16)
        return 0

    lax.fori_loop(0, lx // 2, own_row, 0)
    for x in range(2):
        put(x, lambda m: above[x, :, 128 * m : 128 * m + 128], 8, 8 + ly)
        put(lx + 2 + x, lambda m: below[x, :, 128 * m : 128 * m + 128], 8, 8 + ly)

    def side_row(i, _):
        for k in range(4):
            x = 4 * i + k
            for base in (0, 8 + ly):
                for m in range(4):
                    ms[m, x, base : base + 8, :] = jnp.zeros((8, 128), F32)
                for p in range(5):
                    fx[p, x, base : base + 8, :] = jnp.zeros((8, 128), F32)
            put(x, lambda m: left[x, :, 128 * m : 128 * m + 128], 6, 8)
            put(x, lambda m: right[x, :, 128 * m : 128 * m + 128], 8 + ly, 10 + ly)
        return 0

    lax.fori_loop(0, (lx + 4) // 4, side_row, 0)

    def gather_one(s, _):
        x0, y0, _ = place(slots, s)
        for p in range(5):
            view = fx.at[p, pl.ds(x0, 12), pl.ds(y0, 24), :]
            for oy in range(3):
                lane = (p * 3 + oy) * 128
                c1[s, :, :, lane : lane + 128] = view[:, 6 + oy : 22 + oy, :].astype(BF16)
        return 0

    lax.fori_loop(0, ACT_MAX, gather_one, 0)
    build_bands(bands_b, lambda t, d: tiles[1, t, d])
    convolve(c1, bands_a, acc, 10)

    def hidden_of(i, _):
        s = i // 2
        x0, y0, live = place(slots, s)
        keep_rows = lax.broadcasted_iota(jnp.int32, (16, 128), 0) < jnp.where(live > 0, 10, 0)
        for k in range(5):
            x = (i % 2) * 5 + k
            at = pl.multiple_of((s * 10 + x) * 16, 16)
            pieces = []
            for m in range(4):
                lanes = slice(128 * m, 128 * m + 128)
                mask = ms.at[m, x0 + x + 1, pl.ds(y0, 24), :][7:23, :]
                mask = jnp.where(keep_rows, mask, 0.0)
                pre = acc[pl.ds(at, 16), lanes] * scale_one + shift_one
                sig = 1.0 / (1.0 + jnp.exp(-pre))
                pieces.append(pre * sig * mask)
                slope[pl.ds(at, 16), lanes] = (
                    scale_one * mask * (sig * (1.0 + pre * (1.0 - sig)))
                )
            for p, v in enumerate(to_shifted(pieces)):
                h[s, p, x] = v
        return 0

    lax.fori_loop(0, 2 * ACT_MAX, hidden_of, 0)

    def gather_two(q, _):
        for p in range(5):
            for oy in range(3):
                lane = (p * 3 + oy) * 128
                one = h[2 * q, p, :, oy : oy + 8, :]
                two = h[2 * q + 1, p, :, oy : oy + 8, :]
                c2[q, :, :, lane : lane + 128] = jnp.concatenate([one, two], axis=1).astype(BF16)
        return 0

    lax.fori_loop(0, ACT_MAX // 2, gather_two, 0)
    build_bands(bands_c, lambda t, d: tiles[2, t, d])
    convolve(c2, bands_b, acc, 8)

    def finish_two(s, _):
        x0, y0, live = place(slots, s)
        odd = lax.rem(slots[ACT_MAX + s], 2) == 1
        y16 = pl.multiple_of(slots[ACT_MAX + s] // 2 * 16, 16)
        alive = jnp.where(live > 0, 1.0, 0.0)
        zero = jnp.zeros((8, 128), F32)
        for p in range(5):
            for x in (0, 1, 10, 11):
                e2[s, p, x] = jnp.zeros((24, 128), F32)
        for x in range(8):
            at = pl.multiple_of(((s // 2) * 8 + x) * 16 + (s % 2) * 8, 8)
            centre = to_aligned([fx[p, x0 + 2 + x, pl.ds(y0 + 8, 8), :] for p in range(5)])
            errors = []
            for m in range(4):
                lanes = slice(128 * m, 128 * m + 128)
                mask = ms[m, x0 + 2 + x, pl.ds(y0 + 8, 8), :] * alive
                pre = acc[pl.ds(at, 8), lanes] * scale_two + shift_two + centre[m]
                sig = 1.0 / (1.0 + jnp.exp(-pre))
                result = pre * sig * mask
                both = cotangent[x0 + x, pl.ds(y16, 16), lanes].astype(F32)
                target = jnp.where(odd, both[8:16], both[0:8])
                grad = target * mask * (sig * (1.0 + pre * (1.0 - sig)))
                error = grad * scale_two
                errors.append(error)
                er2[pl.ds(at, 8), lanes] = error
                grads_out[s, x, :, lanes] = grad
                result = jnp.where(
                    odd,
                    jnp.concatenate([zero, result], axis=0),
                    jnp.concatenate([result, zero], axis=0),
                )
                now = out[x0 + x, pl.ds(y16, 16), lanes].astype(F32)
                out[x0 + x, pl.ds(y16, 16), lanes] = (now + result).astype(BF16)
            for p, v in enumerate(to_shifted(errors)):
                e2[s, p, x + 2, 0:8, :] = zero
                e2[s, p, x + 2, 8:16, :] = v
                e2[s, p, x + 2, 16:24, :] = zero
        return 0

    lax.fori_loop(0, ACT_MAX, finish_two, 0)

    def gather_three(s, _):
        for p in range(5):
            for oy in range(3):
                lane = (p * 3 + oy) * 128
                c3[s, :, :, lane : lane + 128] = e2[s, p, :, 6 + oy : 22 + oy, :].astype(BF16)
        return 0

    lax.fori_loop(0, ACT_MAX, gather_three, 0)
    ets[0:128] = jnp.zeros((128, ets.shape[1]), BF16)
    ets[640:768] = jnp.zeros((128, ets.shape[1]), BF16)
    ets[128:640] = er2[...].astype(BF16).T
    convolve(c3, bands_c, acc, 10)

    def finish_three(i, _):
        for k in range(4):
            at = pl.multiple_of((i * 4 + k) * 16, 16)
            for m in range(4):
                lanes = slice(128 * m, 128 * m + 128)
                error = acc[pl.ds(at, 16), lanes] * slope[pl.ds(at, 16), lanes]
                errors_out[pl.ds(at, 16), lanes] = error.astype(BF16)
        return 0

    lax.fori_loop(0, ACT_MAX * 10 // 4, finish_three, 0)

    def weight_sums(source, errors_t, xs, which):
        rows = source.shape[0] * xs * 16
        sums = None
        for p in range(5):
            parts = [
                source[:, ox : ox + xs, :, 384 * p : 384 * p + 384].reshape(rows, 384)
                for ox in range(3)
            ]
            part = jnp.dot(
                errors_t[128 * p : 128 * p + 256, :],
                jnp.concatenate(parts, axis=1),
                preferred_element_type=F32,
            )
            sums = part if sums is None else sums + part
        for tap in range(9):
            block = sums[:, 128 * tap : 128 * tap + 128]
            turned = turn(block)
            for oz in range(3):
                one, two = 64 * (2 - oz), 64 * (3 - oz)
                n = tap * 3 + oz
                if which == 0:
                    folded[n] = block[one : one + 64] + turned[two : two + 64]
                else:
                    v = turned[one : one + 64] + block[two : two + 64]
                    total[n] = jnp.where(low_row, folded[n], v).astype(BF16)

    et1[0:128] = jnp.zeros((128, et1.shape[1]), BF16)
    et1[640:768] = jnp.zeros((128, et1.shape[1]), BF16)
    et1[128:640] = errors_out[...].T
    weight_sums(c1, et1, 10, 0)
    weight_sums(c2, ets, 8, 1)
    total[27] = jnp.zeros((64, 128), BF16)


def brick_call(slots, packed, above, below, left, right, cotangent, tiles, *vectors):
    lx, ly, width = cotangent.shape
    n = ACT_MAX
    wide = ly + 16
    return pl.pallas_call(
        brick_kernel,
        out_shape=(
            shape((lx, ly, width), BF16),
            held((n * 160, width), BF16),
            held((n, 8, 8, width), F32),
            held((28, 64, 128), BF16),
        ),
        in_specs=[SMEM] + [VMEM] * 11,
        out_specs=(VMEM,) * 4,
        scratch_shapes=[
            pltpu.VMEM((5, lx + 4, wide, 128), F32),
            pltpu.VMEM((4, lx + 4, wide, 128), F32),
            pltpu.VMEM((3456, 256), BF16),
            pltpu.VMEM((3456, 256), BF16),
            pltpu.VMEM((3456, 256), BF16),
            pltpu.VMEM((n, 12, 16, 1920), BF16),
            pltpu.VMEM((n // 2, 10, 16, 1920), BF16),
            pltpu.VMEM((n, 12, 16, 1920), BF16),
            pltpu.VMEM((n * 160, width), F32),
            pltpu.VMEM((n * 160, width), F32),
            pltpu.VMEM((n, 5, 10, 16, 128), F32),
            pltpu.VMEM((n, 5, 12, 24, 128), F32),
            pltpu.VMEM((n * 64, width), F32),
            pltpu.VMEM((768, n * 64), BF16),
            pltpu.VMEM((768, n * 160), BF16),
            pltpu.VMEM((27, 64, 128), F32),
        ],
        compiler_params=pltpu.CompilerParams(vmem_limit_bytes=40 << 20),
        name="bricks",
    )(
        slots,
        *near(packed, above, below, left, right),
        cotangent,
        *near(tiles),
        *vectors,
    )


def input_kernel(
    slots, errors, grads, packed, tiles, grad_own, grad_above, grad_below, grad_left, grad_right,
    e1, c4, bands, acc, grid,
):
    lx, ly = grad_own.shape[0], grad_own.shape[1]
    wide = grid.shape[2]
    build_bands(bands, lambda t, d: tiles[t, d])

    def clear_row(i, _):
        for k in range(2):
            for m in range(4):
                grid[m, 2 * i + k] = jnp.zeros((wide, 128), F32)
        return 0

    lax.fori_loop(0, (lx + 4) // 2, clear_row, 0)

    def spread(s, _):
        for p in range(5):
            for x in (0, 1, 12, 13):
                e1[p, x] = jnp.zeros((24, 128), F32)
        for x in range(10):
            at = pl.multiple_of((s * 10 + x) * 16, 16)
            rows = [
                errors[pl.ds(at, 16), 128 * m : 128 * m + 128].astype(F32) for m in range(4)
            ]
            for p, v in enumerate(to_shifted(rows)):
                e1[p, x + 2, 0:8, :] = jnp.zeros((8, 128), F32)
                e1[p, x + 2, 8:24, :] = v
        for p in range(5):
            for oy in range(3):
                lane = (p * 3 + oy) * 128
                c4[s, :, :, lane : lane + 128] = e1[p, :, 6 + oy : 22 + oy, :].astype(BF16)
        return 0

    lax.fori_loop(0, ACT_MAX, spread, 0)
    convolve(c4, bands, acc, 12)

    def finish(s, _):
        x0, y0, _ = place(slots, s)
        for x in range(12):
            at = pl.multiple_of((s * 12 + x) * 16, 16)
            for m in range(4):
                lanes = slice(128 * m, 128 * m + 128)
                view = grid.at[m, x0 + x, pl.ds(y0, 24), :]
                view[6:22, :] = view[6:22, :] + acc[pl.ds(at, 16), lanes]
        for x in range(8):
            for m in range(4):
                lanes = slice(128 * m, 128 * m + 128)
                view = grid.at[m, x0 + 2 + x, pl.ds(y0 + 8, 8), :]
                view[...] = view[...] + grads[s, x, :, lanes]
        return 0

    lax.fori_loop(0, ACT_MAX, finish, 0)

    def own_rows(i, _):
        for k in range(2):
            x = 2 * i + k
            for m in range(4):
                lanes = slice(128 * m, 128 * m + 128)
                v = grid[m, x + 2, 8 : 8 + ly, :]
                v = jnp.where(packed[x, :, lanes].astype(F32) == 0.0, 0.0, v)
                grad_own[x, :, lanes] = v.astype(BF16)
                grad_left[x, :, lanes] = grid[m, x + 2, 6:8, :].astype(BF16)
                grad_right[x, :, lanes] = grid[m, x + 2, 8 + ly : 10 + ly, :].astype(BF16)
        return 0

    lax.fori_loop(0, lx // 2, own_rows, 0)
    for target, base in ((grad_above, 0), (grad_below, lx + 2)):
        for x in range(2):
            for m in range(4):
                lanes = slice(128 * m, 128 * m + 128)
                target[x, 0:ly, lanes] = grid[m, base + x, 8 : 8 + ly, :].astype(BF16)
                corners = [
                    grid[m, base + x, 6:8, :],
                    grid[m, base + x, 8 + ly : 10 + ly, :],
                    jnp.zeros((4, 128), F32),
                ]
                target[x, ly : ly + 8, lanes] = jnp.concatenate(corners, axis=0).astype(BF16)


def input_call(slots, errors, grads, packed, tiles):
    lx, ly, width = packed.shape
    n = ACT_MAX
    return pl.pallas_call(
        input_kernel,
        out_shape=(
            shape((lx, ly, width), BF16),
            held((2, ly + 8, width), BF16),
            held((2, ly + 8, width), BF16),
            held((lx, 2, width), BF16),
            held((lx, 2, width), BF16),
        ),
        in_specs=[SMEM] + [VMEM] * 4,
        out_specs=(VMEM,) * 5,
        scratch_shapes=[
            pltpu.VMEM((5, 14, 24, 128), F32),
            pltpu.VMEM((n, 14, 16, 1920), BF16),
            pltpu.VMEM((3456, 256), BF16),
            pltpu.VMEM((n * 192, width), F32),
            pltpu.VMEM((4, lx + 4, ly + 16, 128), F32),
        ],
        compiler_params=pltpu.CompilerParams(vmem_limit_bytes=24 << 20),
        name="inputs",
    )(slots, *near(errors, grads, packed, tiles))


def ends_kernel(left, right, from_above, from_below, to_left, to_right):
    lx = left.shape[0]
    ly = from_above.shape[1] - 8
    to_left[...] = left[...]
    to_right[...] = right[...]
    for source, base in ((from_above, 0), (from_below, lx - 2)):
        for x in range(2):
            v = source[x, ly : ly + 8].astype(F32)
            for strip, target, at in ((left, to_left, 0), (right, to_right, 2)):
                target[base + x] = (strip[base + x].astype(F32) + v[at : at + 2]).astype(BF16)


def ends_call(left, right, from_above, from_below):
    return pl.pallas_call(
        ends_kernel,
        out_shape=(held(left.shape, BF16), held(left.shape, BF16)),
        in_specs=[VMEM] * 4,
        out_specs=(VMEM, VMEM),
        compiler_params=pltpu.CompilerParams(vmem_limit_bytes=12 << 20),
        name="ends",
    )(*near(left, right, from_above, from_below))


def join_kernel(
    grads, top, bottom, first, last, from_left, from_right, from_above, from_below, joined,
    rows_a, rows_b, cols_a, cols_b, sems,
):
    lx, ly, _ = joined.shape
    places = (
        (rows_a, lambda ref: ref.at[0:2]),
        (rows_b, lambda ref: ref.at[lx - 2 : lx]),
        (cols_a, lambda ref: ref.at[2 : lx - 2, 0:16, :]),
        (cols_b, lambda ref: ref.at[2 : lx - 2, ly - 16 : ly, :]),
    )
    copies = [
        pltpu.make_async_copy(at(grads), held, sems.at[n]) for n, (held, at) in enumerate(places)
    ]
    for copy in copies:
        copy.start()
    for copy in copies:
        copy.wait()
    width = rows_a.shape[2]

    def first_add(strip, rows):
        return jnp.concatenate([strip.astype(F32), jnp.zeros((rows - 2, width), F32)], axis=0)

    def last_add(strip, rows):
        return jnp.concatenate([jnp.zeros((rows - 2, width), F32), strip.astype(F32)], axis=0)

    for held, code, extra, base in (
        (rows_a, top, from_above, 0),
        (rows_b, bottom, from_below, lx - 2),
    ):
        for x in range(2):
            v = held[x].astype(F32) + extra[x, 0:ly].astype(F32)
            one = v[0:8] + first_add(from_left[base + x], 8)
            two = v[ly - 8 : ly] + last_add(from_right[base + x], 8)
            v = jnp.concatenate([one, v[8 : ly - 8], two], axis=0)
            held[x] = jnp.where(code[x].astype(F32) == 0.0, 0.0, v).astype(BF16)
    for x in range(2, lx - 2):
        kept = jnp.where(first[x].astype(F32) == 0.0, 0.0, from_left[x].astype(F32))
        kept = first_add(kept, 16)
        cols_a[x - 2] = (cols_a[x - 2].astype(F32) + kept).astype(BF16)
        kept = jnp.where(last[x].astype(F32) == 0.0, 0.0, from_right[x].astype(F32))
        kept = last_add(kept, 16)
        cols_b[x - 2] = (cols_b[x - 2].astype(F32) + kept).astype(BF16)
    copies = [
        pltpu.make_async_copy(held, at(joined), sems.at[n]) for n, (held, at) in enumerate(places)
    ]
    for copy in copies:
        copy.start()
    for copy in copies:
        copy.wait()


def join_call(grads, *strips):
    lx, ly, width = grads.shape
    anywhere = pl.BlockSpec(memory_space=pl.ANY)
    return pl.pallas_call(
        join_kernel,
        out_shape=shape(grads.shape, BF16),
        in_specs=[anywhere] + [VMEM] * 8,
        out_specs=anywhere,
        scratch_shapes=[
            pltpu.VMEM((2, ly, width), BF16),
            pltpu.VMEM((2, ly, width), BF16),
            pltpu.VMEM((lx - 4, 16, width), BF16),
            pltpu.VMEM((lx - 4, 16, width), BF16),
            pltpu.SemaphoreType.DMA((4,)),
        ],
        input_output_aliases={0: 0},
        compiler_params=pltpu.CompilerParams(vmem_limit_bytes=16 << 20),
        name="join",
    )(grads, *near(*strips))


def sums_kernel(sums, grad_one, grad_two, *, scale):
    base = pl.program_id(0) * 9
    for n in range(9):
        at = pl.multiple_of(64 * (base + n), 64)
        v = sums[pl.ds(at, 64)].astype(F32).T * scale
        grad_one[n] = v[0:64]
        grad_two[n] = v[64:128]


def sums_call(sums, scale):
    taps = pl.BlockSpec((9, 64, 64), lambda i: (i, 0, 0))
    return pl.pallas_call(
        functools.partial(sums_kernel, scale=scale),
        out_shape=(shape((27, 64, 64), F32), shape((27, 64, 64), F32)),
        grid=(3,),
        in_specs=[VMEM],
        out_specs=(taps, taps),
        compiler_params=pltpu.CompilerParams(vmem_limit_bytes=16 << 20),
        name="sums",
    )(*near(sums))


def shards(
    features, cotangent, low, high, weight_one, weight_two, scale_one, shift_one, scale_two,
    shift_two,
):
    nx, ny = lax.axis_size("gx"), lax.axis_size("gy")
    top, bottom = strip_call(features, low, high)
    above = shifted_in(bottom, "gx", 1)
    below = shifted_in(top, "gx", -1)
    slots, tiles, tiles_last, packed, first, last = tile_call(
        features, low, high, weight_one, weight_two
    )
    to_left, to_right = side_call(above, below, first, last)
    left = shifted_in(to_right, "gy", 1)
    right = shifted_in(to_left, "gy", -1)
    vectors = [v.reshape(1, -1) for v in (scale_one, shift_one, scale_two, shift_two)]
    out, errors, grads, sums = brick_call(
        slots, packed, above, below, left, right, cotangent, tiles, *vectors
    )

    devices = nx * ny
    parts = sums.reshape(devices, -1, 128)
    slots, errors, parts = lax.optimization_barrier((slots, errors, parts))
    got = lax.all_to_all(parts, ("gx", "gy"), 0, 0, tiled=True)
    own, grad_above, grad_below, grad_left, grad_right = input_call(
        slots, errors, grads, packed, tiles_last
    )
    from_below = shifted_in(grad_above, "gx", -1)
    from_above = shifted_in(grad_below, "gx", 1)
    got, own = lax.optimization_barrier((got, own))
    mine = jnp.sum(got.astype(F32), axis=0, keepdims=True).astype(BF16)
    back = lax.all_to_all(
        jnp.broadcast_to(mine, parts.shape), ("gx", "gy"), 0, 0, tiled=True
    )
    to_left, to_right = ends_call(grad_left, grad_right, from_above, from_below)
    from_right = shifted_in(to_left, "gy", -1)
    from_left = shifted_in(to_right, "gy", 1)
    grad_features = join_call(
        own, top, bottom, first, last, from_left, from_right, from_above, from_below
    )
    back, grad_features = lax.optimization_barrier((back, grad_features))
    grad_one, grad_two = sums_call(back.reshape(-1, 128), 1.0 / (devices * SHARE))
    return (out, grad_features, grad_one, grad_two)


def solution(mesh):
    whole = P("gx", "gy", None)
    columns = P("gx", "gy")

    return jax.shard_map(
        shards,
        mesh=mesh,
        in_specs=(whole, whole, columns, columns) + (P(),) * 6,
        out_specs=(whole, whole, P(), P()),
        check_vma=False,
    )
```

```python
import functools

import jax
import jax.numpy as jnp
from jax import lax
from jax.experimental import pallas as pl
from jax.experimental.pallas import tpu as pltpu
from jax.sharding import PartitionSpec as P


BRICK = 8
ACT_MAX = 4
SHARE = 2
F32 = jnp.float32
BF16 = jnp.bfloat16


def shifted_in(array, axis, by):
    devices = lax.axis_size(axis)
    pairs = [(i, i + by) for i in range(devices) if 0 <= i + by < devices]
    return lax.ppermute(array, axis, pairs)


def low_lanes(shape):
    return lax.broadcasted_iota(jnp.int32, shape, len(shape) - 1) < 64


def turn(value):
    return pltpu.roll(value, 64, value.ndim - 1)


def to_shifted(pairs):
    turned = [turn(v) for v in pairs]
    low = low_lanes(pairs[0].shape)
    zero = jnp.zeros_like(pairs[0])
    before = [zero] + turned
    after = turned + [zero]
    return [jnp.where(low, b, a) for b, a in zip(before, after)]


def to_aligned(shifted):
    turned = [turn(v) for v in shifted]
    low = low_lanes(shifted[0].shape)
    return [jnp.where(low, turned[m], turned[m + 1]) for m in range(len(shifted) - 1)]


VMEM = pl.BlockSpec(memory_space=pltpu.VMEM)
SMEM = pl.BlockSpec(memory_space=pltpu.SMEM)
shape = jax.ShapeDtypeStruct
held = pltpu.VMEM


def near(*arrays):
    return [pltpu.with_memory_space_constraint(a, pltpu.VMEM) for a in arrays]


def far(*arrays):
    return [pltpu.with_memory_space_constraint(a, pltpu.HBM) for a in arrays]


EMPTY_FEATURE = 256.0


def encode(feature, low, high, z_low):
    z = jnp.where(low_lanes((1, 128)), 1.0 * z_low, z_low + 1.0)
    feature = jnp.where(feature == 0.0, EMPTY_FEATURE, feature)
    return jnp.where((z >= low) & (z < high), feature, 0.0)


def column_bounds(low, high, x):
    ly = low.shape[1]
    code = (low[x : x + 1, :] * 16 + high[x : x + 1, :]).astype(F32)
    same = lax.broadcasted_iota(jnp.int32, (ly, ly), 0) == lax.broadcasted_iota(
        jnp.int32, (ly, ly), 1
    )
    spread = jnp.where(same, code, 0.0).astype(BF16)
    column = jnp.dot(spread, jnp.ones((ly, 128), BF16), preferred_element_type=F32)
    floor = jnp.floor(column * (1.0 / 16.0))
    return floor, column - 16.0 * floor


def strip_kernel(top_in, bottom_in, low, high, top, bottom):
    lx = low.shape[0]
    for source, target, base in ((top_in, top, 0), (bottom_in, bottom, lx - 2)):
        for x in range(2):
            floor, high_of = column_bounds(low, high, base + x)
            for m in range(4):
                lanes = slice(128 * m, 128 * m + 128)
                v = encode(source[x, :, lanes].astype(F32), floor, high_of, 2 * m)
                target[x, :, lanes] = v.astype(BF16)


def strip_call(features, low, high):
    lx, ly, width = features.shape
    end = lx // 2 - 1
    return pl.pallas_call(
        strip_kernel,
        out_shape=(held((2, ly, width), BF16), held((2, ly, width), BF16)),
        grid=(1,),
        in_specs=[
            pl.BlockSpec((2, ly, width), lambda i: (0, 0, 0)),
            pl.BlockSpec((2, ly, width), lambda i: (end, 0, 0)),
            VMEM,
            VMEM,
        ],
        out_specs=(VMEM, VMEM),
        compiler_params=pltpu.CompilerParams(vmem_limit_bytes=4 << 20),
        name="strips",
    )(*far(features, features, low, high))


def side_kernel(above, below, first, last, to_left, to_right):
    lx = first.shape[0]
    ly = above.shape[1]
    for strip, base in ((above, 0), (below, lx + 2)):
        for x in range(2):
            v = strip[x].astype(F32)
            to_left[base + x] = v[0:2].astype(BF16)
            to_right[base + x] = v[ly - 2 : ly].astype(BF16)
    to_left[2 : lx + 2] = first[...]
    to_right[2 : lx + 2] = last[...]


def side_call(above, below, first, last):
    tall = (first.shape[0] + 4,) + first.shape[1:]
    return pl.pallas_call(
        side_kernel,
        out_shape=(held(tall, BF16), held(tall, BF16)),
        in_specs=[VMEM] * 4,
        out_specs=(VMEM, VMEM),
        compiler_params=pltpu.CompilerParams(vmem_limit_bytes=4 << 20),
        name="sides",
    )(*near(above, below, first, last))


def tile_kernel(
    features, low, high, weight_one, weight_two, slots, tiles, tiles_last, packed, first, last
):
    lx, ly = low.shape
    filled = jnp.where(high[...] > low[...], 1.0, 0.0)
    rows = [
        jnp.sum(filled[8 * i : 8 * i + 8], axis=0, keepdims=True) for i in range(lx // BRICK)
    ]
    rows = jnp.concatenate(rows + [jnp.zeros((8 - len(rows), ly), F32)], axis=0)
    among = lax.broadcasted_iota(jnp.int32, (ly, 128), 0) // BRICK
    among = among == lax.broadcasted_iota(jnp.int32, (ly, 128), 1)
    counts = jnp.dot(
        rows.astype(BF16), jnp.where(among, 1.0, 0.0).astype(BF16), preferred_element_type=F32
    )
    for i in range(3 * ACT_MAX):
        slots[i] = 0
    r = lax.broadcasted_iota(jnp.int32, (8, 128), 0)
    c = lax.broadcasted_iota(jnp.int32, (8, 128), 1)
    flags = [
        jnp.sum(jnp.where((r == i) & (c == j), counts, 0.0))
        for i in range(lx // BRICK)
        for j in range(ly // BRICK)
    ]
    seat = jnp.int32(0)
    for n, flag in enumerate(flags):
        i, j = n // (ly // BRICK), n % (ly // BRICK)
        has = (flag > 0.5) & (seat < ACT_MAX)

        @pl.when(has)
        def _(seat=seat, i=i, j=j):
            slots[seat] = i
            slots[ACT_MAX + seat] = j
            slots[2 * ACT_MAX + seat] = 1

        seat = seat + has.astype(jnp.int32)

    for x in range(lx):
        floor, high_of = column_bounds(low, high, x)
        for m in range(4):
            lanes = slice(128 * m, 128 * m + 128)
            v = encode(features[x, :, lanes].astype(F32), floor, high_of, 2 * m)
            packed[x, :, lanes] = v.astype(BF16)
            first[x, :, lanes] = v[0:2].astype(BF16)
            last[x, :, lanes] = v[ly - 2 : ly].astype(BF16)

    zero = jnp.zeros((64, 64), BF16)
    for conv, weight in enumerate((weight_one, weight_two, weight_two, weight_one)):
        for tap in range(9):
            taps = []
            for oz in range(3):
                if conv < 2:
                    taps.append(weight[3 * tap + oz])
                else:
                    taps.append(weight[26 - 3 * tap - oz].astype(F32).T.astype(BF16))
            taps = [zero] + taps + [zero]
            for d in range(4):
                tile = jnp.concatenate([taps[d + 1], taps[d]], axis=1)
                if conv < 3:
                    tiles[conv, tap, d] = tile
                else:
                    tiles_last[tap, d] = tile


def tile_call(features, low, high, weight_one, weight_two):
    lx, _, width = features.shape
    return pl.pallas_call(
        tile_kernel,
        out_shape=(
            shape((3 * ACT_MAX,), jnp.int32),
            held((3, 9, 4, 64, 128), BF16),
            held((9, 4, 64, 128), BF16),
            held(features.shape, BF16),
            held((lx, 2, width), BF16),
            held((lx, 2, width), BF16),
        ),
        in_specs=[VMEM] * 5,
        out_specs=(SMEM,) + (VMEM,) * 5,
        compiler_params=pltpu.CompilerParams(vmem_limit_bytes=8 << 20),
        name="tiles",
    )(features, low, high, weight_one, weight_two)


def build_bands(bands, tile_at):
    bands[...] = jnp.zeros(bands.shape, BF16)
    for ox in range(3):
        for oy in range(3):
            for r in range(6):
                for q in range(2):
                    d = r - 2 * q
                    if 0 <= d < 4:
                        row = 1152 * ox + ((r // 2) * 3 + oy) * 128 + (r % 2) * 64
                        bands[row : row + 64, 128 * q : 128 * q + 128] = tile_at(
                            ox * 3 + oy, d
                        )


def convolve(source, bands, acc, xs):
    rows = source.shape[0] * xs * 16
    for half in range(2):
        parts = [
            source[:, ox : ox + xs, :, 768 * half : 768 * half + 1152].reshape(rows, 1152)
            for ox in range(3)
        ]
        acc[0:rows, 256 * half : 256 * half + 256] = jnp.dot(
            jnp.concatenate(parts, axis=1), bands[...], preferred_element_type=F32
        )


def place(slots, s):
    x0 = pl.multiple_of(slots[s] * 8, 8)
    y0 = pl.multiple_of(slots[ACT_MAX + s] * 8, 8)
    return x0, y0, slots[2 * ACT_MAX + s]


def twice(row):
    return jnp.concatenate([row, row], axis=1)


def brick_kernel(
    slots, packed, above, below, left, right, cotangent, tiles, s_one, t_one, s_two, t_two,
    out, errors_out, grads_out, total,
    fx, ms, bands_a, bands_b, bands_c, c1, c2, c3, acc, slope, h, e2, er2, ets, et1, folded,
):
    lx, ly = out.shape[0], out.shape[1]
    low_row = low_lanes((1, 128))
    scale_one, shift_one = twice(s_one[...]), twice(t_one[...])
    scale_two, shift_two = twice(s_two[...]), twice(t_two[...])

    build_bands(bands_a, lambda t, d: tiles[0, t, d])

    def put(x, strip, start, stop):
        pieces = []
        for m in range(4):
            v = strip(m).astype(F32)
            ms[m, x, start:stop, :] = jnp.where(v == 0.0, 0.0, 1.0)
            pieces.append(jnp.where(v == EMPTY_FEATURE, 0.0, v))
        for p, v in enumerate(to_shifted(pieces)):
            fx[p, x, start:stop, :] = v

    def own_row(i, _):
        for k in range(2):
            x = 2 * i + k
            put(x + 2, lambda m: packed[x, :, 128 * m : 128 * m + 128], 8, 8 + ly)
            out[x] = jnp.zeros(out.shape[1:], BF16)
        return 0

    lax.fori_loop(0, lx // 2, own_row, 0)
    for x in range(2):
        put(x, lambda m: above[x, :, 128 * m : 128 * m + 128], 8, 8 + ly)
        put(lx + 2 + x, lambda m: below[x, :, 128 * m : 128 * m + 128], 8, 8 + ly)

    def side_row(i, _):
        for k in range(4):
            x = 4 * i + k
            for base in (0, 8 + ly):
                for m in range(4):
                    ms[m, x, base : base + 8, :] = jnp.zeros((8, 128), F32)
                for p in range(5):
                    fx[p, x, base : base + 8, :] = jnp.zeros((8, 128), F32)
            put(x, lambda m: left[x, :, 128 * m : 128 * m + 128], 6, 8)
            put(x, lambda m: right[x, :, 128 * m : 128 * m + 128], 8 + ly, 10 + ly)
        return 0

    lax.fori_loop(0, (lx + 4) // 4, side_row, 0)

    def gather_one(s, _):
        x0, y0, _ = place(slots, s)
        for p in range(5):
            view = fx.at[p, pl.ds(x0, 12), pl.ds(y0, 24), :]
            for oy in range(3):
                lane = (p * 3 + oy) * 128
                c1[s, :, :, lane : lane + 128] = view[:, 6 + oy : 22 + oy, :].astype(BF16)
        return 0

    lax.fori_loop(0, ACT_MAX, gather_one, 0)
    build_bands(bands_b, lambda t, d: tiles[1, t, d])
    convolve(c1, bands_a, acc, 10)

    def hidden_of(i, _):
        s = i // 2
        x0, y0, live = place(slots, s)
        keep_rows = lax.broadcasted_iota(jnp.int32, (16, 128), 0) < jnp.where(live > 0, 10, 0)
        for k in range(5):
            x = (i % 2) * 5 + k
            at = pl.multiple_of((s * 10 + x) * 16, 16)
            pieces = []
            for m in range(4):
                lanes = slice(128 * m, 128 * m + 128)
                mask = ms.at[m, x0 + x + 1, pl.ds(y0, 24), :][7:23, :]
                mask = jnp.where(keep_rows, mask, 0.0)
                pre = acc[pl.ds(at, 16), lanes] * scale_one + shift_one
                sig = 1.0 / (1.0 + jnp.exp(-pre))
                pieces.append(pre * sig * mask)
                slope[pl.ds(at, 16), lanes] = (
                    scale_one * mask * (sig * (1.0 + pre * (1.0 - sig)))
                )
            for p, v in enumerate(to_shifted(pieces)):
                h[s, p, x] = v
        return 0

    lax.fori_loop(0, 2 * ACT_MAX, hidden_of, 0)

    def gather_two(q, _):
        for p in range(5):
            for oy in range(3):
                lane = (p * 3 + oy) * 128
                one = h[2 * q, p, :, oy : oy + 8, :]
                two = h[2 * q + 1, p, :, oy : oy + 8, :]
                c2[q, :, :, lane : lane + 128] = jnp.concatenate([one, two], axis=1).astype(BF16)
        return 0

    lax.fori_loop(0, ACT_MAX // 2, gather_two, 0)
    build_bands(bands_c, lambda t, d: tiles[2, t, d])
    convolve(c2, bands_b, acc, 8)

    def finish_two(s, _):
        x0, y0, live = place(slots, s)
        odd = lax.rem(slots[ACT_MAX + s], 2) == 1
        y16 = pl.multiple_of(slots[ACT_MAX + s] // 2 * 16, 16)
        alive = jnp.where(live > 0, 1.0, 0.0)
        zero = jnp.zeros((8, 128), F32)
        for p in range(5):
            for x in (0, 1, 10, 11):
                e2[s, p, x] = jnp.zeros((24, 128), F32)
        for x in range(8):
            at = pl.multiple_of(((s // 2) * 8 + x) * 16 + (s % 2) * 8, 8)
            centre = to_aligned([fx[p, x0 + 2 + x, pl.ds(y0 + 8, 8), :] for p in range(5)])
            errors = []
            for m in range(4):
                lanes = slice(128 * m, 128 * m + 128)
                mask = ms[m, x0 + 2 + x, pl.ds(y0 + 8, 8), :] * alive
                pre = acc[pl.ds(at, 8), lanes] * scale_two + shift_two + centre[m]
                sig = 1.0 / (1.0 + jnp.exp(-pre))
                result = pre * sig * mask
                both = cotangent[x0 + x, pl.ds(y16, 16), lanes].astype(F32)
                target = jnp.where(odd, both[8:16], both[0:8])
                grad = target * mask * (sig * (1.0 + pre * (1.0 - sig)))
                error = grad * scale_two
                errors.append(error)
                er2[pl.ds(at, 8), lanes] = error
                grads_out[s, x, :, lanes] = grad
                result = jnp.where(
                    odd,
                    jnp.concatenate([zero, result], axis=0),
                    jnp.concatenate([result, zero], axis=0),
                )
                now = out[x0 + x, pl.ds(y16, 16), lanes].astype(F32)
                out[x0 + x, pl.ds(y16, 16), lanes] = (now + result).astype(BF16)
            for p, v in enumerate(to_shifted(errors)):
                e2[s, p, x + 2, 0:8, :] = zero
                e2[s, p, x + 2, 8:16, :] = v
                e2[s, p, x + 2, 16:24, :] = zero
        return 0

    lax.fori_loop(0, ACT_MAX, finish_two, 0)

    def gather_three(s, _):
        for p in range(5):
            for oy in range(3):
                lane = (p * 3 + oy) * 128
                c3[s, :, :, lane : lane + 128] = e2[s, p, :, 6 + oy : 22 + oy, :].astype(BF16)
        return 0

    lax.fori_loop(0, ACT_MAX, gather_three, 0)
    ets[0:128] = jnp.zeros((128, ets.shape[1]), BF16)
    ets[640:768] = jnp.zeros((128, ets.shape[1]), BF16)
    ets[128:640] = er2[...].astype(BF16).T
    convolve(c3, bands_c, acc, 10)

    def finish_three(i, _):
        for k in range(4):
            at = pl.multiple_of((i * 4 + k) * 16, 16)
            for m in range(4):
                lanes = slice(128 * m, 128 * m + 128)
                error = acc[pl.ds(at, 16), lanes] * slope[pl.ds(at, 16), lanes]
                errors_out[pl.ds(at, 16), lanes] = error.astype(BF16)
        return 0

    lax.fori_loop(0, ACT_MAX * 10 // 4, finish_three, 0)

    def weight_sums(source, errors_t, xs, which):
        rows = source.shape[0] * xs * 16
        left_side = jnp.concatenate(
            [errors_t[128 * p : 128 * p + 256, :] for p in range(5)], axis=1
        )
        right_side = [
            jnp.concatenate(
                [
                    source[:, ox : ox + xs, :, 384 * p : 384 * p + 384].reshape(rows, 384)
                    for ox in range(3)
                ],
                axis=1,
            )
            for p in range(5)
        ]
        sums = jnp.dot(
            left_side, jnp.concatenate(right_side, axis=0), preferred_element_type=F32
        )
        for tap in range(9):
            block = sums[:, 128 * tap : 128 * tap + 128]
            turned = turn(block)
            for oz in range(3):
                one, two = 64 * (2 - oz), 64 * (3 - oz)
                n = tap * 3 + oz
                if which == 0:
                    folded[n] = block[one : one + 64] + turned[two : two + 64]
                else:
                    v = turned[one : one + 64] + block[two : two + 64]
                    total[n] = jnp.where(low_row, folded[n], v).astype(BF16)

    et1[0:128] = jnp.zeros((128, et1.shape[1]), BF16)
    et1[640:768] = jnp.zeros((128, et1.shape[1]), BF16)
    et1[128:640] = errors_out[...].T
    weight_sums(c1, et1, 10, 0)
    weight_sums(c2, ets, 8, 1)
    total[27] = jnp.zeros((64, 128), BF16)


def brick_call(slots, packed, above, below, left, right, cotangent, tiles, *vectors):
    lx, ly, width = cotangent.shape
    n = ACT_MAX
    wide = ly + 16
    return pl.pallas_call(
        brick_kernel,
        out_shape=(
            shape((lx, ly, width), BF16),
            held((n * 160, width), BF16),
            held((n, 8, 8, width), F32),
            pltpu.HBM((28, 64, 128), BF16),
        ),
        in_specs=[SMEM] + [VMEM] * 11,
        out_specs=(VMEM,) * 4,
        scratch_shapes=[
            pltpu.VMEM((5, lx + 4, wide, 128), F32),
            pltpu.VMEM((4, lx + 4, wide, 128), F32),
            pltpu.VMEM((3456, 256), BF16),
            pltpu.VMEM((3456, 256), BF16),
            pltpu.VMEM((3456, 256), BF16),
            pltpu.VMEM((n, 12, 16, 1920), BF16),
            pltpu.VMEM((n // 2, 10, 16, 1920), BF16),
            pltpu.VMEM((n, 12, 16, 1920), BF16),
            pltpu.VMEM((n * 160, width), F32),
            pltpu.VMEM((n * 160, width), F32),
            pltpu.VMEM((n, 5, 10, 16, 128), F32),
            pltpu.VMEM((n, 5, 12, 24, 128), F32),
            pltpu.VMEM((n * 64, width), F32),
            pltpu.VMEM((768, n * 64), BF16),
            pltpu.VMEM((768, n * 160), BF16),
            pltpu.VMEM((27, 64, 128), F32),
        ],
        compiler_params=pltpu.CompilerParams(vmem_limit_bytes=33 << 20),
        name="bricks",
    )(
        slots,
        *near(packed, above, below, left, right, cotangent, tiles),
        *vectors,
    )


def input_kernel(
    slots, errors, grads, packed, tiles, grad_own, grad_above, grad_below, grad_left, grad_right,
    e1, c4, bands, acc, grid,
):
    lx, ly = grad_own.shape[0], grad_own.shape[1]
    wide = grid.shape[2]
    build_bands(bands, lambda t, d: tiles[t, d])

    def clear_row(i, _):
        for k in range(2):
            for m in range(4):
                grid[m, 2 * i + k] = jnp.zeros((wide, 128), F32)
        return 0

    lax.fori_loop(0, (lx + 4) // 2, clear_row, 0)

    def spread(s, _):
        for p in range(5):
            for x in (0, 1, 12, 13):
                e1[p, x] = jnp.zeros((24, 128), F32)
        for x in range(10):
            at = pl.multiple_of((s * 10 + x) * 16, 16)
            rows = [
                errors[pl.ds(at, 16), 128 * m : 128 * m + 128].astype(F32) for m in range(4)
            ]
            for p, v in enumerate(to_shifted(rows)):
                e1[p, x + 2, 0:8, :] = jnp.zeros((8, 128), F32)
                e1[p, x + 2, 8:24, :] = v
        for p in range(5):
            for oy in range(3):
                lane = (p * 3 + oy) * 128
                c4[s, :, :, lane : lane + 128] = e1[p, :, 6 + oy : 22 + oy, :].astype(BF16)
        return 0

    lax.fori_loop(0, ACT_MAX, spread, 0)
    convolve(c4, bands, acc, 12)

    def finish(s, _):
        x0, y0, _ = place(slots, s)
        for x in range(12):
            at = pl.multiple_of((s * 12 + x) * 16, 16)
            for m in range(4):
                lanes = slice(128 * m, 128 * m + 128)
                view = grid.at[m, x0 + x, pl.ds(y0, 24), :]
                view[6:22, :] = view[6:22, :] + acc[pl.ds(at, 16), lanes]
        for x in range(8):
            for m in range(4):
                lanes = slice(128 * m, 128 * m + 128)
                view = grid.at[m, x0 + 2 + x, pl.ds(y0 + 8, 8), :]
                view[...] = view[...] + grads[s, x, :, lanes]
        return 0

    lax.fori_loop(0, ACT_MAX, finish, 0)

    def own_rows(i, _):
        for k in range(2):
            x = 2 * i + k
            for m in range(4):
                lanes = slice(128 * m, 128 * m + 128)
                v = grid[m, x + 2, 8 : 8 + ly, :]
                v = jnp.where(packed[x, :, lanes].astype(F32) == 0.0, 0.0, v)
                grad_own[x, :, lanes] = v.astype(BF16)
                grad_left[x, :, lanes] = grid[m, x + 2, 6:8, :].astype(BF16)
                grad_right[x, :, lanes] = grid[m, x + 2, 8 + ly : 10 + ly, :].astype(BF16)
        return 0

    lax.fori_loop(0, lx // 2, own_rows, 0)
    for target, base in ((grad_above, 0), (grad_below, lx + 2)):
        for x in range(2):
            for m in range(4):
                lanes = slice(128 * m, 128 * m + 128)
                target[x, 0:ly, lanes] = grid[m, base + x, 8 : 8 + ly, :].astype(BF16)
                corners = [
                    grid[m, base + x, 6:8, :],
                    grid[m, base + x, 8 + ly : 10 + ly, :],
                    jnp.zeros((4, 128), F32),
                ]
                target[x, ly : ly + 8, lanes] = jnp.concatenate(corners, axis=0).astype(BF16)


def input_call(slots, errors, grads, packed, tiles):
    lx, ly, width = packed.shape
    n = ACT_MAX
    return pl.pallas_call(
        input_kernel,
        out_shape=(
            shape((lx, ly, width), BF16),
            held((2, ly + 8, width), BF16),
            held((2, ly + 8, width), BF16),
            held((lx, 2, width), BF16),
            held((lx, 2, width), BF16),
        ),
        in_specs=[SMEM] + [VMEM] * 4,
        out_specs=(VMEM,) * 5,
        scratch_shapes=[
            pltpu.VMEM((5, 14, 24, 128), F32),
            pltpu.VMEM((n, 14, 16, 1920), BF16),
            pltpu.VMEM((3456, 256), BF16),
            pltpu.VMEM((n * 192, width), F32),
            pltpu.VMEM((4, lx + 4, ly + 16, 128), F32),
        ],
        compiler_params=pltpu.CompilerParams(vmem_limit_bytes=15 << 20),
        name="inputs",
    )(slots, *near(errors, grads, packed, tiles))


def ends_kernel(left, right, from_above, from_below, to_left, to_right):
    lx = left.shape[0]
    ly = from_above.shape[1] - 8
    to_left[...] = left[...]
    to_right[...] = right[...]
    for source, base in ((from_above, 0), (from_below, lx - 2)):
        for x in range(2):
            v = source[x, ly : ly + 8].astype(F32)
            for strip, target, at in ((left, to_left, 0), (right, to_right, 2)):
                target[base + x] = (strip[base + x].astype(F32) + v[at : at + 2]).astype(BF16)


def ends_call(left, right, from_above, from_below):
    return pl.pallas_call(
        ends_kernel,
        out_shape=(held(left.shape, BF16), held(left.shape, BF16)),
        in_specs=[VMEM] * 4,
        out_specs=(VMEM, VMEM),
        compiler_params=pltpu.CompilerParams(vmem_limit_bytes=4 << 20),
        name="ends",
    )(*near(left, right, from_above, from_below))


def join_kernel(
    grads, top, bottom, first, last, from_left, from_right, from_above, from_below, joined,
    rows_a, rows_b, cols_a, cols_b, sems,
):
    lx, ly, _ = joined.shape
    places = (
        (rows_a, lambda ref: ref.at[0:2]),
        (rows_b, lambda ref: ref.at[lx - 2 : lx]),
        (cols_a, lambda ref: ref.at[2 : lx - 2, 0:16, :]),
        (cols_b, lambda ref: ref.at[2 : lx - 2, ly - 16 : ly, :]),
    )
    copies = [
        pltpu.make_async_copy(at(grads), held, sems.at[n]) for n, (held, at) in enumerate(places)
    ]
    for copy in copies:
        copy.start()
    for copy in copies:
        copy.wait()
    width = rows_a.shape[2]

    def first_add(strip, rows):
        return jnp.concatenate([strip.astype(F32), jnp.zeros((rows - 2, width), F32)], axis=0)

    def last_add(strip, rows):
        return jnp.concatenate([jnp.zeros((rows - 2, width), F32), strip.astype(F32)], axis=0)

    for held, code, extra, base in (
        (rows_a, top, from_above, 0),
        (rows_b, bottom, from_below, lx - 2),
    ):
        for x in range(2):
            v = held[x].astype(F32) + extra[x, 0:ly].astype(F32)
            one = v[0:8] + first_add(from_left[base + x], 8)
            two = v[ly - 8 : ly] + last_add(from_right[base + x], 8)
            v = jnp.concatenate([one, v[8 : ly - 8], two], axis=0)
            held[x] = jnp.where(code[x].astype(F32) == 0.0, 0.0, v).astype(BF16)
    for x in range(2, lx - 2):
        kept = jnp.where(first[x].astype(F32) == 0.0, 0.0, from_left[x].astype(F32))
        kept = first_add(kept, 16)
        cols_a[x - 2] = (cols_a[x - 2].astype(F32) + kept).astype(BF16)
        kept = jnp.where(last[x].astype(F32) == 0.0, 0.0, from_right[x].astype(F32))
        kept = last_add(kept, 16)
        cols_b[x - 2] = (cols_b[x - 2].astype(F32) + kept).astype(BF16)
    copies = [
        pltpu.make_async_copy(held, at(joined), sems.at[n]) for n, (held, at) in enumerate(places)
    ]
    for copy in copies:
        copy.start()
    for copy in copies:
        copy.wait()


def join_call(grads, *strips):
    lx, ly, width = grads.shape
    anywhere = pl.BlockSpec(memory_space=pl.ANY)
    return pl.pallas_call(
        join_kernel,
        out_shape=shape(grads.shape, BF16),
        in_specs=[anywhere] + [VMEM] * 8,
        out_specs=anywhere,
        scratch_shapes=[
            pltpu.VMEM((2, ly, width), BF16),
            pltpu.VMEM((2, ly, width), BF16),
            pltpu.VMEM((lx - 4, 16, width), BF16),
            pltpu.VMEM((lx - 4, 16, width), BF16),
            pltpu.SemaphoreType.DMA((4,)),
        ],
        input_output_aliases={0: 0},
        compiler_params=pltpu.CompilerParams(vmem_limit_bytes=8 << 20),
        name="join",
    )(grads, *near(*strips))


def part_kernel(got, whole):
    mine = jnp.sum(got[...].astype(F32), axis=0).astype(BF16)
    for n in range(whole.shape[0]):
        whole[n] = mine


def part_call(got):
    return pl.pallas_call(
        part_kernel,
        out_shape=held(got.shape, BF16),
        in_specs=[VMEM],
        out_specs=VMEM,
        compiler_params=pltpu.CompilerParams(vmem_limit_bytes=4 << 20),
        name="part",
    )(*near(got))


def sums_kernel(sums, grad_one, grad_two, *, scale):
    base = pl.program_id(0) * 9
    for n in range(9):
        at = pl.multiple_of(64 * (base + n), 64)
        v = sums[pl.ds(at, 64)].astype(F32).T * scale
        grad_one[n] = v[0:64]
        grad_two[n] = v[64:128]


def sums_call(sums, scale):
    taps = pl.BlockSpec((9, 64, 64), lambda i: (i, 0, 0))
    return pl.pallas_call(
        functools.partial(sums_kernel, scale=scale),
        out_shape=(shape((27, 64, 64), F32), shape((27, 64, 64), F32)),
        grid=(3,),
        in_specs=[VMEM],
        out_specs=(taps, taps),
        compiler_params=pltpu.CompilerParams(vmem_limit_bytes=8 << 20),
        name="sums",
    )(*near(sums))


def shards(
    features, cotangent, low, high, weight_one, weight_two, scale_one, shift_one, scale_two,
    shift_two,
):
    nx, ny = lax.axis_size("gx"), lax.axis_size("gy")
    top, bottom = strip_call(features, low, high)
    above = shifted_in(bottom, "gx", 1)
    below = shifted_in(top, "gx", -1)
    slots, tiles, tiles_last, packed, first, last = tile_call(
        features, low, high, weight_one, weight_two
    )
    to_left, to_right = side_call(above, below, first, last)
    left = shifted_in(to_right, "gy", 1)
    right = shifted_in(to_left, "gy", -1)
    vectors = [v.reshape(1, -1) for v in (scale_one, shift_one, scale_two, shift_two)]
    out, errors, grads, sums = brick_call(
        slots, packed, above, below, left, right, cotangent, tiles, *vectors
    )

    devices = nx * ny
    parts = sums.reshape(devices, -1, 128)
    slots, errors, parts = lax.optimization_barrier((slots, errors, parts))
    got = lax.all_to_all(parts, ("gx", "gy"), 0, 0, tiled=True)
    own, grad_above, grad_below, grad_left, grad_right = input_call(
        slots, errors, grads, packed, tiles_last
    )
    from_below = shifted_in(grad_above, "gx", -1)
    from_above = shifted_in(grad_below, "gx", 1)
    got, own = lax.optimization_barrier((got, own))
    mine = part_call(got)
    back = lax.all_to_all(mine, ("gx", "gy"), 0, 0, tiled=True)
    to_left, to_right = ends_call(grad_left, grad_right, from_above, from_below)
    from_right = shifted_in(to_left, "gy", -1)
    from_left = shifted_in(to_right, "gy", 1)
    grad_features = join_call(
        own, top, bottom, first, last, from_left, from_right, from_above, from_below
    )
    back, grad_features = lax.optimization_barrier((back, grad_features))
    grad_one, grad_two = sums_call(back.reshape(-1, 128), 1.0 / (devices * SHARE))
    return (out, grad_features, grad_one, grad_two)


def solution(mesh):
    whole = P("gx", "gy", None)
    columns = P("gx", "gy")

    return jax.shard_map(
        shards,
        mesh=mesh,
        in_specs=(whole, whole, columns, columns) + (P(),) * 6,
        out_specs=(whole, whole, P(), P()),
        check_vma=False,
    )
```

```python
import functools

import jax
import jax.numpy as jnp
from jax import lax
from jax.experimental import pallas as pl
from jax.experimental.pallas import tpu as pltpu
from jax.sharding import PartitionSpec as P


BRICK = 8
ACT_MAX = 4
SHARE = 2
F32 = jnp.float32
BF16 = jnp.bfloat16


def shifted_in(array, axis, by):
    devices = lax.axis_size(axis)
    pairs = [(i, i + by) for i in range(devices) if 0 <= i + by < devices]
    return lax.ppermute(array, axis, pairs)


def low_lanes(shape):
    return lax.broadcasted_iota(jnp.int32, shape, len(shape) - 1) < 64


def turn(value):
    return pltpu.roll(value, 64, value.ndim - 1)


def to_shifted(pairs):
    turned = [turn(v) for v in pairs]
    low = low_lanes(pairs[0].shape)
    zero = jnp.zeros_like(pairs[0])
    before = [zero] + turned
    after = turned + [zero]
    return [jnp.where(low, b, a) for b, a in zip(before, after)]


def to_aligned(shifted):
    turned = [turn(v) for v in shifted]
    low = low_lanes(shifted[0].shape)
    return [jnp.where(low, turned[m], turned[m + 1]) for m in range(len(shifted) - 1)]


VMEM = pl.BlockSpec(memory_space=pltpu.VMEM)
SMEM = pl.BlockSpec(memory_space=pltpu.SMEM)
ANY = pl.BlockSpec(memory_space=pl.ANY)
shape = jax.ShapeDtypeStruct
held = pltpu.VMEM


def near(*arrays):
    return [pltpu.with_memory_space_constraint(a, pltpu.VMEM) for a in arrays]


def far(*arrays):
    return [pltpu.with_memory_space_constraint(a, pltpu.HBM) for a in arrays]


EMPTY_FEATURE = 256.0


def encode(feature, low, high, z_low):
    z = jnp.where(low_lanes((1, 128)), 1.0 * z_low, z_low + 1.0)
    feature = jnp.where(feature == 0.0, EMPTY_FEATURE, feature)
    return jnp.where((z >= low) & (z < high), feature, 0.0)


def column_bounds(low, high, x):
    ly = low.shape[1]
    code = (low[x : x + 1, :] * 16 + high[x : x + 1, :]).astype(F32)
    same = lax.broadcasted_iota(jnp.int32, (ly, ly), 0) == lax.broadcasted_iota(
        jnp.int32, (ly, ly), 1
    )
    spread = jnp.where(same, code, 0.0).astype(BF16)
    column = jnp.dot(spread, jnp.ones((ly, 128), BF16), preferred_element_type=F32)
    floor = jnp.floor(column * (1.0 / 16.0))
    return floor, column - 16.0 * floor


def strip_kernel(top_in, bottom_in, low, high, top, bottom):
    lx = low.shape[0]
    for source, target, base in ((top_in, top, 0), (bottom_in, bottom, lx - 2)):
        for x in range(2):
            floor, high_of = column_bounds(low, high, base + x)
            for m in range(4):
                lanes = slice(128 * m, 128 * m + 128)
                v = encode(source[x, :, lanes].astype(F32), floor, high_of, 2 * m)
                target[x, :, lanes] = v.astype(BF16)


def strip_call(features, low, high):
    lx, ly, width = features.shape
    end = lx // 2 - 1
    return pl.pallas_call(
        strip_kernel,
        out_shape=(held((2, ly, width), BF16), held((2, ly, width), BF16)),
        grid=(1,),
        in_specs=[
            pl.BlockSpec((2, ly, width), lambda i: (0, 0, 0)),
            pl.BlockSpec((2, ly, width), lambda i: (end, 0, 0)),
            VMEM,
            VMEM,
        ],
        out_specs=(VMEM, VMEM),
        compiler_params=pltpu.CompilerParams(vmem_limit_bytes=4 << 20),
        name="strips",
    )(*far(features, features, low, high))


def side_kernel(above, below, first, last, to_left, to_right):
    lx = first.shape[0]
    ly = above.shape[1]
    for strip, base in ((above, 0), (below, lx + 2)):
        for x in range(2):
            v = strip[x].astype(F32)
            to_left[base + x] = v[0:2].astype(BF16)
            to_right[base + x] = v[ly - 2 : ly].astype(BF16)
    to_left[2 : lx + 2] = first[...]
    to_right[2 : lx + 2] = last[...]


def side_call(above, below, first, last):
    tall = (first.shape[0] + 4,) + first.shape[1:]
    return pl.pallas_call(
        side_kernel,
        out_shape=(held(tall, BF16), held(tall, BF16)),
        in_specs=[VMEM] * 4,
        out_specs=(VMEM, VMEM),
        compiler_params=pltpu.CompilerParams(vmem_limit_bytes=4 << 20),
        name="sides",
    )(*near(above, below, first, last))


def decode(fx, ms, x, pieces, start, stop):
    kept = []
    for m, v in enumerate(pieces):
        ms[m, x, start:stop, :] = jnp.where(v == 0.0, 0.0, 1.0)
        kept.append(jnp.where(v == EMPTY_FEATURE, 0.0, v))
    for p, v in enumerate(to_shifted(kept)):
        fx[p, x, start:stop, :] = v


def tile_kernel(
    features, low, high, weight_one, weight_two, slots, bands_a, bands_b, bands_c, bands_d,
    packed, first, last, fx, ms,
):
    lx, ly = low.shape
    filled = jnp.where(high[...] > low[...], 1.0, 0.0)
    rows = [
        jnp.sum(filled[8 * i : 8 * i + 8], axis=0, keepdims=True) for i in range(lx // BRICK)
    ]
    rows = jnp.concatenate(rows + [jnp.zeros((8 - len(rows), ly), F32)], axis=0)
    among = lax.broadcasted_iota(jnp.int32, (ly, 128), 0) // BRICK
    among = among == lax.broadcasted_iota(jnp.int32, (ly, 128), 1)
    counts = jnp.dot(
        rows.astype(BF16), jnp.where(among, 1.0, 0.0).astype(BF16), preferred_element_type=F32
    )
    for i in range(3 * ACT_MAX):
        slots[i] = 0
    r = lax.broadcasted_iota(jnp.int32, (8, 128), 0)
    c = lax.broadcasted_iota(jnp.int32, (8, 128), 1)
    flags = [
        jnp.sum(jnp.where((r == i) & (c == j), counts, 0.0))
        for i in range(lx // BRICK)
        for j in range(ly // BRICK)
    ]
    seat = jnp.int32(0)
    for n, flag in enumerate(flags):
        i, j = n // (ly // BRICK), n % (ly // BRICK)
        has = (flag > 0.5) & (seat < ACT_MAX)

        @pl.when(has)
        def _(seat=seat, i=i, j=j):
            slots[seat] = i
            slots[ACT_MAX + seat] = j
            slots[2 * ACT_MAX + seat] = 1

        seat = seat + has.astype(jnp.int32)

    for x in range(lx):
        floor, high_of = column_bounds(low, high, x)
        pieces = []
        for m in range(4):
            lanes = slice(128 * m, 128 * m + 128)
            v = encode(features[x, :, lanes].astype(F32), floor, high_of, 2 * m)
            packed[x, :, lanes] = v.astype(BF16)
            first[x, :, lanes] = v[0:2].astype(BF16)
            last[x, :, lanes] = v[ly - 2 : ly].astype(BF16)
            pieces.append(v)
        decode(fx, ms, x + 2, pieces, 8, 8 + ly)
    for x in range(lx + 4):
        for base in (0, 8 + ly):
            for m in range(4):
                ms[m, x, base : base + 8, :] = jnp.zeros((8, 128), F32)
            for p in range(5):
                fx[p, x, base : base + 8, :] = jnp.zeros((8, 128), F32)

    zero = jnp.zeros((64, 64), BF16)
    for conv, (weight, bands) in enumerate(
        (
            (weight_one, bands_a),
            (weight_two, bands_b),
            (weight_two, bands_c),
            (weight_one, bands_d),
        )
    ):
        bands[...] = jnp.zeros(bands.shape, BF16)
        for tap in range(9):
            taps = []
            for oz in range(3):
                if conv < 2:
                    taps.append(weight[3 * tap + oz])
                else:
                    taps.append(weight[26 - 3 * tap - oz].astype(F32).T.astype(BF16))
            taps = [zero] + taps + [zero]
            for d in range(4):
                tile = jnp.concatenate([taps[d + 1], taps[d]], axis=1)
                for q in range(2):
                    r = d + 2 * q
                    row = 1152 * (tap // 3) + ((r // 2) * 3 + tap % 3) * 128 + (r % 2) * 64
                    bands[row : row + 64, 128 * q : 128 * q + 128] = tile


def tile_call(features, low, high, weight_one, weight_two):
    lx, ly, width = features.shape
    return pl.pallas_call(
        tile_kernel,
        out_shape=(
            shape((3 * ACT_MAX,), jnp.int32),
            held((3456, 256), BF16),
            held((3456, 256), BF16),
            held((3456, 256), BF16),
            held((3456, 256), BF16),
            held(features.shape, BF16),
            held((lx, 2, width), BF16),
            held((lx, 2, width), BF16),
            held((5, lx + 4, ly + 16, 128), F32),
            held((4, lx + 4, ly + 16, 128), F32),
        ),
        in_specs=[VMEM] * 5,
        out_specs=(SMEM,) + (VMEM,) * 9,
        compiler_params=pltpu.CompilerParams(vmem_limit_bytes=8 << 20),
        name="tiles",
    )(*far(features, low, high, weight_one, weight_two))


def convolve(source, bands, acc, xs):
    rows = source.shape[0] * xs * 16
    for half in range(2):
        parts = [
            source[:, ox : ox + xs, :, 768 * half : 768 * half + 1152].reshape(rows, 1152)
            for ox in range(3)
        ]
        acc[0:rows, 256 * half : 256 * half + 256] = jnp.dot(
            jnp.concatenate(parts, axis=1), bands[...], preferred_element_type=F32
        )


def place(slots, s):
    x0 = pl.multiple_of(slots[s] * 8, 8)
    y0 = pl.multiple_of(slots[ACT_MAX + s] * 8, 8)
    return x0, y0, slots[2 * ACT_MAX + s]


def twice(row):
    return jnp.concatenate([row, row], axis=1)


def brick_kernel(
    slots, bands_a, bands_b, bands_c, fx_in, ms_in, above, below, left, right, cotangent,
    s_one, t_one, s_two, t_two,
    results, errors_out, grads_out, total, fx, ms,
    c1, c2, c3, acc, slope, h, e2, er2, ets, et1, folded,
):
    lx, ly = cotangent.shape[0], cotangent.shape[1]
    low_row = low_lanes((1, 128))
    scale_one, shift_one = twice(s_one[...]), twice(t_one[...])
    scale_two, shift_two = twice(s_two[...]), twice(t_two[...])

    def put(x, strip, start, stop):
        lanes = [slice(128 * m, 128 * m + 128) for m in range(4)]
        decode(fx, ms, x, [strip[:, at].astype(F32) for at in lanes], start, stop)

    for x in range(2):
        put(x, above.at[x], 8, 8 + ly)
        put(lx + 2 + x, below.at[x], 8, 8 + ly)

    def side_row(i, _):
        for k in range(4):
            x = 4 * i + k
            put(x, left.at[x], 6, 8)
            put(x, right.at[x], 8 + ly, 10 + ly)
        return 0

    lax.fori_loop(0, (lx + 4) // 4, side_row, 0)

    def gather_one(s, _):
        x0, y0, _ = place(slots, s)
        for p in range(5):
            view = fx.at[p, pl.ds(x0, 12), pl.ds(y0, 24), :]
            for oy in range(3):
                lane = (p * 3 + oy) * 128
                c1[s, :, :, lane : lane + 128] = view[:, 6 + oy : 22 + oy, :].astype(BF16)
        return 0

    lax.fori_loop(0, ACT_MAX, gather_one, 0)
    convolve(c1, bands_a, acc, 10)

    def hidden_of(i, _):
        s = i // 2
        x0, y0, live = place(slots, s)
        keep_rows = lax.broadcasted_iota(jnp.int32, (16, 128), 0) < jnp.where(live > 0, 10, 0)
        for k in range(5):
            x = (i % 2) * 5 + k
            at = pl.multiple_of((s * 10 + x) * 16, 16)
            pieces = []
            for m in range(4):
                lanes = slice(128 * m, 128 * m + 128)
                mask = ms.at[m, x0 + x + 1, pl.ds(y0, 24), :][7:23, :]
                mask = jnp.where(keep_rows, mask, 0.0)
                pre = acc[pl.ds(at, 16), lanes] * scale_one + shift_one
                sig = 1.0 / (1.0 + jnp.exp(-pre))
                pieces.append(pre * sig * mask)
                slope[pl.ds(at, 16), lanes] = (
                    scale_one * mask * (sig * (1.0 + pre * (1.0 - sig)))
                )
            for p, v in enumerate(to_shifted(pieces)):
                h[s, p, x] = v
        return 0

    lax.fori_loop(0, 2 * ACT_MAX, hidden_of, 0)

    def gather_two(q, _):
        for p in range(5):
            for oy in range(3):
                lane = (p * 3 + oy) * 128
                one = h[2 * q, p, :, oy : oy + 8, :]
                two = h[2 * q + 1, p, :, oy : oy + 8, :]
                c2[q, :, :, lane : lane + 128] = jnp.concatenate([one, two], axis=1).astype(BF16)
        return 0

    lax.fori_loop(0, ACT_MAX // 2, gather_two, 0)
    convolve(c2, bands_b, acc, 8)

    def finish_two(s, _):
        x0, y0, live = place(slots, s)
        odd = lax.rem(slots[ACT_MAX + s], 2) == 1
        y16 = pl.multiple_of(slots[ACT_MAX + s] // 2 * 16, 16)
        alive = jnp.where(live > 0, 1.0, 0.0)
        zero = jnp.zeros((8, 128), F32)
        for p in range(5):
            for x in (0, 1, 10, 11):
                e2[s, p, x] = jnp.zeros((24, 128), F32)
        for x in range(8):
            at = pl.multiple_of(((s // 2) * 8 + x) * 16 + (s % 2) * 8, 8)
            centre = to_aligned([fx[p, x0 + 2 + x, pl.ds(y0 + 8, 8), :] for p in range(5)])
            errors = []
            for m in range(4):
                lanes = slice(128 * m, 128 * m + 128)
                mask = ms[m, x0 + 2 + x, pl.ds(y0 + 8, 8), :] * alive
                pre = acc[pl.ds(at, 8), lanes] * scale_two + shift_two + centre[m]
                sig = 1.0 / (1.0 + jnp.exp(-pre))
                result = pre * sig * mask
                both = cotangent[x0 + x, pl.ds(y16, 16), lanes].astype(F32)
                target = jnp.where(odd, both[8:16], both[0:8])
                grad = target * mask * (sig * (1.0 + pre * (1.0 - sig)))
                error = grad * scale_two
                errors.append(error)
                er2[pl.ds(at, 8), lanes] = error
                grads_out[s, x, :, lanes] = grad
                results[s, x, :, lanes] = result.astype(BF16)
            for p, v in enumerate(to_shifted(errors)):
                e2[s, p, x + 2, 0:8, :] = zero
                e2[s, p, x + 2, 8:16, :] = v
                e2[s, p, x + 2, 16:24, :] = zero
        return 0

    lax.fori_loop(0, ACT_MAX, finish_two, 0)

    def gather_three(s, _):
        for p in range(5):
            for oy in range(3):
                lane = (p * 3 + oy) * 128
                c3[s, :, :, lane : lane + 128] = e2[s, p, :, 6 + oy : 22 + oy, :].astype(BF16)
        return 0

    lax.fori_loop(0, ACT_MAX, gather_three, 0)
    ets[0:128] = jnp.zeros((128, ets.shape[1]), BF16)
    ets[640:768] = jnp.zeros((128, ets.shape[1]), BF16)
    ets[128:640] = er2[...].astype(BF16).T
    convolve(c3, bands_c, acc, 10)

    def finish_three(i, _):
        for k in range(4):
            at = pl.multiple_of((i * 4 + k) * 16, 16)
            for m in range(4):
                lanes = slice(128 * m, 128 * m + 128)
                error = acc[pl.ds(at, 16), lanes] * slope[pl.ds(at, 16), lanes]
                errors_out[pl.ds(at, 16), lanes] = error.astype(BF16)
        return 0

    lax.fori_loop(0, ACT_MAX * 10 // 4, finish_three, 0)

    def weight_sums(source, errors_t, xs, which):
        rows = source.shape[0] * xs * 16
        left_side = jnp.concatenate(
            [errors_t[128 * p : 128 * p + 256, :] for p in range(5)], axis=1
        )
        right_side = [
            jnp.concatenate(
                [
                    source[:, ox : ox + xs, :, 384 * p : 384 * p + 384].reshape(rows, 384)
                    for ox in range(3)
                ],
                axis=1,
            )
            for p in range(5)
        ]
        sums = jnp.dot(
            left_side, jnp.concatenate(right_side, axis=0), preferred_element_type=F32
        )
        for tap in range(9):
            block = sums[:, 128 * tap : 128 * tap + 128]
            turned = turn(block)
            for oz in range(3):
                one, two = 64 * (2 - oz), 64 * (3 - oz)
                n = tap * 3 + oz
                if which == 0:
                    folded[n] = block[one : one + 64] + turned[two : two + 64]
                else:
                    v = turned[one : one + 64] + block[two : two + 64]
                    total[n] = jnp.where(low_row, folded[n], v).astype(BF16)

    et1[0:128] = jnp.zeros((128, et1.shape[1]), BF16)
    et1[640:768] = jnp.zeros((128, et1.shape[1]), BF16)
    et1[128:640] = errors_out[...].T
    weight_sums(c1, et1, 10, 0)
    weight_sums(c2, ets, 8, 1)
    total[27] = jnp.zeros((64, 128), BF16)


def brick_call(slots, bands, fx, ms, above, below, left, right, cotangent, *vectors):
    _, _, width = cotangent.shape
    n = ACT_MAX
    return pl.pallas_call(
        brick_kernel,
        out_shape=(
            pltpu.HBM((n, 8, 8, width), BF16),
            pltpu.HBM((n * 160, width), BF16),
            pltpu.HBM((n, 8, 8, width), F32),
            pltpu.HBM((28, 64, 128), BF16),
            held(fx.shape, F32),
            held(ms.shape, F32),
        ),
        in_specs=[SMEM] + [VMEM] * 14,
        out_specs=(VMEM,) * 6,
        scratch_shapes=[
            pltpu.VMEM((n, 12, 16, 1920), BF16),
            pltpu.VMEM((n // 2, 10, 16, 1920), BF16),
            pltpu.VMEM((n, 12, 16, 1920), BF16),
            pltpu.VMEM((n * 160, width), F32),
            pltpu.VMEM((n * 160, width), F32),
            pltpu.VMEM((n, 5, 10, 16, 128), F32),
            pltpu.VMEM((n, 5, 12, 24, 128), F32),
            pltpu.VMEM((n * 64, width), F32),
            pltpu.VMEM((768, n * 64), BF16),
            pltpu.VMEM((768, n * 160), BF16),
            pltpu.VMEM((27, 64, 128), F32),
        ],
        input_output_aliases={4: 4, 5: 5},
        compiler_params=pltpu.CompilerParams(vmem_limit_bytes=24 << 20),
        name="bricks",
    )(slots, *near(*bands, fx, ms, above, below, left, right, cotangent), *vectors)


def input_kernel(
    slots, errors, grads, packed, bands, grad_own, grad_above, grad_below, grad_left, grad_right,
    e1, c4, acc, grid,
):
    lx, ly = grad_own.shape[0], grad_own.shape[1]
    wide = grid.shape[2]

    def clear_row(i, _):
        for k in range(2):
            for m in range(4):
                grid[m, 2 * i + k] = jnp.zeros((wide, 128), F32)
        return 0

    lax.fori_loop(0, (lx + 4) // 2, clear_row, 0)

    def spread(s, _):
        for p in range(5):
            for x in (0, 1, 12, 13):
                e1[p, x] = jnp.zeros((24, 128), F32)
        for x in range(10):
            at = pl.multiple_of((s * 10 + x) * 16, 16)
            rows = [
                errors[pl.ds(at, 16), 128 * m : 128 * m + 128].astype(F32) for m in range(4)
            ]
            for p, v in enumerate(to_shifted(rows)):
                e1[p, x + 2, 0:8, :] = jnp.zeros((8, 128), F32)
                e1[p, x + 2, 8:24, :] = v
        for p in range(5):
            for oy in range(3):
                lane = (p * 3 + oy) * 128
                c4[s, :, :, lane : lane + 128] = e1[p, :, 6 + oy : 22 + oy, :].astype(BF16)
        return 0

    lax.fori_loop(0, ACT_MAX, spread, 0)
    convolve(c4, bands, acc, 12)

    def finish(s, _):
        x0, y0, _ = place(slots, s)
        for x in range(12):
            at = pl.multiple_of((s * 12 + x) * 16, 16)
            for m in range(4):
                lanes = slice(128 * m, 128 * m + 128)
                view = grid.at[m, x0 + x, pl.ds(y0, 24), :]
                view[6:22, :] = view[6:22, :] + acc[pl.ds(at, 16), lanes]
        for x in range(8):
            for m in range(4):
                lanes = slice(128 * m, 128 * m + 128)
                view = grid.at[m, x0 + 2 + x, pl.ds(y0 + 8, 8), :]
                view[...] = view[...] + grads[s, x, :, lanes]
        return 0

    lax.fori_loop(0, ACT_MAX, finish, 0)

    def own_rows(i, _):
        for k in range(2):
            x = 2 * i + k
            for m in range(4):
                lanes = slice(128 * m, 128 * m + 128)
                v = grid[m, x + 2, 8 : 8 + ly, :]
                v = jnp.where(packed[x, :, lanes].astype(F32) == 0.0, 0.0, v)
                grad_own[x, :, lanes] = v.astype(BF16)
                grad_left[x, :, lanes] = grid[m, x + 2, 6:8, :].astype(BF16)
                grad_right[x, :, lanes] = grid[m, x + 2, 8 + ly : 10 + ly, :].astype(BF16)
        return 0

    lax.fori_loop(0, lx // 2, own_rows, 0)
    for target, base in ((grad_above, 0), (grad_below, lx + 2)):
        for x in range(2):
            for m in range(4):
                lanes = slice(128 * m, 128 * m + 128)
                target[x, 0:ly, lanes] = grid[m, base + x, 8 : 8 + ly, :].astype(BF16)
                corners = [
                    grid[m, base + x, 6:8, :],
                    grid[m, base + x, 8 + ly : 10 + ly, :],
                    jnp.zeros((4, 128), F32),
                ]
                target[x, ly : ly + 8, lanes] = jnp.concatenate(corners, axis=0).astype(BF16)


def input_call(slots, errors, grads, packed, bands):
    lx, ly, width = packed.shape
    n = ACT_MAX
    return pl.pallas_call(
        input_kernel,
        out_shape=(
            shape((lx, ly, width), BF16),
            held((2, ly + 8, width), BF16),
            held((2, ly + 8, width), BF16),
            held((lx, 2, width), BF16),
            held((lx, 2, width), BF16),
        ),
        in_specs=[SMEM] + [VMEM] * 4,
        out_specs=(VMEM,) * 5,
        scratch_shapes=[
            pltpu.VMEM((5, 14, 24, 128), F32),
            pltpu.VMEM((n, 14, 16, 1920), BF16),
            pltpu.VMEM((n * 192, width), F32),
            pltpu.VMEM((4, lx + 4, ly + 16, 128), F32),
        ],
        compiler_params=pltpu.CompilerParams(vmem_limit_bytes=15 << 20),
        name="inputs",
    )(slots, *far(errors, grads), *near(packed, bands))


def ends_kernel(left, right, from_above, from_below, to_left, to_right):
    lx = left.shape[0]
    ly = from_above.shape[1] - 8
    to_left[...] = left[...]
    to_right[...] = right[...]
    for source, base in ((from_above, 0), (from_below, lx - 2)):
        for x in range(2):
            v = source[x, ly : ly + 8].astype(F32)
            for strip, target, at in ((left, to_left, 0), (right, to_right, 2)):
                target[base + x] = (strip[base + x].astype(F32) + v[at : at + 2]).astype(BF16)


def ends_call(left, right, from_above, from_below):
    return pl.pallas_call(
        ends_kernel,
        out_shape=(held(left.shape, BF16), held(left.shape, BF16)),
        in_specs=[VMEM] * 4,
        out_specs=(VMEM, VMEM),
        compiler_params=pltpu.CompilerParams(vmem_limit_bytes=4 << 20),
        name="ends",
    )(*near(left, right, from_above, from_below))


def join_kernel(
    slots, grads, results, top, bottom, first, last, from_left, from_right, from_above,
    from_below, joined, out,
    rows_a, rows_b, cols_a, cols_b, sems,
):
    lx, ly, _ = joined.shape
    places = (
        (rows_a, lambda ref: ref.at[0:2]),
        (rows_b, lambda ref: ref.at[lx - 2 : lx]),
        (cols_a, lambda ref: ref.at[2 : lx - 2, 0:16, :]),
        (cols_b, lambda ref: ref.at[2 : lx - 2, ly - 16 : ly, :]),
    )
    copies = [
        pltpu.make_async_copy(at(grads), held, sems.at[n]) for n, (held, at) in enumerate(places)
    ]
    for copy in copies:
        copy.start()
    width = rows_a.shape[2]

    def clear_row(x, _):
        out[x] = jnp.zeros(out.shape[1:], BF16)
        return 0

    lax.fori_loop(0, lx, clear_row, 0)

    def put_brick(s, _):
        x0, _, _ = place(slots, s)
        odd = lax.rem(slots[ACT_MAX + s], 2) == 1
        y16 = pl.multiple_of(slots[ACT_MAX + s] // 2 * 16, 16)
        for x in range(8):
            v = results[s, x].astype(F32)
            zero = jnp.zeros_like(v)
            v = jnp.where(
                odd, jnp.concatenate([zero, v], axis=0), jnp.concatenate([v, zero], axis=0)
            )
            now = out[x0 + x, pl.ds(y16, 16), :].astype(F32)
            out[x0 + x, pl.ds(y16, 16), :] = (now + v).astype(BF16)
        return 0

    lax.fori_loop(0, ACT_MAX, put_brick, 0)
    for copy in copies:
        copy.wait()

    def first_add(strip, rows):
        return jnp.concatenate([strip.astype(F32), jnp.zeros((rows - 2, width), F32)], axis=0)

    def last_add(strip, rows):
        return jnp.concatenate([jnp.zeros((rows - 2, width), F32), strip.astype(F32)], axis=0)

    for held, code, extra, base in (
        (rows_a, top, from_above, 0),
        (rows_b, bottom, from_below, lx - 2),
    ):
        for x in range(2):
            v = held[x].astype(F32) + extra[x, 0:ly].astype(F32)
            one = v[0:8] + first_add(from_left[base + x], 8)
            two = v[ly - 8 : ly] + last_add(from_right[base + x], 8)
            v = jnp.concatenate([one, v[8 : ly - 8], two], axis=0)
            held[x] = jnp.where(code[x].astype(F32) == 0.0, 0.0, v).astype(BF16)
    for x in range(2, lx - 2):
        kept = jnp.where(first[x].astype(F32) == 0.0, 0.0, from_left[x].astype(F32))
        kept = first_add(kept, 16)
        cols_a[x - 2] = (cols_a[x - 2].astype(F32) + kept).astype(BF16)
        kept = jnp.where(last[x].astype(F32) == 0.0, 0.0, from_right[x].astype(F32))
        kept = last_add(kept, 16)
        cols_b[x - 2] = (cols_b[x - 2].astype(F32) + kept).astype(BF16)
    copies = [
        pltpu.make_async_copy(held, at(joined), sems.at[n]) for n, (held, at) in enumerate(places)
    ]
    for copy in copies:
        copy.start()
    for copy in copies:
        copy.wait()


def join_call(slots, grads, results, *strips):
    lx, ly, width = grads.shape
    return pl.pallas_call(
        join_kernel,
        out_shape=(shape(grads.shape, BF16), shape(grads.shape, BF16)),
        in_specs=[SMEM, ANY] + [VMEM] * 9,
        out_specs=(ANY, VMEM),
        scratch_shapes=[
            pltpu.VMEM((2, ly, width), BF16),
            pltpu.VMEM((2, ly, width), BF16),
            pltpu.VMEM((lx - 4, 16, width), BF16),
            pltpu.VMEM((lx - 4, 16, width), BF16),
            pltpu.SemaphoreType.DMA((4,)),
        ],
        input_output_aliases={1: 0},
        compiler_params=pltpu.CompilerParams(vmem_limit_bytes=8 << 20),
        name="join",
    )(slots, grads, *far(results), *near(*strips))


def part_kernel(got, whole):
    mine = jnp.sum(got[...].astype(F32), axis=0).astype(BF16)
    for n in range(whole.shape[0]):
        whole[n] = mine


def part_call(got):
    return pl.pallas_call(
        part_kernel,
        out_shape=held(got.shape, BF16),
        in_specs=[VMEM],
        out_specs=VMEM,
        compiler_params=pltpu.CompilerParams(vmem_limit_bytes=4 << 20),
        name="part",
    )(*near(got))


def sums_kernel(sums, grad_one, grad_two, *, scale):
    base = pl.program_id(0) * 9
    for n in range(9):
        at = pl.multiple_of(64 * (base + n), 64)
        v = sums[pl.ds(at, 64)].astype(F32).T * scale
        grad_one[n] = v[0:64]
        grad_two[n] = v[64:128]


def sums_call(sums, scale):
    taps = pl.BlockSpec((9, 64, 64), lambda i: (i, 0, 0))
    return pl.pallas_call(
        functools.partial(sums_kernel, scale=scale),
        out_shape=(shape((27, 64, 64), F32), shape((27, 64, 64), F32)),
        grid=(3,),
        in_specs=[VMEM],
        out_specs=(taps, taps),
        compiler_params=pltpu.CompilerParams(vmem_limit_bytes=8 << 20),
        name="sums",
    )(*near(sums))


def shards(
    features, cotangent, low, high, weight_one, weight_two, scale_one, shift_one, scale_two,
    shift_two,
):
    nx, ny = lax.axis_size("gx"), lax.axis_size("gy")
    top, bottom = strip_call(features, low, high)
    above = shifted_in(bottom, "gx", 1)
    below = shifted_in(top, "gx", -1)
    slots, *bands, bands_last, packed, first, last, fx, ms = tile_call(
        features, low, high, weight_one, weight_two
    )
    to_left, to_right = side_call(above, below, first, last)
    left = shifted_in(to_right, "gy", 1)
    right = shifted_in(to_left, "gy", -1)
    vectors = [v.reshape(1, -1) for v in (scale_one, shift_one, scale_two, shift_two)]
    results, errors, grads, sums, _, _ = brick_call(
        slots, bands, fx, ms, above, below, left, right, cotangent, *vectors
    )

    devices = nx * ny
    parts = sums.reshape(devices, -1, 128)
    slots, errors, parts = lax.optimization_barrier((slots, errors, parts))
    got = lax.all_to_all(parts, ("gx", "gy"), 0, 0, tiled=True)
    own, grad_above, grad_below, grad_left, grad_right = input_call(
        slots, errors, grads, packed, bands_last
    )
    from_below = shifted_in(grad_above, "gx", -1)
    from_above = shifted_in(grad_below, "gx", 1)
    got, own = lax.optimization_barrier((got, own))
    mine = part_call(got)
    back = lax.all_to_all(mine, ("gx", "gy"), 0, 0, tiled=True)
    to_left, to_right = ends_call(grad_left, grad_right, from_above, from_below)
    from_right = shifted_in(to_left, "gy", -1)
    from_left = shifted_in(to_right, "gy", 1)
    grad_features, out = join_call(
        slots, own, results, top, bottom, first, last, from_left, from_right, from_above,
        from_below,
    )
    back, grad_features, out = lax.optimization_barrier((back, grad_features, out))
    grad_one, grad_two = sums_call(back.reshape(-1, 128), 1.0 / (devices * SHARE))
    return (out, grad_features, grad_one, grad_two)


def solution(mesh):
    whole = P("gx", "gy", None)
    columns = P("gx", "gy")

    return jax.shard_map(
        shards,
        mesh=mesh,
        in_specs=(whole, whole, columns, columns) + (P(),) * 6,
        out_specs=(whole, whole, P(), P()),
        check_vma=False,
    )
```

```python
import functools

import jax
import jax.numpy as jnp
from jax import lax
from jax.experimental import pallas as pl
from jax.experimental.pallas import tpu as pltpu
from jax.sharding import PartitionSpec as P


BRICK = 8
ACT_MAX = 4
SHARE = 2
F32 = jnp.float32
BF16 = jnp.bfloat16


def shifted_in(array, axis, by):
    devices = lax.axis_size(axis)
    pairs = [(i, i + by) for i in range(devices) if 0 <= i + by < devices]
    return lax.ppermute(array, axis, pairs)


def low_lanes(shape):
    return lax.broadcasted_iota(jnp.int32, shape, len(shape) - 1) < 64


def turn(value):
    return pltpu.roll(value, 64, value.ndim - 1)


def to_shifted(pairs):
    turned = [turn(v) for v in pairs]
    low = low_lanes(pairs[0].shape)
    zero = jnp.zeros_like(pairs[0])
    before = [zero] + turned
    after = turned + [zero]
    return [jnp.where(low, b, a) for b, a in zip(before, after)]


def to_aligned(shifted):
    turned = [turn(v) for v in shifted]
    low = low_lanes(shifted[0].shape)
    return [jnp.where(low, turned[m], turned[m + 1]) for m in range(len(shifted) - 1)]


VMEM = pl.BlockSpec(memory_space=pltpu.VMEM)
SMEM = pl.BlockSpec(memory_space=pltpu.SMEM)
ANY = pl.BlockSpec(memory_space=pl.ANY)
shape = jax.ShapeDtypeStruct
held = pltpu.VMEM


def near(*arrays):
    return [pltpu.with_memory_space_constraint(a, pltpu.VMEM) for a in arrays]


def far(*arrays):
    return [pltpu.with_memory_space_constraint(a, pltpu.HBM) for a in arrays]


EMPTY_FEATURE = 256.0


def encode(feature, low, high, z_low):
    z = jnp.where(low_lanes((1, 128)), 1.0 * z_low, z_low + 1.0)
    feature = jnp.where(feature == 0.0, EMPTY_FEATURE, feature)
    return jnp.where((z >= low) & (z < high), feature, 0.0)


def column_bounds(low, high, x):
    ly = low.shape[1]
    code = (low[x : x + 1, :] * 16 + high[x : x + 1, :]).astype(F32)
    same = lax.broadcasted_iota(jnp.int32, (ly, ly), 0) == lax.broadcasted_iota(
        jnp.int32, (ly, ly), 1
    )
    spread = jnp.where(same, code, 0.0).astype(BF16)
    column = jnp.dot(spread, jnp.ones((ly, 128), BF16), preferred_element_type=F32)
    floor = jnp.floor(column * (1.0 / 16.0))
    return floor, column - 16.0 * floor


def strip_kernel(top_in, bottom_in, low, high, top, bottom):
    lx = low.shape[0]
    for source, target, base in ((top_in, top, 0), (bottom_in, bottom, lx - 2)):
        for x in range(2):
            floor, high_of = column_bounds(low, high, base + x)
            for m in range(4):
                lanes = slice(128 * m, 128 * m + 128)
                v = encode(source[x, :, lanes].astype(F32), floor, high_of, 2 * m)
                target[x, :, lanes] = v.astype(BF16)


def strip_call(features, low, high):
    lx, ly, width = features.shape
    end = lx // 2 - 1
    return pl.pallas_call(
        strip_kernel,
        out_shape=(held((2, ly, width), BF16), held((2, ly, width), BF16)),
        grid=(1,),
        in_specs=[
            pl.BlockSpec((2, ly, width), lambda i: (0, 0, 0)),
            pl.BlockSpec((2, ly, width), lambda i: (end, 0, 0)),
            VMEM,
            VMEM,
        ],
        out_specs=(VMEM, VMEM),
        compiler_params=pltpu.CompilerParams(vmem_limit_bytes=4 << 20),
        name="strips",
    )(*far(features, features, low, high))


def side_kernel(above, below, first, last, to_left, to_right):
    lx = first.shape[0]
    ly = above.shape[1]
    for strip, base in ((above, 0), (below, lx + 2)):
        for x in range(2):
            v = strip[x].astype(F32)
            to_left[base + x] = v[0:2].astype(BF16)
            to_right[base + x] = v[ly - 2 : ly].astype(BF16)
    to_left[2 : lx + 2] = first[...]
    to_right[2 : lx + 2] = last[...]


def side_call(above, below, first, last):
    tall = (first.shape[0] + 4,) + first.shape[1:]
    return pl.pallas_call(
        side_kernel,
        out_shape=(held(tall, BF16), held(tall, BF16)),
        in_specs=[VMEM] * 4,
        out_specs=(VMEM, VMEM),
        compiler_params=pltpu.CompilerParams(vmem_limit_bytes=4 << 20),
        name="sides",
    )(*near(above, below, first, last))


def decode(fx, ms, x, pieces, start, stop):
    kept = []
    for m, v in enumerate(pieces):
        ms[m, x, start:stop, :] = jnp.where(v == 0.0, 0.0, 1.0)
        kept.append(jnp.where(v == EMPTY_FEATURE, 0.0, v))
    for p, v in enumerate(to_shifted(kept)):
        fx[p, x, start:stop, :] = v


def tile_kernel(
    features, low, high, weight_one, weight_two, slots, bands_a, bands_b, bands_c, bands_d,
    packed, first, last, fx, ms,
):
    lx, ly = low.shape
    filled = jnp.where(high[...] > low[...], 1.0, 0.0)
    rows = [
        jnp.sum(filled[8 * i : 8 * i + 8], axis=0, keepdims=True) for i in range(lx // BRICK)
    ]
    rows = jnp.concatenate(rows + [jnp.zeros((8 - len(rows), ly), F32)], axis=0)
    among = lax.broadcasted_iota(jnp.int32, (ly, 128), 0) // BRICK
    among = among == lax.broadcasted_iota(jnp.int32, (ly, 128), 1)
    counts = jnp.dot(
        rows.astype(BF16), jnp.where(among, 1.0, 0.0).astype(BF16), preferred_element_type=F32
    )
    for i in range(3 * ACT_MAX):
        slots[i] = 0
    r = lax.broadcasted_iota(jnp.int32, (8, 128), 0)
    c = lax.broadcasted_iota(jnp.int32, (8, 128), 1)
    flags = [
        jnp.sum(jnp.where((r == i) & (c == j), counts, 0.0))
        for i in range(lx // BRICK)
        for j in range(ly // BRICK)
    ]
    seat = jnp.int32(0)
    for n, flag in enumerate(flags):
        i, j = n // (ly // BRICK), n % (ly // BRICK)
        has = (flag > 0.5) & (seat < ACT_MAX)

        @pl.when(has)
        def _(seat=seat, i=i, j=j):
            slots[seat] = i
            slots[ACT_MAX + seat] = j
            slots[2 * ACT_MAX + seat] = 1

        seat = seat + has.astype(jnp.int32)

    for x in range(lx):
        floor, high_of = column_bounds(low, high, x)
        pieces = []
        for m in range(4):
            lanes = slice(128 * m, 128 * m + 128)
            v = encode(features[x, :, lanes].astype(F32), floor, high_of, 2 * m)
            packed[x, :, lanes] = v.astype(BF16)
            first[x, :, lanes] = v[0:2].astype(BF16)
            last[x, :, lanes] = v[ly - 2 : ly].astype(BF16)
            pieces.append(v)
        decode(fx, ms, x + 2, pieces, 8, 8 + ly)
    for x in range(lx + 4):
        for base in (0, 8 + ly):
            for m in range(4):
                ms[m, x, base : base + 8, :] = jnp.zeros((8, 128), F32)
            for p in range(5):
                fx[p, x, base : base + 8, :] = jnp.zeros((8, 128), F32)

    zero = jnp.zeros((64, 64), BF16)
    for conv, (weight, bands) in enumerate(
        (
            (weight_one, bands_a),
            (weight_two, bands_b),
            (weight_two, bands_c),
            (weight_one, bands_d),
        )
    ):
        bands[...] = jnp.zeros(bands.shape, BF16)
        for tap in range(9):
            taps = []
            for oz in range(3):
                if conv < 2:
                    taps.append(weight[3 * tap + oz])
                else:
                    taps.append(weight[26 - 3 * tap - oz].astype(F32).T.astype(BF16))
            taps = [zero] + taps + [zero]
            for d in range(4):
                tile = jnp.concatenate([taps[d + 1], taps[d]], axis=1)
                for q in range(2):
                    r = d + 2 * q
                    row = 1152 * (tap // 3) + ((r // 2) * 3 + tap % 3) * 128 + (r % 2) * 64
                    bands[row : row + 64, 128 * q : 128 * q + 128] = tile


def tile_call(features, low, high, weight_one, weight_two):
    lx, ly, width = features.shape
    return pl.pallas_call(
        tile_kernel,
        out_shape=(
            shape((3 * ACT_MAX,), jnp.int32),
            held((3456, 256), BF16),
            held((3456, 256), BF16),
            held((3456, 256), BF16),
            held((3456, 256), BF16),
            held(features.shape, BF16),
            held((lx, 2, width), BF16),
            held((lx, 2, width), BF16),
            held((5, lx + 4, ly + 16, 128), F32),
            held((4, lx + 4, ly + 16, 128), F32),
        ),
        in_specs=[VMEM] * 5,
        out_specs=(SMEM,) + (VMEM,) * 9,
        compiler_params=pltpu.CompilerParams(vmem_limit_bytes=8 << 20),
        name="tiles",
    )(*far(features, low, high, weight_one, weight_two))


def convolve(source, bands, acc, xs):
    rows = source.shape[0] * xs * 16
    for half in range(2):
        parts = [
            source[:, ox : ox + xs, :, 768 * half : 768 * half + 1152].reshape(rows, 1152)
            for ox in range(3)
        ]
        acc[0:rows, 256 * half : 256 * half + 256] = jnp.dot(
            jnp.concatenate(parts, axis=1), bands[...], preferred_element_type=F32
        )


def place(slots, s):
    x0 = pl.multiple_of(slots[s] * 8, 8)
    y0 = pl.multiple_of(slots[ACT_MAX + s] * 8, 8)
    return x0, y0, slots[2 * ACT_MAX + s]


def twice(row):
    return jnp.concatenate([row, row], axis=1)


def brick_kernel(
    slots, bands_a, bands_b, bands_c, fx_in, ms_in, above, below, left, right, cotangent,
    s_one, t_one, s_two, t_two,
    results, errors_out, grads_out, total, fx, ms,
    c1, c2, c3, acc, slope, h, e2, er2, ets, et1, folded,
):
    lx, ly = cotangent.shape[0], cotangent.shape[1]
    low_row = low_lanes((1, 128))
    scale_one, shift_one = twice(s_one[...]), twice(t_one[...])
    scale_two, shift_two = twice(s_two[...]), twice(t_two[...])

    def put(x, strip, start, stop):
        lanes = [slice(128 * m, 128 * m + 128) for m in range(4)]
        decode(fx, ms, x, [strip[:, at].astype(F32) for at in lanes], start, stop)

    for x in range(2):
        put(x, above.at[x], 8, 8 + ly)
        put(lx + 2 + x, below.at[x], 8, 8 + ly)

    def side_row(i, _):
        for k in range(4):
            x = 4 * i + k
            put(x, left.at[x], 6, 8)
            put(x, right.at[x], 8 + ly, 10 + ly)
        return 0

    lax.fori_loop(0, (lx + 4) // 4, side_row, 0)

    def gather_one(s, _):
        x0, y0, _ = place(slots, s)
        for p in range(5):
            view = fx.at[p, pl.ds(x0, 12), pl.ds(y0, 24), :]
            for oy in range(3):
                lane = (p * 3 + oy) * 128
                c1[s, :, :, lane : lane + 128] = view[:, 6 + oy : 22 + oy, :].astype(BF16)
        return 0

    lax.fori_loop(0, ACT_MAX, gather_one, 0)
    convolve(c1, bands_a, acc, 10)

    def hidden_of(i, _):
        s = i // 2
        x0, y0, live = place(slots, s)
        keep_rows = lax.broadcasted_iota(jnp.int32, (16, 128), 0) < jnp.where(live > 0, 10, 0)
        for k in range(5):
            x = (i % 2) * 5 + k
            at = pl.multiple_of((s * 10 + x) * 16, 16)
            pieces = []
            for m in range(4):
                lanes = slice(128 * m, 128 * m + 128)
                mask = ms.at[m, x0 + x + 1, pl.ds(y0, 24), :][7:23, :]
                mask = jnp.where(keep_rows, mask, 0.0)
                pre = acc[pl.ds(at, 16), lanes] * scale_one + shift_one
                sig = 1.0 / (1.0 + jnp.exp(-pre))
                pieces.append(pre * sig * mask)
                slope[pl.ds(at, 16), lanes] = (
                    scale_one * mask * (sig * (1.0 + pre * (1.0 - sig)))
                )
            for p, v in enumerate(to_shifted(pieces)):
                h[s, p, x] = v
        return 0

    lax.fori_loop(0, 2 * ACT_MAX, hidden_of, 0)

    def gather_two(q, _):
        for p in range(5):
            for oy in range(3):
                lane = (p * 3 + oy) * 128
                one = h[2 * q, p, :, oy : oy + 8, :]
                two = h[2 * q + 1, p, :, oy : oy + 8, :]
                c2[q, :, :, lane : lane + 128] = jnp.concatenate([one, two], axis=1).astype(BF16)
        return 0

    lax.fori_loop(0, ACT_MAX // 2, gather_two, 0)
    convolve(c2, bands_b, acc, 8)

    def finish_two(s, _):
        x0, y0, live = place(slots, s)
        odd = lax.rem(slots[ACT_MAX + s], 2) == 1
        y16 = pl.multiple_of(slots[ACT_MAX + s] // 2 * 16, 16)
        alive = jnp.where(live > 0, 1.0, 0.0)
        zero = jnp.zeros((8, 128), F32)
        for p in range(5):
            for x in (0, 1, 10, 11):
                e2[s, p, x] = jnp.zeros((24, 128), F32)
        for x in range(8):
            at = pl.multiple_of(((s // 2) * 8 + x) * 16 + (s % 2) * 8, 8)
            centre = to_aligned([fx[p, x0 + 2 + x, pl.ds(y0 + 8, 8), :] for p in range(5)])
            errors = []
            for m in range(4):
                lanes = slice(128 * m, 128 * m + 128)
                mask = ms[m, x0 + 2 + x, pl.ds(y0 + 8, 8), :] * alive
                pre = acc[pl.ds(at, 8), lanes] * scale_two + shift_two + centre[m]
                sig = 1.0 / (1.0 + jnp.exp(-pre))
                result = pre * sig * mask
                both = cotangent[x0 + x, pl.ds(y16, 16), lanes].astype(F32)
                target = jnp.where(odd, both[8:16], both[0:8])
                grad = target * mask * (sig * (1.0 + pre * (1.0 - sig)))
                error = grad * scale_two
                errors.append(error)
                er2[pl.ds(at, 8), lanes] = error
                grads_out[s, x, :, lanes] = grad
                results[s, x, :, lanes] = result.astype(BF16)
            for p, v in enumerate(to_shifted(errors)):
                e2[s, p, x + 2, 0:8, :] = zero
                e2[s, p, x + 2, 8:16, :] = v
                e2[s, p, x + 2, 16:24, :] = zero
        return 0

    lax.fori_loop(0, ACT_MAX, finish_two, 0)

    def gather_three(s, _):
        for p in range(5):
            for oy in range(3):
                lane = (p * 3 + oy) * 128
                c3[s, :, :, lane : lane + 128] = e2[s, p, :, 6 + oy : 22 + oy, :].astype(BF16)
        return 0

    lax.fori_loop(0, ACT_MAX, gather_three, 0)
    ets[0:128] = jnp.zeros((128, ets.shape[1]), BF16)
    ets[640:768] = jnp.zeros((128, ets.shape[1]), BF16)
    ets[128:640] = er2[...].astype(BF16).T
    convolve(c3, bands_c, acc, 10)

    def finish_three(i, _):
        for k in range(4):
            at = pl.multiple_of((i * 4 + k) * 16, 16)
            for m in range(4):
                lanes = slice(128 * m, 128 * m + 128)
                error = acc[pl.ds(at, 16), lanes] * slope[pl.ds(at, 16), lanes]
                errors_out[pl.ds(at, 16), lanes] = error.astype(BF16)
        return 0

    lax.fori_loop(0, ACT_MAX * 10 // 4, finish_three, 0)

    def weight_sums(source, errors_t, xs, which):
        rows = source.shape[0] * xs * 16
        left_side = jnp.concatenate(
            [errors_t[128 * p : 128 * p + 256, :] for p in range(5)], axis=1
        )
        right_side = [
            jnp.concatenate(
                [
                    source[:, ox : ox + xs, :, 384 * p : 384 * p + 384].reshape(rows, 384)
                    for ox in range(3)
                ],
                axis=1,
            )
            for p in range(5)
        ]
        sums = jnp.dot(
            left_side, jnp.concatenate(right_side, axis=0), preferred_element_type=F32
        )
        for tap in range(9):
            block = sums[:, 128 * tap : 128 * tap + 128]
            turned = turn(block)
            for oz in range(3):
                one, two = 64 * (2 - oz), 64 * (3 - oz)
                n = tap * 3 + oz
                if which == 0:
                    folded[n] = block[one : one + 64] + turned[two : two + 64]
                else:
                    v = turned[one : one + 64] + block[two : two + 64]
                    total[n] = jnp.where(low_row, folded[n], v).astype(BF16)

    et1[0:128] = jnp.zeros((128, et1.shape[1]), BF16)
    et1[640:768] = jnp.zeros((128, et1.shape[1]), BF16)
    et1[128:640] = errors_out[...].T
    weight_sums(c1, et1, 10, 0)
    weight_sums(c2, ets, 8, 1)
    total[27] = jnp.zeros((64, 128), BF16)


def brick_call(slots, bands, fx, ms, above, below, left, right, cotangent, *vectors):
    _, _, width = cotangent.shape
    n = ACT_MAX
    return pl.pallas_call(
        brick_kernel,
        out_shape=(
            pltpu.HBM((n, 8, 8, width), BF16),
            pltpu.HBM((n * 160, width), BF16),
            pltpu.HBM((n, 8, 8, width), F32),
            pltpu.HBM((28, 64, 128), BF16),
            held(fx.shape, F32),
            held(ms.shape, F32),
        ),
        in_specs=[SMEM] + [VMEM] * 14,
        out_specs=(VMEM,) * 6,
        scratch_shapes=[
            pltpu.VMEM((n, 12, 16, 1920), BF16),
            pltpu.VMEM((n // 2, 10, 16, 1920), BF16),
            pltpu.VMEM((n, 12, 16, 1920), BF16),
            pltpu.VMEM((n * 160, width), F32),
            pltpu.VMEM((n * 160, width), F32),
            pltpu.VMEM((n, 5, 10, 16, 128), F32),
            pltpu.VMEM((n, 5, 12, 24, 128), F32),
            pltpu.VMEM((n * 64, width), F32),
            pltpu.VMEM((768, n * 64), BF16),
            pltpu.VMEM((768, n * 160), BF16),
            pltpu.VMEM((27, 64, 128), F32),
        ],
        input_output_aliases={4: 4, 5: 5},
        compiler_params=pltpu.CompilerParams(vmem_limit_bytes=24 << 20),
        name="bricks",
    )(slots, *near(*bands, fx, ms, above, below, left, right, cotangent), *vectors)


def input_kernel(
    slots, errors, grads, packed, bands, grad_own, grad_above, grad_below, grad_left, grad_right,
    e1, c4, acc, grid,
):
    lx, ly = grad_own.shape[0], grad_own.shape[1]
    wide = grid.shape[2]

    def clear_row(i, _):
        for k in range(2):
            for m in range(4):
                grid[m, 2 * i + k] = jnp.zeros((wide, 128), F32)
        return 0

    lax.fori_loop(0, (lx + 4) // 2, clear_row, 0)

    def spread(s, _):
        for p in range(5):
            for x in (0, 1, 12, 13):
                e1[p, x] = jnp.zeros((24, 128), F32)
        for x in range(10):
            at = pl.multiple_of((s * 10 + x) * 16, 16)
            rows = [
                errors[pl.ds(at, 16), 128 * m : 128 * m + 128].astype(F32) for m in range(4)
            ]
            for p, v in enumerate(to_shifted(rows)):
                e1[p, x + 2, 0:8, :] = jnp.zeros((8, 128), F32)
                e1[p, x + 2, 8:24, :] = v
        for p in range(5):
            for oy in range(3):
                lane = (p * 3 + oy) * 128
                c4[s, :, :, lane : lane + 128] = e1[p, :, 6 + oy : 22 + oy, :].astype(BF16)
        return 0

    lax.fori_loop(0, ACT_MAX, spread, 0)
    convolve(c4, bands, acc, 12)

    def finish(s, _):
        x0, y0, _ = place(slots, s)
        for x in range(12):
            at = pl.multiple_of((s * 12 + x) * 16, 16)
            for m in range(4):
                lanes = slice(128 * m, 128 * m + 128)
                view = grid.at[m, x0 + x, pl.ds(y0, 24), :]
                view[6:22, :] = view[6:22, :] + acc[pl.ds(at, 16), lanes]
        for x in range(8):
            for m in range(4):
                lanes = slice(128 * m, 128 * m + 128)
                view = grid.at[m, x0 + 2 + x, pl.ds(y0 + 8, 8), :]
                view[...] = view[...] + grads[s, x, :, lanes]
        return 0

    lax.fori_loop(0, ACT_MAX, finish, 0)

    def own_rows(i, _):
        for k in range(2):
            x = 2 * i + k
            for m in range(4):
                lanes = slice(128 * m, 128 * m + 128)
                v = grid[m, x + 2, 8 : 8 + ly, :]
                v = jnp.where(packed[x, :, lanes].astype(F32) == 0.0, 0.0, v)
                grad_own[x, :, lanes] = v.astype(BF16)
                grad_left[x, :, lanes] = grid[m, x + 2, 6:8, :].astype(BF16)
                grad_right[x, :, lanes] = grid[m, x + 2, 8 + ly : 10 + ly, :].astype(BF16)
        return 0

    lax.fori_loop(0, lx // 2, own_rows, 0)
    for target, base in ((grad_above, 0), (grad_below, lx + 2)):
        for x in range(2):
            for m in range(4):
                lanes = slice(128 * m, 128 * m + 128)
                target[x, 0:ly, lanes] = grid[m, base + x, 8 : 8 + ly, :].astype(BF16)
                corners = [
                    grid[m, base + x, 6:8, :],
                    grid[m, base + x, 8 + ly : 10 + ly, :],
                    jnp.zeros((4, 128), F32),
                ]
                target[x, ly : ly + 8, lanes] = jnp.concatenate(corners, axis=0).astype(BF16)


def input_call(slots, errors, grads, packed, bands):
    lx, ly, width = packed.shape
    n = ACT_MAX
    return pl.pallas_call(
        input_kernel,
        out_shape=(
            shape((lx, ly, width), BF16),
            held((2, ly + 8, width), BF16),
            held((2, ly + 8, width), BF16),
            held((lx, 2, width), BF16),
            held((lx, 2, width), BF16),
        ),
        in_specs=[SMEM] + [VMEM] * 4,
        out_specs=(VMEM,) * 5,
        scratch_shapes=[
            pltpu.VMEM((5, 14, 24, 128), F32),
            pltpu.VMEM((n, 14, 16, 1920), BF16),
            pltpu.VMEM((n * 192, width), F32),
            pltpu.VMEM((4, lx + 4, ly + 16, 128), F32),
        ],
        compiler_params=pltpu.CompilerParams(vmem_limit_bytes=15 << 20),
        name="inputs",
    )(slots, *far(errors, grads), *near(packed, bands))


def ends_kernel(left, right, from_above, from_below, to_left, to_right):
    lx = left.shape[0]
    ly = from_above.shape[1] - 8
    to_left[...] = left[...]
    to_right[...] = right[...]
    for source, base in ((from_above, 0), (from_below, lx - 2)):
        for x in range(2):
            v = source[x, ly : ly + 8].astype(F32)
            for strip, target, at in ((left, to_left, 0), (right, to_right, 2)):
                target[base + x] = (strip[base + x].astype(F32) + v[at : at + 2]).astype(BF16)


def ends_call(left, right, from_above, from_below):
    return pl.pallas_call(
        ends_kernel,
        out_shape=(held(left.shape, BF16), held(left.shape, BF16)),
        in_specs=[VMEM] * 4,
        out_specs=(VMEM, VMEM),
        compiler_params=pltpu.CompilerParams(vmem_limit_bytes=4 << 20),
        name="ends",
    )(*near(left, right, from_above, from_below))


def join_kernel(
    slots, grads, results, top, bottom, first, last, from_left, from_right, from_above,
    from_below, joined, out,
    rows_a, rows_b, cols_a, cols_b, sems,
):
    lx, ly, _ = joined.shape
    places = (
        (rows_a, lambda ref: ref.at[0:2]),
        (rows_b, lambda ref: ref.at[lx - 2 : lx]),
        (cols_a, lambda ref: ref.at[2 : lx - 2, 0:16, :]),
        (cols_b, lambda ref: ref.at[2 : lx - 2, ly - 16 : ly, :]),
    )
    copies = [
        pltpu.make_async_copy(at(grads), held, sems.at[n]) for n, (held, at) in enumerate(places)
    ]
    for copy in copies:
        copy.start()
    width = rows_a.shape[2]

    def clear_row(x, _):
        out[x] = jnp.zeros(out.shape[1:], BF16)
        return 0

    lax.fori_loop(0, lx, clear_row, 0)

    def put_brick(s, _):
        x0, _, _ = place(slots, s)
        odd = lax.rem(slots[ACT_MAX + s], 2) == 1
        y16 = pl.multiple_of(slots[ACT_MAX + s] // 2 * 16, 16)
        for x in range(8):
            v = results[s, x].astype(F32)
            zero = jnp.zeros_like(v)
            v = jnp.where(
                odd, jnp.concatenate([zero, v], axis=0), jnp.concatenate([v, zero], axis=0)
            )
            now = out[x0 + x, pl.ds(y16, 16), :].astype(F32)
            out[x0 + x, pl.ds(y16, 16), :] = (now + v).astype(BF16)
        return 0

    lax.fori_loop(0, ACT_MAX, put_brick, 0)
    for copy in copies:
        copy.wait()

    def first_add(strip, rows):
        return jnp.concatenate([strip.astype(F32), jnp.zeros((rows - 2, width), F32)], axis=0)

    def last_add(strip, rows):
        return jnp.concatenate([jnp.zeros((rows - 2, width), F32), strip.astype(F32)], axis=0)

    for held, code, extra, base in (
        (rows_a, top, from_above, 0),
        (rows_b, bottom, from_below, lx - 2),
    ):
        for x in range(2):
            v = held[x].astype(F32) + extra[x, 0:ly].astype(F32)
            one = v[0:8] + first_add(from_left[base + x], 8)
            two = v[ly - 8 : ly] + last_add(from_right[base + x], 8)
            v = jnp.concatenate([one, v[8 : ly - 8], two], axis=0)
            held[x] = jnp.where(code[x].astype(F32) == 0.0, 0.0, v).astype(BF16)
    for x in range(2, lx - 2):
        kept = jnp.where(first[x].astype(F32) == 0.0, 0.0, from_left[x].astype(F32))
        kept = first_add(kept, 16)
        cols_a[x - 2] = (cols_a[x - 2].astype(F32) + kept).astype(BF16)
        kept = jnp.where(last[x].astype(F32) == 0.0, 0.0, from_right[x].astype(F32))
        kept = last_add(kept, 16)
        cols_b[x - 2] = (cols_b[x - 2].astype(F32) + kept).astype(BF16)
    copies = [
        pltpu.make_async_copy(held, at(joined), sems.at[n]) for n, (held, at) in enumerate(places)
    ]
    for copy in copies:
        copy.start()
    for copy in copies:
        copy.wait()


def join_call(slots, grads, results, *strips):
    lx, ly, width = grads.shape
    return pl.pallas_call(
        join_kernel,
        out_shape=(shape(grads.shape, BF16), shape(grads.shape, BF16)),
        in_specs=[SMEM, ANY] + [VMEM] * 9,
        out_specs=(ANY, VMEM),
        scratch_shapes=[
            pltpu.VMEM((2, ly, width), BF16),
            pltpu.VMEM((2, ly, width), BF16),
            pltpu.VMEM((lx - 4, 16, width), BF16),
            pltpu.VMEM((lx - 4, 16, width), BF16),
            pltpu.SemaphoreType.DMA((4,)),
        ],
        input_output_aliases={1: 0},
        compiler_params=pltpu.CompilerParams(vmem_limit_bytes=8 << 20),
        name="join",
    )(slots, grads, *far(results), *near(*strips))


def part_kernel(got, whole):
    mine = jnp.sum(got[...].astype(F32), axis=0).astype(BF16)
    for n in range(whole.shape[0]):
        whole[n] = mine


def part_call(got):
    return pl.pallas_call(
        part_kernel,
        out_shape=held(got.shape, BF16),
        in_specs=[VMEM],
        out_specs=VMEM,
        compiler_params=pltpu.CompilerParams(vmem_limit_bytes=4 << 20),
        name="part",
    )(*near(got))


def sums_kernel(sums, one_to, two_to, grad_one, grad_two, sems, *, scale):
    leaving = []
    for k in range(3):
        taps = slice(9 * k, 9 * k + 9)
        for n in range(9 * k, 9 * k + 9):
            v = sums[64 * n : 64 * n + 64].astype(F32).T * scale
            grad_one[n] = v[0:64]
            grad_two[n] = v[64:128]
        for side, (held_in, target) in enumerate(((grad_one, one_to), (grad_two, two_to))):
            copy = pltpu.make_async_copy(held_in.at[taps], target.at[taps], sems.at[side, k])
            copy.start()
            leaving.append(copy)
    for copy in leaving:
        copy.wait()


def sums_call(sums, scale):
    return pl.pallas_call(
        functools.partial(sums_kernel, scale=scale),
        out_shape=(shape((27, 64, 64), F32), shape((27, 64, 64), F32)),
        in_specs=[VMEM],
        out_specs=(ANY, ANY),
        scratch_shapes=[
            pltpu.VMEM((27, 64, 64), F32),
            pltpu.VMEM((27, 64, 64), F32),
            pltpu.SemaphoreType.DMA((2, 3)),
        ],
        compiler_params=pltpu.CompilerParams(vmem_limit_bytes=8 << 20),
        name="sums",
    )(*near(sums))


def shards(
    features, cotangent, low, high, weight_one, weight_two, scale_one, shift_one, scale_two,
    shift_two,
):
    nx, ny = lax.axis_size("gx"), lax.axis_size("gy")
    top, bottom = strip_call(features, low, high)
    above = shifted_in(bottom, "gx", 1)
    below = shifted_in(top, "gx", -1)
    slots, *bands, bands_last, packed, first, last, fx, ms = tile_call(
        features, low, high, weight_one, weight_two
    )
    to_left, to_right = side_call(above, below, first, last)
    left = shifted_in(to_right, "gy", 1)
    right = shifted_in(to_left, "gy", -1)
    vectors = [v.reshape(1, -1) for v in (scale_one, shift_one, scale_two, shift_two)]
    results, errors, grads, sums, _, _ = brick_call(
        slots, bands, fx, ms, above, below, left, right, cotangent, *vectors
    )

    devices = nx * ny
    parts = sums.reshape(devices, -1, 128)
    slots, errors, parts = lax.optimization_barrier((slots, errors, parts))
    got = lax.all_to_all(parts, ("gx", "gy"), 0, 0, tiled=True)
    own, grad_above, grad_below, grad_left, grad_right = input_call(
        slots, errors, grads, packed, bands_last
    )
    from_below = shifted_in(grad_above, "gx", -1)
    from_above = shifted_in(grad_below, "gx", 1)
    got, own = lax.optimization_barrier((got, own))
    mine = part_call(got)
    back = lax.all_to_all(mine, ("gx", "gy"), 0, 0, tiled=True)
    to_left, to_right = ends_call(grad_left, grad_right, from_above, from_below)
    from_right = shifted_in(to_left, "gy", -1)
    from_left = shifted_in(to_right, "gy", 1)
    grad_features, out = join_call(
        slots, own, results, top, bottom, first, last, from_left, from_right, from_above,
        from_below,
    )
    back, grad_features, out = lax.optimization_barrier((back, grad_features, out))
    grad_one, grad_two = sums_call(back.reshape(-1, 128), 1.0 / (devices * SHARE))
    return (out, grad_features, grad_one, grad_two)


def solution(mesh):
    whole = P("gx", "gy", None)
    columns = P("gx", "gy")

    return jax.shard_map(
        shards,
        mesh=mesh,
        in_specs=(whole, whole, columns, columns) + (P(),) * 6,
        out_specs=(whole, whole, P(), P()),
        check_vma=False,
    )
```
